32 devices in a mesh: wide: 8 (over y, x, core), narrow: 4 (over z).
Axes of the slice: x: 2, y: 2, z: 4, core: 2. Of those that a mesh axis runs over, the one named last changes fastest.
Arguments:
- hidden_in: bfloat16 [4096, 1536], P('wide'), may hold values from -64 to 64
- segment_ids: int32 [4096], P('wide'), may hold values from 0 to 7, as said below
- seg_lengths: int32 [8], replicated, may hold values from 1 to 2048, as said below
- seg_offsets: int32 [8], replicated, may hold values from 0 to 4095, as said below
- block_table: int32 [8, 16], replicated, may hold values from -1 to 39, as said below
- attn_gain: bfloat16 [1536], replicated, may hold values from 0.099609375 to 1.8984375
- w_query: bfloat16 [1536, 1536], P('wide', 'narrow'), may hold values from -0.15625 to 0.15625
- b_query: bfloat16 [1536], P('narrow'), may hold values from -128 to 128
- w_keyval: bfloat16 [1536, 512], P('wide'), may hold values from -0.15625 to 0.15625
- b_keyval: bfloat16 [512], replicated, may hold values from -128 to 128
- w_out: bfloat16 [1536, 1536], P('narrow', 'wide'), may hold values from -0.15625 to 0.15625
- mlp_gain: bfloat16 [1536], replicated, may hold values from 0.099609375 to 1.8984375
- w_gate: bfloat16 [1536, 8960], P('wide', 'narrow'), may hold values from -0.15625 to 0.15625
- w_up: bfloat16 [1536, 8960], P('wide', 'narrow'), may hold values from -0.15625 to 0.15625
- w_down: bfloat16 [8960, 1536], P('narrow', 'wide'), may hold values from -0.0625 to 0.0625
- next_gain: bfloat16 [1536], replicated, may hold values from 0.099609375 to 1.8984375
- w_query2: bfloat16 [1536, 1536], P('wide', 'narrow'), may hold values from -0.15625 to 0.15625
- b_query2: bfloat16 [1536], P('narrow'), may hold values from -3 to 3
- w_keyval2: bfloat16 [1536, 512], P('wide'), may hold values from -0.15625 to 0.15625
- b_keyval2: bfloat16 [512], replicated, may hold values from -3 to 3
Outputs:
- hidden_out: bfloat16 [4096, 1536], P('wide')
- next_query: bfloat16 [4096, 1536], P('wide', 'narrow')
- next_keyval: bfloat16 [4096, 512], P('wide', 'narrow')
- kv_cache: bfloat16 [4, 40, 128, 128], P('narrow', 'wide')
The draws below stay inside these ranges and needn't reach their ends.
Inputs may be any that keep to these rules, and one draw needn't show every extreme that they name: `segment_ids`: segment s covers tokens seg_offsets[s] to seg_offsets[s] + seg_lengths[s] - 1. `seg_lengths`: they sum to 4096. seg_offsets[0] = 0 and seg_offsets[s + 1] = seg_offsets[s] + seg_lengths[s]. `block_table`: entry j of row s is a page for j below ceil(seg_lengths[s] / 128) and -1 beyond; no page appears twice.
All inputs are finite; a program needn't handle non-finite values.
Results may differ from the reference program's by a relative error of at most 0.017.
Values may be sent and summed in bfloat16 or wider, within the bound.
No kernel may reach another device: no remote copies, remote signals or barrier semaphores. Data moves between devices by JAX's collectives and lax.ppermute only.
A program may use at most 128 MiB of HBM per device.

```python
import math
import jax
import jax.numpy as jnp
from jax import lax

D = 1536
HEADS = 12
KVH = 2
HD = 128
FF = 8960
PAGE_LEN = 128
SEGS = 8
TOKENS = 4096
MOST_LEN = 2048
QD = 1536
KVW = 512
NUM_PAGES = 40
MAX_PAGES = 16


def segment_lengths(key):
    folded = jax.random.fold_in(key, 7)
    cut_key = jax.random.fold_in(folded, 1)
    place_key = jax.random.fold_in(folded, 2)
    remaining = TOKENS - MOST_LEN
    cut_points = jnp.sort(jax.random.permutation(cut_key, remaining - 2)[:SEGS - 3] + 1).astype(jnp.int32)
    cut_edges = jnp.concatenate([jnp.zeros((1,), jnp.int32), cut_points, jnp.full((1,), remaining - 1, jnp.int32)])
    others = jnp.concatenate([cut_edges[1:] - cut_edges[:-1], jnp.ones((1,), jnp.int32)])
    placed = jax.random.randint(place_key, (), 0, SEGS - 1)
    indices = jnp.arange(SEGS, dtype=jnp.int32)
    before = others[jnp.minimum(indices, SEGS - 2)]
    after_long = others[jnp.maximum(indices - 1, 0)]
    return jnp.where(indices < placed, before, jnp.where(indices == placed, MOST_LEN, after_long)).astype(jnp.int32)


def segment_starts(key):
    lengths = segment_lengths(key)
    return (jnp.cumsum(lengths) - lengths).astype(jnp.int32)


def draw_seg_lengths(key, part):
    return segment_lengths(key)


def draw_seg_offsets(key, part):
    return segment_starts(key)


def draw_segment_ids(key, part):
    offsets = segment_starts(key)
    token_index = jnp.arange(TOKENS, dtype=jnp.int32)
    return jnp.sum((token_index[:, None] >= offsets[None, 1:]).astype(jnp.int32), axis=1).astype(jnp.int32)


def draw_block_table(key, part):
    lengths = segment_lengths(key)
    pages_used = (lengths + PAGE_LEN - 1) // PAGE_LEN
    first_page = jnp.cumsum(pages_used) - pages_used
    page_order = jax.random.permutation(jax.random.fold_in(key, 11), NUM_PAGES).astype(jnp.int32)
    page_order = (page_order - page_order[0] + NUM_PAGES - 1) % NUM_PAGES
    slot_index = jnp.arange(MAX_PAGES, dtype=jnp.int32)
    page_picks = jnp.clip(first_page[:, None] + slot_index[None, :], 0, NUM_PAGES - 1)
    return jnp.where(slot_index[None, :] < pages_used[:, None], page_order[page_picks], -1).astype(jnp.int32)


def segment_side(key):
    lengths = segment_lengths(key)
    offsets = (jnp.cumsum(lengths) - lengths).astype(jnp.int32)
    token_index = jnp.arange(TOKENS, dtype=jnp.int32)
    seg_of_token = jnp.sum((token_index[:, None] >= offsets[None, 1:]).astype(jnp.int32), axis=1)
    seg_match = seg_of_token[:, None] == jnp.arange(SEGS, dtype=jnp.int32)[None, :]
    seg_start = jnp.sum(jnp.where(seg_match, offsets[None, :], 0), axis=1)
    seg_size = jnp.sum(jnp.where(seg_match, lengths[None, :], 0), axis=1)
    early = 2 * (token_index - seg_start) < seg_size
    return jnp.where(early, 1.0, -1.0).astype(jnp.float32)[:, None]


def draw_hidden_in(key, part):
    folded = jax.random.fold_in(key, 41)
    row_scales = jnp.exp(jax.random.uniform(jax.random.fold_in(folded, 1), (TOKENS, 1), jnp.float32, math.log(0.316), math.log(3.16)))
    column_scales = jnp.exp(jax.random.uniform(jax.random.fold_in(folded, 2), (1, D), jnp.float32, math.log(0.316), math.log(3.16)))
    common = jnp.clip(jax.random.normal(jax.random.fold_in(folded, 4), (1, D), jnp.float32), -4.0, 4.0)
    side = segment_side(key)
    values = jnp.clip(jax.random.normal(jax.random.fold_in(folded, 3), (TOKENS, D), jnp.float32), -6.0, 6.0) + 1.5 * side * common
    return jnp.clip(values * row_scales * column_scales, -63.0, 63.0).astype(jnp.bfloat16)


def bias_pair(key):
    folded = jax.random.fold_in(key, 31)
    query_bias = 0.5 * jnp.clip(jax.random.normal(jax.random.fold_in(folded, 1), (HEADS * HD,), jnp.float32), -4.0, 4.0)
    keyval_bias = 0.5 * jnp.clip(jax.random.normal(jax.random.fold_in(folded, 3), (2 * KVH * HD,), jnp.float32), -4.0, 4.0)
    return (query_bias, keyval_bias)


def draw_b_query(key, part):
    return bias_pair(key)[0].astype(jnp.bfloat16)


def draw_b_keyval(key, part):
    return bias_pair(key)[1].astype(jnp.bfloat16)


def steps_of(key, extent, pieces, low, top_value):
    loudness, own = 1.0, jax.random.fold_in(key, 6)
    for dim, shards_of in pieces:
        steps = jnp.exp(jax.random.uniform(jax.random.fold_in(own, dim), (shards_of,), jnp.float32, low / len(pieces), top_value / len(pieces)))
        loudness = loudness * jnp.repeat(steps, extent[dim] // shards_of).reshape([-1 if axis == dim else 1 for axis in range(len(extent))])
    return loudness


def normal_values(key, extent, width, limit, split=(), kind=jnp.bfloat16):
    result = jax.random.normal(key, extent, jnp.float32) * width
    if len(split) > 0:
        result = steps_of(key, extent, split, -0.22, 0.18) * result
    return jnp.clip(result, min=-limit, max=limit).astype(kind)


def setup_inputs(seed: int = 0) -> dict:
    keys = jax.random.split(jax.random.key(seed), 21)
    hidden_in = draw_hidden_in(jax.random.fold_in(keys[20], 71), 0)
    segment_ids = draw_segment_ids(jax.random.fold_in(keys[20], 71), 0)
    seg_lengths = draw_seg_lengths(jax.random.fold_in(keys[20], 71), 0)
    seg_offsets = draw_seg_offsets(jax.random.fold_in(keys[20], 71), 0)
    block_table = draw_block_table(jax.random.fold_in(keys[20], 71), 0)
    attn_gain = jnp.clip(1.0 + 0.18 * jax.random.normal(keys[5], (D,), jnp.float32), 0.099609375, 1.8984375).astype(jnp.bfloat16)
    w_query = normal_values(keys[6], (D, QD), D ** -0.5, 0.15625, ((0, 8), (1, 4)))
    b_query = draw_b_query(jax.random.fold_in(keys[20], 71), 0)
    w_keyval = normal_values(keys[8], (D, KVW), D ** -0.5, 0.15625, ((0, 8),))
    b_keyval = draw_b_keyval(jax.random.fold_in(keys[20], 71), 0)
    w_out = normal_values(keys[10], (QD, D), QD ** -0.5, 0.15625, ((0, 4), (1, 8)))
    mlp_gain = jnp.clip(1.0 + 0.18 * jax.random.normal(keys[11], (D,), jnp.float32), 0.099609375, 1.8984375).astype(jnp.bfloat16)
    w_gate = normal_values(keys[12], (D, FF), D ** -0.5, 0.15625, ((0, 8), (1, 4)))
    w_up = normal_values(keys[13], (D, FF), D ** -0.5, 0.15625, ((0, 8), (1, 4)))
    w_down = normal_values(keys[14], (FF, D), FF ** -0.5, 0.0625, ((0, 4), (1, 8)))
    next_gain = jnp.clip(1.0 + 0.18 * jax.random.normal(keys[15], (D,), jnp.float32), 0.099609375, 1.8984375).astype(jnp.bfloat16)
    w_query2 = normal_values(keys[16], (D, QD), D ** -0.5, 0.15625, ((0, 8), (1, 4)))
    b_query2 = normal_values(keys[17], (QD,), 0.5, 3.0, ((0, 4),))
    w_keyval2 = normal_values(keys[18], (D, KVW), D ** -0.5, 0.15625, ((0, 8),))
    b_keyval2 = normal_values(keys[19], (KVW,), 0.5, 3.0)
    return dict(hidden_in=hidden_in, segment_ids=segment_ids, seg_lengths=seg_lengths, seg_offsets=seg_offsets, block_table=block_table, attn_gain=attn_gain, w_query=w_query, b_query=b_query, w_keyval=w_keyval, b_keyval=b_keyval, w_out=w_out, mlp_gain=mlp_gain, w_gate=w_gate, w_up=w_up, w_down=w_down, next_gain=next_gain, w_query2=w_query2, b_query2=b_query2, w_keyval2=w_keyval2, b_keyval2=b_keyval2)


norm_eps = 1e-06
rope_base = 1000000.0

def rms_norm(activations, gain_vector):
    values = activations.astype(jnp.float32)
    row_scale = lax.rsqrt(lax.optimization_barrier(jnp.mean(values * values, axis=-1, keepdims=True)) + norm_eps)
    return (values * row_scale * gain_vector.astype(jnp.float32)).astype(jnp.bfloat16)

def rotate(values, positions):
    half_dim = values.shape[-1] // 2
    frequency = rope_base ** (-(jnp.arange(half_dim, dtype=jnp.float32) * 2.0 / values.shape[-1]))
    angles = positions.astype(jnp.float32)[:, None, None] * frequency
    cosine = jnp.cos(angles)
    sine_part = jnp.sin(angles)
    lower_half = values[..., :half_dim]
    upper_half = values[..., half_dim:]
    return jnp.concatenate([lower_half * cosine - upper_half * sine_part, upper_half * cosine + lower_half * sine_part], axis=-1)

def attend(queries, keyvals, segment_ids):
    query_block_len = math.gcd(TOKENS, 512)
    window = min(MOST_LEN + query_block_len, TOKENS)
    groups = HEADS // KVH
    keys_all = keyvals[:, :, 0, :]
    values_all = keyvals[:, :, 1, :]

    def one_block(block_start):
        block_start = block_start.astype(jnp.int32)
        key_start = jnp.clip(block_start + query_block_len - window, 0, TOKENS - window).astype(jnp.int32)
        query_rows = lax.dynamic_slice_in_dim(queries, block_start, query_block_len, 0)
        query_rows = query_rows.reshape(query_block_len, KVH, groups, HD).astype(jnp.float32)
        key_rows = lax.dynamic_slice_in_dim(keys_all, key_start, window, 0).astype(jnp.float32)
        value_rows = lax.dynamic_slice_in_dim(values_all, key_start, window, 0).astype(jnp.float32)
        query_seg = lax.dynamic_slice_in_dim(segment_ids, block_start, query_block_len, 0)
        key_seg = lax.dynamic_slice_in_dim(segment_ids, key_start, window, 0)
        query_pos = block_start + jnp.arange(query_block_len, dtype=jnp.int32)
        key_pos = key_start + jnp.arange(window, dtype=jnp.int32)
        visible = (query_seg[:, None] == key_seg[None, :]) & (key_pos[None, :] <= query_pos[:, None])
        scores = jnp.einsum('qhgd,khd->hgqk', query_rows, key_rows) * HD ** (-0.5)
        scores = jnp.where(visible, scores, -jnp.inf)
        row_top = lax.optimization_barrier(jnp.max(scores, axis=-1, keepdims=True))
        weights = jnp.exp(scores - row_top)
        row_total = lax.optimization_barrier(jnp.sum(weights, axis=-1, keepdims=True))
        rounded = lax.optimization_barrier(weights.astype(jnp.bfloat16)).astype(jnp.float32)
        mixed_heads = jnp.einsum('hgqk,khd->hgqd', rounded, value_rows) / row_total
        mixed_heads = mixed_heads.transpose(2, 0, 1, 3).reshape(query_block_len, QD)
        return mixed_heads.astype(jnp.bfloat16)
    starts = jnp.arange(TOKENS // query_block_len, dtype=jnp.int32) * query_block_len
    return lax.map(one_block, starts).reshape(TOKENS, QD)

def fill_pages(source, seg_lengths, seg_offsets, block_table):
    pages_here = jnp.arange(NUM_PAGES, dtype=jnp.int32)
    page_match = block_table[None, :, :] == pages_here[:, None, None]
    seg_grid = jnp.arange(SEGS, dtype=jnp.int32)[None, :, None]
    page_grid = jnp.arange(MAX_PAGES, dtype=jnp.int32)[None, None, :]
    page_owner = lax.optimization_barrier(jnp.sum(jnp.where(page_match, seg_grid, 0), axis=(1, 2))).astype(jnp.int32)
    logical = lax.optimization_barrier(jnp.sum(jnp.where(page_match, page_grid, 0), axis=(1, 2))).astype(jnp.int32)
    in_use = jnp.any(page_match, axis=(1, 2))
    first_token = (seg_offsets[page_owner] + logical * PAGE_LEN).astype(jnp.int32)
    filled = (seg_lengths[page_owner] - logical * PAGE_LEN).astype(jnp.int32)
    slot_index = jnp.arange(PAGE_LEN, dtype=jnp.int32)
    row_ids = jnp.clip(first_token[:, None] + slot_index[None, :], 0, TOKENS - 1).astype(jnp.int32)
    keep_slot = in_use[:, None] & (slot_index[None, :] < filled[:, None])
    taken_rows = jnp.take(source, row_ids.reshape(-1), axis=0).reshape(NUM_PAGES, PAGE_LEN, 2 * KVH, HD)
    taken_rows = jnp.where(keep_slot[:, :, None, None], taken_rows, jnp.zeros((), source.dtype))
    return taken_rows.transpose(2, 0, 1, 3)

def reference(hidden_in, segment_ids, seg_lengths, seg_offsets, block_table, attn_gain, w_query, b_query, w_keyval, b_keyval, w_out, mlp_gain, w_gate, w_up, w_down, next_gain, w_query2, b_query2, w_keyval2, b_keyval2):
    positions = (jnp.arange(TOKENS, dtype=jnp.int32) - seg_offsets[segment_ids]).astype(jnp.int32)
    normed = rms_norm(hidden_in, attn_gain)
    queries = jnp.dot(normed, w_query, preferred_element_type=jnp.float32) + b_query.astype(jnp.float32)
    queries = rotate(queries.reshape(TOKENS, HEADS, HD), positions).reshape(TOKENS, QD).astype(jnp.bfloat16)
    keyvals = jnp.dot(normed, w_keyval, preferred_element_type=jnp.float32) + b_keyval.astype(jnp.float32)
    keyvals = keyvals.reshape(TOKENS, KVH, 2, HD)
    keyvals = jnp.stack([rotate(keyvals[:, :, 0, :], positions), keyvals[:, :, 1, :]], axis=2).astype(jnp.bfloat16)
    mixed_heads = attend(queries, keyvals, segment_ids)
    residual = (hidden_in.astype(jnp.float32) + jnp.dot(mixed_heads, w_out, preferred_element_type=jnp.float32)).astype(jnp.bfloat16)
    normed_mlp = rms_norm(residual, mlp_gain)
    gate_sum = jnp.dot(normed_mlp, w_gate, preferred_element_type=jnp.float32)
    up_sum = jnp.dot(normed_mlp, w_up, preferred_element_type=jnp.float32)
    hidden_units = (jax.nn.silu(gate_sum) * up_sum).astype(jnp.bfloat16)
    hidden_out = (residual.astype(jnp.float32) + jnp.dot(hidden_units, w_down, preferred_element_type=jnp.float32)).astype(jnp.bfloat16)
    normed_next = rms_norm(hidden_out, next_gain)
    next_query = (jnp.dot(normed_next, w_query2, preferred_element_type=jnp.float32) + b_query2.astype(jnp.float32)).astype(jnp.bfloat16)
    next_keyval = (jnp.dot(normed_next, w_keyval2, preferred_element_type=jnp.float32) + b_keyval2.astype(jnp.float32)).astype(jnp.bfloat16)
    kv_cache = fill_pages(keyvals.reshape(TOKENS, KVW), seg_lengths, seg_offsets, block_table)
    return (hidden_out, next_query, next_keyval, kv_cache)
```

```python
import functools
import math

import jax
import jax.numpy as jnp
from jax import lax
from jax.experimental import pallas as pl
from jax.experimental.pallas import tpu as pltpu
from jax.sharding import PartitionSpec as P

HD = 128
PAGE_LEN = 128

norm_eps = 1e-06
rope_base = 1000000.0
masked_score = -1e30

f32 = jnp.float32
bf16 = jnp.bfloat16
VMEM = pltpu.VMEM
ANY = pl.ANY
SMEM = pltpu.SMEM


def vmem_spec():
    return pl.BlockSpec(memory_space=VMEM)


def any_spec():
    return pl.BlockSpec(memory_space=ANY)


def smem_spec():
    return pl.BlockSpec(memory_space=SMEM)


def params(mib):
    return pltpu.CompilerParams(vmem_limit_bytes=mib << 20)


def norm_rows(values, gain_row):
    row_scale = lax.rsqrt(jnp.mean(values * values, axis=-1, keepdims=True) + norm_eps)
    return (values * row_scale * gain_row).astype(bf16)


def lookup(table, indices):
    table_match = indices[..., None] == jnp.arange(table.shape[0], dtype=jnp.int32)
    return jnp.sum(jnp.where(table_match, table, 0), axis=-1)


def exchange(value, axis, size, mask):
    return lax.ppermute(value, axis, [(i, i ^ mask) for i in range(size)])


def wide_pieces(value, size):
    pieces = {0: value}
    for mask in range(2, size, 2):
        pieces[mask] = exchange(value, "wide", size, mask)
    for mask in range(0, size, 2):
        pieces[mask + 1] = exchange(pieces[mask], "wide", size, 1)
    return [pieces[m] for m in range(size)]


def narrow_swap(pieces, size):
    return [pieces[0]] + [exchange(pieces[k], "narrow", size, k) for k in range(1, size)]


def place_copies(piece_refs, target, sems, wide_index):
    rows = piece_refs[0].shape[0]
    copies = []
    for m, piece in enumerate(piece_refs):
        start = pl.multiple_of((wide_index ^ m) * rows, rows)
        copies.append(pltpu.make_async_copy(piece, target.at[pl.ds(start, rows)], sems.at[m]))
    return copies


def contract_last(left, right):
    return lax.dot_general(left, right, (((1,), (1,)), ((), ())), preferred_element_type=f32)


def qkv_kernel(wide, index_ref, hidden_ref, gain_ref, bias_ref, cos_ref, sin_ref, *rest):
    pieces, (q_ref, kv_ref, weight, sems) = rest[:wide], rest[wide:]
    copies = place_copies(pieces, weight, sems, index_ref[0])
    for c in copies:
        c.start()
    normed = norm_rows(hidden_ref[...].astype(f32), gain_ref[...])
    cosine, sine = cos_ref[...], sin_ref[...]
    for c in copies:
        c.wait()
    heads = weight.shape[1] // HD
    for h in range(heads):
        lanes = slice(h * HD, (h + 1) * HD)
        if h % 2 == 0:
            wider = slice(h * HD, min(h + 2, heads) * HD)
            both = jnp.dot(normed, weight[:, wider], preferred_element_type=f32)
        value = both[:, (h % 2) * HD : (h % 2 + 1) * HD] + bias_ref[:, lanes]
        if h < heads - 1:
            value = value * cosine + pltpu.roll(value, HD // 2, 1) * sine
        value = value.astype(bf16)
        if h < heads - 2:
            q_ref[:, lanes] = value
        else:
            kv_ref[:, (h - heads + 2) * HD : (h - heads + 3) * HD] = value


def attend_kernel(wide, narrow, key_block, scalar_ref, starts_ref, q_ref, *rest):
    kv_pieces, out_pieces = rest[:wide], rest[wide : 2 * wide]
    rest = rest[2 * wide :]
    part_refs, (kv_out, keyvals, w_out, mix, kv_sems, out_sems, flush_sem) = rest[:narrow], rest[narrow:]
    wide_index, narrow_index = scalar_ref[0], scalar_ref[1]
    kv_copies = place_copies(kv_pieces, keyvals, kv_sems, wide_index)
    out_copies = place_copies(out_pieces, w_out, out_sems, wide_index)
    for c in kv_copies:
        c.start()
    for c in out_copies:
        c.start()
    for c in kv_copies:
        c.wait()
    flush = pltpu.make_async_copy(keyvals, kv_out, flush_sem)
    flush.start()
    tok_rows = q_ref.shape[0]
    heads = q_ref.shape[1] // HD
    tile = key_block
    row_base = wide_index * tok_rows
    factor = HD ** (-0.5) * math.log2(math.e)
    for t in range(tok_rows // tile):
        rows = slice(t * tile, (t + 1) * tile)
        stacked = jnp.concatenate(
            [q_ref[rows, h * HD : (h + 1) * HD] for h in range(heads)], axis=0
        )
        first = row_base + t * tile
        diagonal = first // tile
        lowest = scalar_ref[2 + 2 * t] // tile
        whole_from = (scalar_ref[3 + 2 * t] + tile - 1) // tile
        starts = jnp.concatenate([starts_ref[rows, :]] * heads, axis=0)
        own = first + lax.broadcasted_iota(jnp.int32, (tile, 1), 0)
        own = jnp.concatenate([own] * heads, axis=0)

        def visit(block, state, masked, stacked=stacked, starts=starts, own=own):
            top, total, mixed = state
            begin = pl.multiple_of(block * tile, tile)
            keys = keyvals[pl.ds(begin, tile), :HD]
            values = keyvals[pl.ds(begin, tile), HD:]
            scores = contract_last(stacked, keys) * factor
            if masked:
                spot = begin + lax.broadcasted_iota(jnp.int32, (1, tile), 1)
                scores = jnp.where((spot >= starts) & (spot <= own), scores, masked_score)
            new_top = jnp.maximum(top, jnp.max(scores, axis=1, keepdims=True))
            weights = jnp.exp2(scores - new_top)
            scale = jnp.exp2(top - new_top)
            total = total * scale + jnp.sum(weights, axis=1, keepdims=True)
            mixed = mixed * scale + jnp.dot(
                weights.astype(bf16), values, preferred_element_type=f32
            )
            return new_top, total, mixed

        count = heads * tile
        state = (
            jnp.full((count, 1), masked_score, f32),
            jnp.zeros((count, 1), f32),
            jnp.zeros((count, HD), f32),
        )
        state = visit(diagonal, state, True)
        split = jnp.minimum(whole_from, diagonal)
        state = lax.fori_loop(lowest, split, lambda b, s: visit(b, s, True), state)
        split = jnp.maximum(split, lowest)
        _, total, mixed = lax.fori_loop(split, diagonal, lambda b, s: visit(b, s, False), state)
        mixed = (mixed / total).astype(bf16)
        for h in range(heads):
            mix[rows, h * HD : (h + 1) * HD] = mixed[h * tile : (h + 1) * tile]
    for c in out_copies:
        c.wait()
    share = tok_rows // narrow
    for k in range(narrow):
        start = pl.multiple_of((narrow_index ^ k) * share, share)
        part_refs[k][...] = contract_last(mix[pl.ds(start, share), :], w_out[...]).astype(bf16)
    flush.wait()


def join_kernel(narrow, base_ref, gain_ref, *rest):
    parts, (sum_ref, norm_ref) = rest[:narrow], rest[narrow:]
    total = parts[0][...].astype(f32)
    for part in parts[1:]:
        total = total + part[...].astype(f32)
    rounded = (base_ref[...].astype(f32) + total).astype(bf16)
    sum_ref[...] = rounded
    if norm_ref is not None:
        norm_ref[...] = norm_rows(rounded.astype(f32), gain_ref[...])


def ffn_kernel(narrow, *rest):
    x_refs, weights_ref = rest[:narrow], rest[narrow]
    rest = rest[narrow + 1 :]
    part_refs, (x, held, gate, hidden, sems) = rest[:narrow], rest[narrow:]
    copies = [
        pltpu.make_async_copy(weights_ref.at[:, j], held.at[j], sems.at[j]) for j in range(3)
    ]
    for c in copies:
        c.start()
    share = x_refs[0].shape[0]
    for k in range(narrow):
        x[k * share : (k + 1) * share, :] = x_refs[k][...]
    width = hidden.shape[1]
    depth = x.shape[1]
    tile = 256
    whole = width // tile

    def each_tile(body):
        @pl.loop(0, whole)
        def _(j):
            body(pl.ds(pl.multiple_of(j * tile, tile), tile), tile)

        if width % tile:
            body(slice(whole * tile, width), width - whole * tile)

    def gate_tile(lanes, size):
        block = held[0, :, :, lanes].reshape(depth, size)
        gate[:, lanes] = jnp.dot(x[...], block, preferred_element_type=f32)

    def up_tile(lanes, size):
        block = held[1, :, :, lanes].reshape(depth, size)
        up = jnp.dot(x[...], block, preferred_element_type=f32)
        value = gate[:, lanes]
        hidden[:, lanes] = (value / (1.0 + jnp.exp(-value)) * up).astype(bf16)

    copies[0].wait()
    each_tile(gate_tile)
    copies[1].wait()
    each_tile(up_tile)
    copies[2].wait()
    pieces, rows = held.shape[1], held.shape[2]
    group = 768 // rows
    for g in range(pieces // group):
        block = held[2, g * group : (g + 1) * group].reshape(group * rows, width)
        product = contract_last(hidden[...], block)
        lanes = slice(g * group * rows, (g + 1) * group * rows)
        for k in range(narrow):
            part_refs[k][:, lanes] = product[k * share : (k + 1) * share].astype(bf16)


def next_kernel(wide, narrow, scalar_ref, gain_ref, bias_ref, *rest):
    h_refs, pieces = rest[:narrow], rest[narrow : narrow + wide]
    out_ref, query_ref, keyval_ref, weight, sems = rest[narrow + wide :]
    wide_index, narrow_index = scalar_ref[0], scalar_ref[1]
    copies = place_copies(pieces, weight, sems, wide_index)
    for c in copies:
        c.start()
    share = h_refs[0].shape[0]
    queries = query_ref.shape[1]
    for c in copies:
        c.wait()
    for k in range(narrow):
        rows = pl.ds(pl.multiple_of((narrow_index ^ k) * share, share), share)
        value = h_refs[k][...]
        out_ref[rows, :] = value
        normed = norm_rows(value.astype(f32), gain_ref[...])
        product = jnp.dot(normed, weight[...], preferred_element_type=f32) + bias_ref[...]
        query_ref[rows, :] = product[:, :queries].astype(bf16)
        keyval_ref[rows, :] = product[:, queries:].astype(bf16)


def fill_pages(source, seg_lengths, seg_offsets, block_table, first_page, page_count):
    pages_here = first_page + jnp.arange(page_count, dtype=jnp.int32)
    page_match = block_table[None, :, :] == pages_here[:, None, None]
    seg_grid = jnp.arange(block_table.shape[0], dtype=jnp.int32)[None, :, None]
    page_grid = jnp.arange(block_table.shape[1], dtype=jnp.int32)[None, None, :]
    page_owner = jnp.sum(jnp.where(page_match, seg_grid, 0), axis=(1, 2))
    logical = jnp.sum(jnp.where(page_match, page_grid, 0), axis=(1, 2))
    in_use = jnp.any(page_match, axis=(1, 2))
    first_token = lookup(seg_offsets, page_owner) + logical * PAGE_LEN
    filled = lookup(seg_lengths, page_owner) - logical * PAGE_LEN
    slot_index = jnp.arange(PAGE_LEN, dtype=jnp.int32)
    row_ids = jnp.clip(first_token[:, None] + slot_index[None, :], 0, source.shape[0] - 1)
    keep_slot = in_use[:, None] & (slot_index[None, :] < filled[:, None])
    taken_rows = jnp.take(source, row_ids.reshape(-1), axis=0).reshape(
        page_count, PAGE_LEN, source.shape[1]
    )
    return jnp.where(keep_slot[:, :, None], taken_rows, jnp.zeros((), source.dtype))


def local(
    wide,
    narrow,
    hidden_in,
    segment_ids,
    seg_lengths,
    seg_offsets,
    block_table,
    attn_gain,
    w_query,
    b_query,
    w_keyval,
    b_keyval,
    w_out,
    mlp_gain,
    w_gate,
    w_up,
    w_down,
    next_gain,
    w_query2,
    b_query2,
    w_keyval2,
    b_keyval2,
):
    tok_rows, depth = hidden_in.shape
    piece_rows = w_query.shape[0]
    query_width = w_query.shape[1]
    width = w_gate.shape[1]
    wide_index = lax.axis_index("wide")
    narrow_index = lax.axis_index("narrow")
    head_pair = narrow_index // 2
    kind_index = narrow_index % 2
    pair_offset = head_pair * 2 * HD
    share = tok_rows // narrow
    row_base = wide_index * tok_rows

    packed = jnp.stack([w_gate, w_up, w_down.T])
    ffn_weights = lax.all_gather(packed, "wide", axis=0, tiled=False)

    qkv_weight = jnp.concatenate(
        [w_query, lax.dynamic_slice_in_dim(w_keyval, pair_offset, 2 * HD, 1)], axis=1
    )
    qkv_bias = jnp.concatenate(
        [b_query, lax.dynamic_slice_in_dim(b_keyval, pair_offset, 2 * HD, 0)]
    ).astype(f32)[None]
    qkv_pieces = wide_pieces(qkv_weight, wide)

    token_start = lookup(seg_offsets, segment_ids)
    positions = row_base + jnp.arange(tok_rows, dtype=jnp.int32) - token_start
    half = HD // 2
    frequency = rope_base ** (-(jnp.arange(half, dtype=f32) * 2.0 / HD))
    angles = positions.astype(f32)[:, None] * frequency
    cosine, sine = jnp.cos(angles), jnp.sin(angles)
    cosine = jnp.concatenate([cosine, cosine], axis=1)
    sine = jnp.concatenate([-sine, sine], axis=1)

    qkv_width = query_width + 2 * HD
    queries, keyvals = pl.pallas_call(
        functools.partial(qkv_kernel, wide),
        out_shape=(
            jax.ShapeDtypeStruct((tok_rows, query_width), bf16),
            jax.ShapeDtypeStruct((tok_rows, 2 * HD), bf16),
        ),
        in_specs=[smem_spec()] + [vmem_spec()] * 5 + [any_spec()] * wide,
        out_specs=(vmem_spec(), vmem_spec()),
        scratch_shapes=[VMEM((depth, qkv_width), bf16), pltpu.SemaphoreType.DMA((wide,))],
        compiler_params=params(32),
        cost_estimate=pl.CostEstimate(
            flops=2 * tok_rows * depth * qkv_width,
            bytes_accessed=2 * depth * (tok_rows + qkv_width),
            transcendentals=0,
        ),
        name="qkv",
    )(
        wide_index[None],
        hidden_in,
        attn_gain.astype(f32)[None],
        qkv_bias,
        cosine,
        sine,
        *qkv_pieces,
    )

    kv_pieces = wide_pieces(keyvals, wide)
    out_pieces = wide_pieces(w_out.T, wide)

    tile = 256
    ends = []
    for t in range(tok_rows // tile):
        ends += [token_start[t * tile], token_start[(t + 1) * tile - 1]]
    scalars = jnp.stack([wide_index, narrow_index] + ends)
    total_rows = wide * tok_rows
    *parts, kv_all = pl.pallas_call(
        functools.partial(attend_kernel, wide, narrow, tile),
        out_shape=[jax.ShapeDtypeStruct((share, depth), bf16)] * narrow
        + [jax.ShapeDtypeStruct((total_rows, 2 * HD), bf16)],
        in_specs=[smem_spec(), vmem_spec(), vmem_spec()] + [any_spec()] * (2 * wide),
        out_specs=[vmem_spec()] * narrow + [any_spec()],
        scratch_shapes=[
            VMEM((total_rows, 2 * HD), bf16),
            VMEM((depth, query_width), bf16),
            VMEM((tok_rows, query_width), bf16),
            pltpu.SemaphoreType.DMA((wide,)),
            pltpu.SemaphoreType.DMA((wide,)),
            pltpu.SemaphoreType.DMA,
        ],
        compiler_params=params(40),
        cost_estimate=pl.CostEstimate(
            flops=8 * tok_rows * query_width * depth,
            bytes_accessed=4 * total_rows * HD,
            transcendentals=tok_rows * depth,
        ),
        name="attend",
    )(scalars, token_start[:, None], queries, *kv_pieces, *out_pieces)

    def join(parts, base_rows, gain, with_norm):
        shape = jax.ShapeDtypeStruct((share, depth), bf16)
        kernel = functools.partial(join_kernel, narrow)
        if not with_norm:
            body = kernel
            kernel = lambda *refs: body(*refs, None)
        return pl.pallas_call(
            kernel,
            out_shape=[shape, shape] if with_norm else [shape],
            in_specs=[vmem_spec()] * (2 + narrow),
            out_specs=[vmem_spec()] * (2 if with_norm else 1),
            compiler_params=params(24),
            name="join",
        )(base_rows, gain, *parts)

    base_rows = lax.dynamic_slice_in_dim(hidden_in, narrow_index * share, share, 0)
    residual, normed = join(
        narrow_swap(parts, narrow), base_rows, mlp_gain.astype(f32)[None], True
    )
    normed_pieces = [normed] + [exchange(normed, "narrow", narrow, k) for k in range(1, narrow)]

    parts = pl.pallas_call(
        functools.partial(ffn_kernel, narrow),
        out_shape=[jax.ShapeDtypeStruct((share, depth), bf16)] * narrow,
        in_specs=[vmem_spec()] * narrow + [any_spec()],
        out_specs=[vmem_spec()] * narrow,
        scratch_shapes=[
            VMEM((tok_rows, depth), bf16),
            VMEM((3, wide, piece_rows, width), bf16),
            VMEM((tok_rows, width), f32),
            VMEM((tok_rows, width), bf16),
            pltpu.SemaphoreType.DMA((3,)),
        ],
        compiler_params=params(52),
        cost_estimate=pl.CostEstimate(
            flops=6 * tok_rows * depth * width,
            bytes_accessed=6 * depth * width,
            transcendentals=tok_rows * width,
        ),
        name="ffn",
    )(*normed_pieces, ffn_weights)

    (hidden_rows,) = join(
        narrow_swap(parts, narrow), residual, mlp_gain.astype(f32)[None], False
    )
    hidden_pieces = [hidden_rows] + [
        exchange(hidden_rows, "narrow", narrow, k) for k in range(1, narrow)
    ]

    one_offset = pair_offset + kind_index * HD
    next_weight = jnp.concatenate(
        [w_query2, lax.dynamic_slice_in_dim(w_keyval2, one_offset, HD, 1)], axis=1
    )
    next_bias = jnp.concatenate(
        [b_query2, lax.dynamic_slice_in_dim(b_keyval2, one_offset, HD, 0)]
    ).astype(f32)[None]
    next_pieces = wide_pieces(next_weight, wide)
    next_width = query_width + HD
    hidden_out, next_query, next_keyval = pl.pallas_call(
        functools.partial(next_kernel, wide, narrow),
        out_shape=(
            jax.ShapeDtypeStruct((tok_rows, depth), bf16),
            jax.ShapeDtypeStruct((tok_rows, query_width), bf16),
            jax.ShapeDtypeStruct((tok_rows, HD), bf16),
        ),
        in_specs=[smem_spec()] + [vmem_spec()] * (2 + narrow) + [any_spec()] * wide,
        out_specs=(vmem_spec(),) * 3,
        scratch_shapes=[VMEM((depth, next_width), bf16), pltpu.SemaphoreType.DMA((wide,))],
        compiler_params=params(32),
        cost_estimate=pl.CostEstimate(
            flops=2 * tok_rows * depth * next_width,
            bytes_accessed=2 * depth * (2 * tok_rows + next_width),
            transcendentals=0,
        ),
        name="next",
    )(
        scalars[:2],
        next_gain.astype(f32)[None],
        next_bias,
        *hidden_pieces,
        *next_pieces,
    )

    source = lax.dynamic_slice_in_dim(kv_all, kind_index * HD, HD, 1)
    page_count = tok_rows // PAGE_LEN + 1
    cache_block = fill_pages(
        source, seg_lengths, seg_offsets, block_table, wide_index * page_count, page_count
    )
    return (hidden_out, next_query, next_keyval, cache_block[None])


def solution(mesh):
    placed = (
        P("wide", None),
        P("wide"),
        P(),
        P(),
        P(),
        P(),
        P("wide", "narrow"),
        P("narrow"),
        P("wide", None),
        P(),
        P("narrow", "wide"),
        P(),
        P("wide", "narrow"),
        P("wide", "narrow"),
        P("narrow", "wide"),
        P(),
        P("wide", "narrow"),
        P("narrow"),
        P("wide", None),
        P(),
    )
    return jax.shard_map(
        functools.partial(local, mesh.shape["wide"], mesh.shape["narrow"]),
        mesh=mesh,
        in_specs=placed,
        out_specs=(
            P("wide", None),
            P("wide", "narrow"),
            P("wide", "narrow"),
            P("narrow", "wide", None, None),
        ),
        check_vma=False,
    )
```

```python
import functools
import math

import jax
import jax.numpy as jnp
from jax import lax
from jax.experimental import pallas as pl
from jax.experimental.pallas import tpu as pltpu
from jax.sharding import PartitionSpec as P

HD = 128
PAGE_LEN = 128

norm_eps = 1e-06
rope_base = 1000000.0
masked_score = -1e30

f32 = jnp.float32
bf16 = jnp.bfloat16
VMEM = pltpu.VMEM
SMEM = pltpu.SMEM


def vmem_spec():
    return pl.BlockSpec(memory_space=VMEM)


def any_spec():
    return pl.BlockSpec(memory_space=pltpu.HBM)


def smem_spec():
    return pl.BlockSpec(memory_space=SMEM)


def params(mib):
    return pltpu.CompilerParams(vmem_limit_bytes=mib << 20)


def norm_rows(values, gain_row):
    row_scale = lax.rsqrt(jnp.mean(values * values, axis=-1, keepdims=True) + norm_eps)
    return (values * row_scale * gain_row).astype(bf16)


def lookup(table, indices):
    table_match = indices[..., None] == jnp.arange(table.shape[0], dtype=jnp.int32)
    return jnp.sum(jnp.where(table_match, table, 0), axis=-1)


def exchange(value, axis, size, mask):
    return lax.ppermute(value, axis, [(i, i ^ mask) for i in range(size)])


def wide_pieces(value, size):
    pieces = {0: value}
    for mask in range(2, size, 2):
        pieces[mask] = exchange(value, "wide", size, mask)
    for mask in range(0, size, 2):
        pieces[mask + 1] = exchange(pieces[mask], "wide", size, 1)
    return [pieces[m] for m in range(size)]


def narrow_swap(pieces, size):
    return [pieces[0]] + [exchange(pieces[k], "narrow", size, k) for k in range(1, size)]


def place_copies(piece_refs, target, sems, wide_index):
    rows = piece_refs[0].shape[0]
    copies = []
    for m, piece in enumerate(piece_refs):
        start = pl.multiple_of((wide_index ^ m) * rows, rows)
        copies.append(pltpu.make_async_copy(piece, target.at[pl.ds(start, rows)], sems.at[m]))
    return copies


def contract_last(left, right):
    return lax.dot_general(left, right, (((1,), (1,)), ((), ())), preferred_element_type=f32)


def qkv_kernel(wide, index_ref, hidden_ref, gain_ref, bias_ref, cos_ref, sin_ref, *rest):
    pieces, (q_ref, kv_ref, weight, sems) = rest[:wide], rest[wide:]
    copies = place_copies(pieces, weight, sems, index_ref[0])
    for c in copies:
        c.start()
    normed = norm_rows(hidden_ref[...].astype(f32), gain_ref[...])
    cosine, sine = cos_ref[...], sin_ref[...]
    for c in copies:
        c.wait()
    heads = weight.shape[1] // HD
    for h in range(heads):
        lanes = slice(h * HD, (h + 1) * HD)
        if h % 2 == 0:
            wider = slice(h * HD, min(h + 2, heads) * HD)
            both = jnp.dot(normed, weight[:, wider], preferred_element_type=f32)
        value = both[:, (h % 2) * HD : (h % 2 + 1) * HD] + bias_ref[:, lanes]
        if h < heads - 1:
            value = value * cosine + pltpu.roll(value, HD // 2, 1) * sine
        value = value.astype(bf16)
        if h < heads - 2:
            q_ref[:, lanes] = value
        else:
            kv_ref[:, (h - heads + 2) * HD : (h - heads + 3) * HD] = value


def attend_kernel(wide, narrow, key_block, wide_ref, narrow_ref, spots_ref, starts_ref, q_ref, *rest):
    kv_pieces, out_pieces = rest[:wide], rest[wide : 2 * wide]
    rest = rest[2 * wide :]
    part_refs, (kv_out, keyvals, w_out, mix, kv_sems, out_sems, flush_sem) = rest[:narrow], rest[narrow:]
    wide_index, narrow_index = wide_ref[0], narrow_ref[0]
    kv_copies = place_copies(kv_pieces, keyvals, kv_sems, wide_index)
    out_copies = place_copies(out_pieces, w_out, out_sems, wide_index)
    for c in kv_copies:
        c.start()
    for c in out_copies:
        c.start()
    for c in kv_copies:
        c.wait()
    flush = pltpu.make_async_copy(keyvals, kv_out, flush_sem)
    flush.start()
    tok_rows = q_ref.shape[0]
    heads = q_ref.shape[1] // HD
    tile = key_block
    row_base = wide_index * tok_rows
    factor = HD ** (-0.5) * math.log2(math.e)
    for t in range(tok_rows // tile):
        rows = slice(t * tile, (t + 1) * tile)
        stacked = jnp.concatenate(
            [q_ref[rows, h * HD : (h + 1) * HD] for h in range(heads)], axis=0
        )
        first = row_base + t * tile
        diagonal = first // tile
        lowest = spots_ref[t * tile] // tile
        whole_from = (spots_ref[(t + 1) * tile - 1] + tile - 1) // tile
        starts = jnp.concatenate([starts_ref[rows, :]] * heads, axis=0)
        own = first + lax.broadcasted_iota(jnp.int32, (tile, 1), 0)
        own = jnp.concatenate([own] * heads, axis=0)

        def visit(block, state, masked, stacked=stacked, starts=starts, own=own):
            top, total, mixed = state
            begin = pl.multiple_of(block * tile, tile)
            keys = keyvals[pl.ds(begin, tile), :HD]
            values = keyvals[pl.ds(begin, tile), HD:]
            scores = contract_last(stacked, keys) * factor
            if masked:
                spot = begin + lax.broadcasted_iota(jnp.int32, (1, tile), 1)
                scores = jnp.where((spot >= starts) & (spot <= own), scores, masked_score)
            new_top = jnp.maximum(top, jnp.max(scores, axis=1, keepdims=True))
            weights = jnp.exp2(scores - new_top)
            scale = jnp.exp2(top - new_top)
            total = total * scale + jnp.sum(weights, axis=1, keepdims=True)
            mixed = mixed * scale + jnp.dot(
                weights.astype(bf16), values, preferred_element_type=f32
            )
            return new_top, total, mixed

        count = heads * tile
        state = (
            jnp.full((count, 1), masked_score, f32),
            jnp.zeros((count, 1), f32),
            jnp.zeros((count, HD), f32),
        )
        state = visit(diagonal, state, True)
        split = jnp.minimum(whole_from, diagonal)
        state = lax.fori_loop(lowest, split, lambda b, s: visit(b, s, True), state)
        split = jnp.maximum(split, lowest)
        _, total, mixed = lax.fori_loop(split, diagonal, lambda b, s: visit(b, s, False), state)
        mixed = (mixed / total).astype(bf16)
        for h in range(heads):
            mix[rows, h * HD : (h + 1) * HD] = mixed[h * tile : (h + 1) * tile]
    for c in out_copies:
        c.wait()
    share = tok_rows // narrow
    for k in range(narrow):
        start = pl.multiple_of((narrow_index ^ k) * share, share)
        part_refs[k][...] = contract_last(mix[pl.ds(start, share), :], w_out[...]).astype(bf16)
    flush.wait()


def join_kernel(narrow, base_ref, gain_ref, *rest):
    parts, outs = rest[:narrow], rest[narrow:]
    total = parts[0][...].astype(f32)
    for part in parts[1:]:
        total = total + part[...].astype(f32)
    rounded = (base_ref[...].astype(f32) + total).astype(bf16)
    if len(outs) > narrow:
        outs[narrow][...] = rounded
        rounded = norm_rows(rounded.astype(f32), gain_ref[...])
    for out in outs[:narrow]:
        out[...] = rounded


def ffn_kernel(narrow, *rest):
    x_refs, weights_ref = rest[:narrow], rest[narrow]
    rest = rest[narrow + 1 :]
    part_refs, (x, held, gate, hidden, sems) = rest[:narrow], rest[narrow:]
    copies = [
        pltpu.make_async_copy(weights_ref.at[:, j], held.at[j], sems.at[j]) for j in range(3)
    ]
    for c in copies:
        c.start()
    share = x_refs[0].shape[0]
    for k in range(narrow):
        x[k * share : (k + 1) * share, :] = x_refs[k][...]
    width = hidden.shape[1]
    depth = x.shape[1]
    tile = 256
    whole = width // tile

    def each_tile(body):
        @pl.loop(0, whole)
        def _(j):
            body(pl.ds(pl.multiple_of(j * tile, tile), tile), tile)

        if width % tile:
            body(slice(whole * tile, width), width - whole * tile)

    def gate_tile(lanes, size):
        block = held[0, :, :, lanes].reshape(depth, size)
        gate[:, lanes] = jnp.dot(x[...], block, preferred_element_type=f32)

    def up_tile(lanes, size):
        block = held[1, :, :, lanes].reshape(depth, size)
        up = jnp.dot(x[...], block, preferred_element_type=f32)
        value = gate[:, lanes]
        hidden[:, lanes] = (value / (1.0 + jnp.exp(-value)) * up).astype(bf16)

    copies[0].wait()
    each_tile(gate_tile)
    copies[1].wait()
    each_tile(up_tile)
    copies[2].wait()
    pieces, rows = held.shape[1], held.shape[2]
    group = 768 // rows
    for g in range(pieces // group):
        block = held[2, g * group : (g + 1) * group].reshape(group * rows, width)
        product = contract_last(hidden[...], block)
        lanes = slice(g * group * rows, (g + 1) * group * rows)
        for k in range(narrow):
            part_refs[k][:, lanes] = product[k * share : (k + 1) * share].astype(bf16)


def next_kernel(wide, narrow, wide_ref, narrow_ref, gain_ref, bias_ref, *rest):
    h_refs, pieces = rest[:narrow], rest[narrow : narrow + wide]
    out_ref, query_ref, keyval_ref, weight, sems = rest[narrow + wide :]
    wide_index, narrow_index = wide_ref[0], narrow_ref[0]
    copies = place_copies(pieces, weight, sems, wide_index)
    for c in copies:
        c.start()
    share = h_refs[0].shape[0]
    queries = query_ref.shape[1]
    for c in copies:
        c.wait()
    for k in range(narrow):
        rows = pl.ds(pl.multiple_of((narrow_index ^ k) * share, share), share)
        value = h_refs[k][...]
        out_ref[rows, :] = value
        normed = norm_rows(value.astype(f32), gain_ref[...])
        product = jnp.dot(normed, weight[...], preferred_element_type=f32) + bias_ref[...]
        query_ref[rows, :] = product[:, :queries].astype(bf16)
        keyval_ref[rows, :] = product[:, queries:].astype(bf16)


def fill_pages(source, seg_lengths, seg_offsets, block_table, first_page, page_count):
    pages_here = first_page + jnp.arange(page_count, dtype=jnp.int32)
    page_match = block_table[None, :, :] == pages_here[:, None, None]
    seg_grid = jnp.arange(block_table.shape[0], dtype=jnp.int32)[None, :, None]
    page_grid = jnp.arange(block_table.shape[1], dtype=jnp.int32)[None, None, :]
    page_owner = jnp.sum(jnp.where(page_match, seg_grid, 0), axis=(1, 2))
    logical = jnp.sum(jnp.where(page_match, page_grid, 0), axis=(1, 2))
    in_use = jnp.any(page_match, axis=(1, 2))
    first_token = lookup(seg_offsets, page_owner) + logical * PAGE_LEN
    filled = lookup(seg_lengths, page_owner) - logical * PAGE_LEN
    slot_index = jnp.arange(PAGE_LEN, dtype=jnp.int32)
    row_ids = jnp.clip(first_token[:, None] + slot_index[None, :], 0, source.shape[0] - 1)
    keep_slot = in_use[:, None] & (slot_index[None, :] < filled[:, None])
    taken_rows = jnp.take(source, row_ids.reshape(-1), axis=0).reshape(
        page_count, PAGE_LEN, source.shape[1]
    )
    return jnp.where(keep_slot[:, :, None], taken_rows, jnp.zeros((), source.dtype))


def local(
    wide,
    narrow,
    hidden_in,
    segment_ids,
    seg_lengths,
    seg_offsets,
    block_table,
    attn_gain,
    w_query,
    b_query,
    w_keyval,
    b_keyval,
    w_out,
    mlp_gain,
    w_gate,
    w_up,
    w_down,
    next_gain,
    w_query2,
    b_query2,
    w_keyval2,
    b_keyval2,
):
    tok_rows, depth = hidden_in.shape
    piece_rows = w_query.shape[0]
    query_width = w_query.shape[1]
    width = w_gate.shape[1]
    wide_index = lax.axis_index("wide")
    narrow_index = lax.axis_index("narrow")
    head_pair = narrow_index // 2
    kind_index = narrow_index % 2
    pair_offset = head_pair * 2 * HD
    share = tok_rows // narrow
    row_base = wide_index * tok_rows

    packed = jnp.stack([w_gate, w_up, w_down.T])
    ffn_weights = lax.all_gather(packed, "wide", axis=0, tiled=False)

    qkv_weight = jnp.concatenate(
        [w_query, lax.dynamic_slice_in_dim(w_keyval, pair_offset, 2 * HD, 1)], axis=1
    )
    qkv_bias = jnp.concatenate(
        [b_query, lax.dynamic_slice_in_dim(b_keyval, pair_offset, 2 * HD, 0)]
    ).astype(f32)[None]
    qkv_pieces = wide_pieces(qkv_weight, wide)

    token_start = lookup(seg_offsets, segment_ids)
    positions = row_base + jnp.arange(tok_rows, dtype=jnp.int32) - token_start
    half = HD // 2
    frequency = rope_base ** (-(jnp.arange(half, dtype=f32) * 2.0 / HD))
    angles = positions.astype(f32)[:, None] * frequency
    cosine, sine = jnp.cos(angles), jnp.sin(angles)
    cosine = jnp.concatenate([cosine, cosine], axis=1)
    sine = jnp.concatenate([-sine, sine], axis=1)

    qkv_width = query_width + 2 * HD
    queries, keyvals = pl.pallas_call(
        functools.partial(qkv_kernel, wide),
        out_shape=(
            jax.ShapeDtypeStruct((tok_rows, query_width), bf16),
            jax.ShapeDtypeStruct((tok_rows, 2 * HD), bf16),
        ),
        in_specs=[smem_spec()] + [vmem_spec()] * 5 + [any_spec()] * wide,
        out_specs=(vmem_spec(), vmem_spec()),
        scratch_shapes=[VMEM((depth, qkv_width), bf16), pltpu.SemaphoreType.DMA((wide,))],
        compiler_params=params(32),
        cost_estimate=pl.CostEstimate(
            flops=2 * tok_rows * depth * qkv_width,
            bytes_accessed=2 * depth * (tok_rows + qkv_width),
            transcendentals=0,
        ),
        name="qkv",
    )(
        wide_index[None],
        hidden_in,
        attn_gain.astype(f32)[None],
        qkv_bias,
        cosine,
        sine,
        *qkv_pieces,
    )

    kv_pieces = wide_pieces(keyvals, wide)
    out_pieces = wide_pieces(w_out.T, wide)

    tile = 256
    total_rows = wide * tok_rows
    *parts, kv_all = pl.pallas_call(
        functools.partial(attend_kernel, wide, narrow, tile),
        out_shape=[jax.ShapeDtypeStruct((share, depth), bf16)] * narrow
        + [jax.ShapeDtypeStruct((total_rows, 2 * HD), bf16)],
        in_specs=[smem_spec()] * 3 + [vmem_spec()] * 2 + [any_spec()] * (2 * wide),
        out_specs=[vmem_spec()] * narrow + [any_spec()],
        scratch_shapes=[
            VMEM((total_rows, 2 * HD), bf16),
            VMEM((depth, query_width), bf16),
            VMEM((tok_rows, query_width), bf16),
            pltpu.SemaphoreType.DMA((wide,)),
            pltpu.SemaphoreType.DMA((wide,)),
            pltpu.SemaphoreType.DMA,
        ],
        compiler_params=params(40),
        cost_estimate=pl.CostEstimate(
            flops=8 * tok_rows * query_width * depth,
            bytes_accessed=4 * total_rows * HD,
            transcendentals=tok_rows * depth,
        ),
        name="attend",
    )(
        wide_index[None],
        narrow_index[None],
        token_start,
        token_start[:, None],
        queries,
        *kv_pieces,
        *out_pieces,
    )

    def join(parts, base_rows, gain, with_norm):
        shape = jax.ShapeDtypeStruct((share, depth), bf16)
        count = narrow + 1 if with_norm else narrow
        return pl.pallas_call(
            functools.partial(join_kernel, narrow),
            out_shape=[shape] * count,
            in_specs=[vmem_spec()] * (2 + narrow),
            out_specs=[vmem_spec()] * count,
            compiler_params=params(24),
            name="join",
        )(base_rows, gain, *parts)

    base_rows = lax.dynamic_slice_in_dim(hidden_in, narrow_index * share, share, 0)
    mlp_row = mlp_gain.astype(f32)[None]
    *normed, residual = join(narrow_swap(parts, narrow), base_rows, mlp_row, True)
    normed_pieces = narrow_swap(normed, narrow)

    parts = pl.pallas_call(
        functools.partial(ffn_kernel, narrow),
        out_shape=[jax.ShapeDtypeStruct((share, depth), bf16)] * narrow,
        in_specs=[vmem_spec()] * narrow + [any_spec()],
        out_specs=[vmem_spec()] * narrow,
        scratch_shapes=[
            VMEM((tok_rows, depth), bf16),
            VMEM((3, wide, piece_rows, width), bf16),
            VMEM((tok_rows, width), f32),
            VMEM((tok_rows, width), bf16),
            pltpu.SemaphoreType.DMA((3,)),
        ],
        compiler_params=params(52),
        cost_estimate=pl.CostEstimate(
            flops=6 * tok_rows * depth * width,
            bytes_accessed=6 * depth * width,
            transcendentals=tok_rows * width,
        ),
        name="ffn",
    )(*normed_pieces, ffn_weights)

    hidden_rows = join(narrow_swap(parts, narrow), residual, mlp_row, False)
    hidden_pieces = narrow_swap(hidden_rows, narrow)

    one_offset = pair_offset + kind_index * HD
    next_weight = jnp.concatenate(
        [w_query2, lax.dynamic_slice_in_dim(w_keyval2, one_offset, HD, 1)], axis=1
    )
    next_bias = jnp.concatenate(
        [b_query2, lax.dynamic_slice_in_dim(b_keyval2, one_offset, HD, 0)]
    ).astype(f32)[None]
    next_weight, _ = lax.optimization_barrier((next_weight, residual))
    next_pieces = wide_pieces(next_weight, wide)
    next_width = query_width + HD
    hidden_out, next_query, next_keyval = pl.pallas_call(
        functools.partial(next_kernel, wide, narrow),
        out_shape=(
            jax.ShapeDtypeStruct((tok_rows, depth), bf16),
            jax.ShapeDtypeStruct((tok_rows, query_width), bf16),
            jax.ShapeDtypeStruct((tok_rows, HD), bf16),
        ),
        in_specs=[smem_spec()] * 2 + [vmem_spec()] * (2 + narrow) + [any_spec()] * wide,
        out_specs=(vmem_spec(),) * 3,
        scratch_shapes=[VMEM((depth, next_width), bf16), pltpu.SemaphoreType.DMA((wide,))],
        compiler_params=params(32),
        cost_estimate=pl.CostEstimate(
            flops=2 * tok_rows * depth * next_width,
            bytes_accessed=2 * depth * (2 * tok_rows + next_width),
            transcendentals=0,
        ),
        name="next",
    )(
        wide_index[None],
        narrow_index[None],
        next_gain.astype(f32)[None],
        next_bias,
        *hidden_pieces,
        *next_pieces,
    )

    source = lax.dynamic_slice_in_dim(kv_all, kind_index * HD, HD, 1)
    page_count = tok_rows // PAGE_LEN + 1
    cache_block = fill_pages(
        source, seg_lengths, seg_offsets, block_table, wide_index * page_count, page_count
    )
    return (hidden_out, next_query, next_keyval, cache_block[None])


def solution(mesh):
    placed = (
        P("wide", None),
        P("wide"),
        P(),
        P(),
        P(),
        P(),
        P("wide", "narrow"),
        P("narrow"),
        P("wide", None),
        P(),
        P("narrow", "wide"),
        P(),
        P("wide", "narrow"),
        P("wide", "narrow"),
        P("narrow", "wide"),
        P(),
        P("wide", "narrow"),
        P("narrow"),
        P("wide", None),
        P(),
    )
    return jax.shard_map(
        functools.partial(local, mesh.shape["wide"], mesh.shape["narrow"]),
        mesh=mesh,
        in_specs=placed,
        out_specs=(
            P("wide", None),
            P("wide", "narrow"),
            P("wide", "narrow"),
            P("narrow", "wide", None, None),
        ),
        check_vma=False,
    )
```

```python
import functools
import math

import jax
import jax.numpy as jnp
from jax import lax
from jax.experimental import pallas as pl
from jax.experimental.pallas import tpu as pltpu
from jax.sharding import PartitionSpec as P

HD = 128
PAGE_LEN = 128

norm_eps = 1e-06
rope_base = 1000000.0
masked_score = -1e30

f32 = jnp.float32
bf16 = jnp.bfloat16
VMEM = pltpu.VMEM
SMEM = pltpu.SMEM


def vmem_spec():
    return pl.BlockSpec(memory_space=VMEM)


def any_spec():
    return pl.BlockSpec(memory_space=pltpu.HBM)


def smem_spec():
    return pl.BlockSpec(memory_space=SMEM)


def params(mib):
    return pltpu.CompilerParams(vmem_limit_bytes=mib << 20)


def norm_rows(values, gain_row):
    row_scale = lax.rsqrt(jnp.mean(values * values, axis=-1, keepdims=True) + norm_eps)
    return (values * row_scale * gain_row).astype(bf16)


def lookup(table, indices):
    table_match = indices[..., None] == jnp.arange(table.shape[0], dtype=jnp.int32)
    return jnp.sum(jnp.where(table_match, table, 0), axis=-1)


def exchange(value, axis, size, mask):
    return lax.ppermute(value, axis, [(i, i ^ mask) for i in range(size)])


def wide_pieces(value, size):
    pieces = {0: value}
    for mask in range(2, size, 2):
        pieces[mask] = exchange(value, "wide", size, mask)
    for mask in range(0, size, 2):
        pieces[mask + 1] = exchange(pieces[mask], "wide", size, 1)
    return [pieces[m] for m in range(size)]


def narrow_swap(pieces, size):
    return [pieces[0]] + [exchange(pieces[k], "narrow", size, k) for k in range(1, size)]


def place_copies(piece_refs, target, sems, wide_index):
    rows = piece_refs[0].shape[0]
    copies = []
    for m, piece in enumerate(piece_refs):
        start = pl.multiple_of((wide_index ^ m) * rows, rows)
        copies.append(pltpu.make_async_copy(piece, target.at[pl.ds(start, rows)], sems.at[m]))
    return copies


def contract_last(left, right):
    return lax.dot_general(left, right, (((1,), (1,)), ((), ())), preferred_element_type=f32)


def qkv_kernel(wide, index_ref, hidden_ref, gain_ref, bias_ref, cos_ref, sin_ref, *rest):
    pieces, (q_ref, kv_ref, weight, sems) = rest[:wide], rest[wide:]
    copies = place_copies(pieces, weight, sems, index_ref[0])
    for c in copies:
        c.start()
    normed = norm_rows(hidden_ref[...].astype(f32), gain_ref[...])
    cosine, sine = cos_ref[...], sin_ref[...]
    for c in copies:
        c.wait()
    heads = weight.shape[1] // HD
    for h in range(heads):
        lanes = slice(h * HD, (h + 1) * HD)
        if h % 2 == 0:
            wider = slice(h * HD, min(h + 2, heads) * HD)
            both = jnp.dot(normed, weight[:, wider], preferred_element_type=f32)
        value = both[:, (h % 2) * HD : (h % 2 + 1) * HD] + bias_ref[:, lanes]
        if h < heads - 1:
            value = value * cosine + pltpu.roll(value, HD // 2, 1) * sine
        value = value.astype(bf16)
        if h < heads - 2:
            q_ref[:, lanes] = value
        else:
            kv_ref[:, (h - heads + 2) * HD : (h - heads + 3) * HD] = value


def attend_kernel(wide, narrow, key_block, wide_ref, narrow_ref, spots_ref, starts_ref, q_ref, *rest):
    kv_pieces, out_pieces = rest[:wide], rest[wide : 2 * wide]
    rest = rest[2 * wide :]
    part_refs, (kv_out, keyvals, w_out, mix, kv_sems, out_sems, flush_sem) = rest[:narrow], rest[narrow:]
    wide_index, narrow_index = wide_ref[0], narrow_ref[0]
    kv_copies = place_copies(kv_pieces, keyvals, kv_sems, wide_index)
    out_copies = place_copies(out_pieces, w_out, out_sems, wide_index)
    for c in kv_copies:
        c.start()
    for c in out_copies:
        c.start()
    for c in kv_copies:
        c.wait()
    flush = pltpu.make_async_copy(keyvals, kv_out, flush_sem)
    flush.start()
    tok_rows = q_ref.shape[0]
    heads = q_ref.shape[1] // HD
    tile = key_block
    row_base = wide_index * tok_rows
    factor = HD ** (-0.5) * math.log2(math.e)
    for t in range(tok_rows // tile):
        rows = slice(t * tile, (t + 1) * tile)
        stacked = jnp.concatenate(
            [q_ref[rows, h * HD : (h + 1) * HD] for h in range(heads)], axis=0
        )
        first = row_base + t * tile
        diagonal = first // tile
        lowest = spots_ref[t * tile] // tile
        whole_from = (spots_ref[(t + 1) * tile - 1] + tile - 1) // tile
        starts = jnp.concatenate([starts_ref[rows, :]] * heads, axis=0)
        own = first + lax.broadcasted_iota(jnp.int32, (tile, 1), 0)
        own = jnp.concatenate([own] * heads, axis=0)

        def visit(block, state, masked, stacked=stacked, starts=starts, own=own):
            top, total, mixed = state
            begin = pl.multiple_of(block * tile, tile)
            keys = keyvals[pl.ds(begin, tile), :HD]
            values = keyvals[pl.ds(begin, tile), HD:]
            scores = contract_last(stacked, keys) * factor
            if masked:
                spot = begin + lax.broadcasted_iota(jnp.int32, (1, tile), 1)
                scores = jnp.where((spot >= starts) & (spot <= own), scores, masked_score)
            new_top = jnp.maximum(top, jnp.max(scores, axis=1, keepdims=True))
            weights = jnp.exp2(scores - new_top)
            scale = jnp.exp2(top - new_top)
            total = total * scale + jnp.sum(weights, axis=1, keepdims=True)
            mixed = mixed * scale + jnp.dot(
                weights.astype(bf16), values, preferred_element_type=f32
            )
            return new_top, total, mixed

        count = heads * tile
        state = (
            jnp.full((count, 1), masked_score, f32),
            jnp.zeros((count, 1), f32),
            jnp.zeros((count, HD), f32),
        )
        state = visit(diagonal, state, True)
        split = jnp.minimum(whole_from, diagonal)
        state = lax.fori_loop(lowest, split, lambda b, s: visit(b, s, True), state)
        split = jnp.maximum(split, lowest)
        _, total, mixed = lax.fori_loop(split, diagonal, lambda b, s: visit(b, s, False), state)
        mixed = (mixed / total).astype(bf16)
        for h in range(heads):
            mix[rows, h * HD : (h + 1) * HD] = mixed[h * tile : (h + 1) * tile]
    for c in out_copies:
        c.wait()
    share = tok_rows // narrow
    for k in range(narrow):
        start = pl.multiple_of((narrow_index ^ k) * share, share)
        part_refs[k][...] = contract_last(mix[pl.ds(start, share), :], w_out[...]).astype(bf16)
    flush.wait()


def join_kernel(narrow, base_ref, gain_ref, *rest):
    parts, outs = rest[:narrow], rest[narrow:]
    total = parts[0][...].astype(f32)
    for part in parts[1:]:
        total = total + part[...].astype(f32)
    rounded = (base_ref[...].astype(f32) + total).astype(bf16)
    if len(outs) > narrow:
        outs[narrow][...] = rounded
        rounded = norm_rows(rounded.astype(f32), gain_ref[...])
    for out in outs[:narrow]:
        out[...] = rounded


def ffn_kernel(narrow, *rest):
    x_refs, weights_ref = rest[:narrow], rest[narrow]
    rest = rest[narrow + 1 :]
    part_refs, (x, held, gate, hidden, sems) = rest[:narrow], rest[narrow:]
    copies = [
        pltpu.make_async_copy(weights_ref.at[:, j], held.at[j], sems.at[j]) for j in range(3)
    ]
    for c in copies:
        c.start()
    share = x_refs[0].shape[0]
    for k in range(narrow):
        x[k * share : (k + 1) * share, :] = x_refs[k][...]
    width = hidden.shape[1]
    depth = x.shape[1]
    tile = 256
    whole = width // tile

    def each_tile(body):
        @pl.loop(0, whole)
        def _(j):
            body(pl.ds(pl.multiple_of(j * tile, tile), tile), tile)

        if width % tile:
            body(slice(whole * tile, width), width - whole * tile)

    def gate_tile(lanes, size):
        block = held[0, :, :, lanes].reshape(depth, size)
        gate[:, lanes] = jnp.dot(x[...], block, preferred_element_type=f32)

    def up_tile(lanes, size):
        block = held[1, :, :, lanes].reshape(depth, size)
        up = jnp.dot(x[...], block, preferred_element_type=f32)
        value = gate[:, lanes]
        hidden[:, lanes] = (value / (1.0 + jnp.exp(-value)) * up).astype(bf16)

    copies[0].wait()
    each_tile(gate_tile)
    copies[1].wait()
    each_tile(up_tile)
    copies[2].wait()
    pieces, rows = held.shape[1], held.shape[2]
    group = 768 // rows
    for g in range(pieces // group):
        block = held[2, g * group : (g + 1) * group].reshape(group * rows, width)
        product = contract_last(hidden[...], block)
        lanes = slice(g * group * rows, (g + 1) * group * rows)
        for k in range(narrow):
            part_refs[k][:, lanes] = product[k * share : (k + 1) * share].astype(bf16)


def next_kernel(wide, narrow, wide_ref, narrow_ref, gain_ref, bias_ref, *rest):
    h_refs, pieces = rest[:narrow], rest[narrow : narrow + wide]
    out_ref, query_ref, keyval_ref, weight, sems = rest[narrow + wide :]
    wide_index, narrow_index = wide_ref[0], narrow_ref[0]
    copies = place_copies(pieces, weight, sems, wide_index)
    for c in copies:
        c.start()
    share = h_refs[0].shape[0]
    queries = query_ref.shape[1]
    for c in copies:
        c.wait()
    for k in range(narrow):
        rows = pl.ds(pl.multiple_of((narrow_index ^ k) * share, share), share)
        value = h_refs[k][...]
        out_ref[rows, :] = value
        normed = norm_rows(value.astype(f32), gain_ref[...])
        product = jnp.dot(normed, weight[...], preferred_element_type=f32) + bias_ref[...]
        query_ref[rows, :] = product[:, :queries].astype(bf16)
        keyval_ref[rows, :] = product[:, queries:].astype(bf16)


def fill_pages(source, seg_lengths, seg_offsets, block_table, first_page, page_count):
    pages_here = first_page + jnp.arange(page_count, dtype=jnp.int32)
    page_match = block_table[None, :, :] == pages_here[:, None, None]
    seg_grid = jnp.arange(block_table.shape[0], dtype=jnp.int32)[None, :, None]
    page_grid = jnp.arange(block_table.shape[1], dtype=jnp.int32)[None, None, :]
    page_owner = jnp.sum(jnp.where(page_match, seg_grid, 0), axis=(1, 2))
    logical = jnp.sum(jnp.where(page_match, page_grid, 0), axis=(1, 2))
    in_use = jnp.any(page_match, axis=(1, 2))
    first_token = lookup(seg_offsets, page_owner) + logical * PAGE_LEN
    filled = lookup(seg_lengths, page_owner) - logical * PAGE_LEN
    slot_index = jnp.arange(PAGE_LEN, dtype=jnp.int32)
    row_ids = jnp.clip(first_token[:, None] + slot_index[None, :], 0, source.shape[0] - 1)
    keep_slot = in_use[:, None] & (slot_index[None, :] < filled[:, None])
    taken_rows = jnp.take(source, row_ids.reshape(-1), axis=0).reshape(
        page_count, PAGE_LEN, source.shape[1]
    )
    return jnp.where(keep_slot[:, :, None], taken_rows, jnp.zeros((), source.dtype))


def local(
    wide,
    narrow,
    hidden_in,
    segment_ids,
    seg_lengths,
    seg_offsets,
    block_table,
    attn_gain,
    w_query,
    b_query,
    w_keyval,
    b_keyval,
    w_out,
    mlp_gain,
    w_gate,
    w_up,
    w_down,
    next_gain,
    w_query2,
    b_query2,
    w_keyval2,
    b_keyval2,
):
    tok_rows, depth = hidden_in.shape
    piece_rows = w_query.shape[0]
    query_width = w_query.shape[1]
    width = w_gate.shape[1]
    wide_index = lax.axis_index("wide")
    narrow_index = lax.axis_index("narrow")
    head_pair = narrow_index // 2
    kind_index = narrow_index % 2
    pair_offset = head_pair * 2 * HD
    share = tok_rows // narrow
    row_base = wide_index * tok_rows

    qkv_weight = jnp.concatenate(
        [w_query, lax.dynamic_slice_in_dim(w_keyval, pair_offset, 2 * HD, 1)], axis=1
    )
    qkv_bias = jnp.concatenate(
        [b_query, lax.dynamic_slice_in_dim(b_keyval, pair_offset, 2 * HD, 0)]
    ).astype(f32)[None]
    qkv_pieces = wide_pieces(qkv_weight, wide)


    token_start = lookup(seg_offsets, segment_ids)
    positions = row_base + jnp.arange(tok_rows, dtype=jnp.int32) - token_start
    half = HD // 2
    frequency = rope_base ** (-(jnp.arange(half, dtype=f32) * 2.0 / HD))
    angles = positions.astype(f32)[:, None] * frequency
    cosine, sine = jnp.cos(angles), jnp.sin(angles)
    cosine = jnp.concatenate([cosine, cosine], axis=1)
    sine = jnp.concatenate([-sine, sine], axis=1)

    packed = jnp.stack([w_gate, w_up, w_down.T])
    packed, cosine, sine, qkv_bias, *qkv_pieces = lax.optimization_barrier(
        (packed, cosine, sine, qkv_bias, *qkv_pieces)
    )
    ffn_weights = lax.all_gather(packed, "wide", axis=0, tiled=False)

    qkv_width = query_width + 2 * HD
    queries, keyvals = pl.pallas_call(
        functools.partial(qkv_kernel, wide),
        out_shape=(
            jax.ShapeDtypeStruct((tok_rows, query_width), bf16),
            jax.ShapeDtypeStruct((tok_rows, 2 * HD), bf16),
        ),
        in_specs=[smem_spec()] + [vmem_spec()] * 5 + [any_spec()] * wide,
        out_specs=(vmem_spec(), vmem_spec()),
        scratch_shapes=[VMEM((depth, qkv_width), bf16), pltpu.SemaphoreType.DMA((wide,))],
        compiler_params=params(32),
        cost_estimate=pl.CostEstimate(
            flops=2 * tok_rows * depth * qkv_width,
            bytes_accessed=2 * depth * (tok_rows + qkv_width),
            transcendentals=0,
        ),
        name="qkv",
    )(
        wide_index[None],
        hidden_in,
        attn_gain.astype(f32)[None],
        qkv_bias,
        cosine,
        sine,
        *qkv_pieces,
    )

    kv_pieces = wide_pieces(keyvals, wide)
    out_pieces = wide_pieces(w_out.T, wide)

    tile = 256
    total_rows = wide * tok_rows
    *parts, kv_all = pl.pallas_call(
        functools.partial(attend_kernel, wide, narrow, tile),
        out_shape=[jax.ShapeDtypeStruct((share, depth), bf16)] * narrow
        + [jax.ShapeDtypeStruct((total_rows, 2 * HD), bf16)],
        in_specs=[smem_spec()] * 3 + [vmem_spec()] * 2 + [any_spec()] * (2 * wide),
        out_specs=[vmem_spec()] * narrow + [any_spec()],
        scratch_shapes=[
            VMEM((total_rows, 2 * HD), bf16),
            VMEM((depth, query_width), bf16),
            VMEM((tok_rows, query_width), bf16),
            pltpu.SemaphoreType.DMA((wide,)),
            pltpu.SemaphoreType.DMA((wide,)),
            pltpu.SemaphoreType.DMA,
        ],
        compiler_params=params(40),
        cost_estimate=pl.CostEstimate(
            flops=8 * tok_rows * query_width * depth,
            bytes_accessed=4 * total_rows * HD,
            transcendentals=tok_rows * depth,
        ),
        name="attend",
    )(
        wide_index[None],
        narrow_index[None],
        token_start,
        token_start[:, None],
        queries,
        *kv_pieces,
        *out_pieces,
    )

    def join(parts, base_rows, gain, with_norm):
        shape = jax.ShapeDtypeStruct((share, depth), bf16)
        count = narrow + 1 if with_norm else narrow
        return pl.pallas_call(
            functools.partial(join_kernel, narrow),
            out_shape=[shape] * count,
            in_specs=[vmem_spec()] * (2 + narrow),
            out_specs=[vmem_spec()] * count,
            compiler_params=params(24),
            name="join",
        )(base_rows, gain, *parts)

    base_rows = lax.dynamic_slice_in_dim(hidden_in, narrow_index * share, share, 0)
    mlp_row = mlp_gain.astype(f32)[None]
    *normed, residual = join(narrow_swap(parts, narrow), base_rows, mlp_row, True)
    normed_pieces = narrow_swap(normed, narrow)

    parts = pl.pallas_call(
        functools.partial(ffn_kernel, narrow),
        out_shape=[jax.ShapeDtypeStruct((share, depth), bf16)] * narrow,
        in_specs=[vmem_spec()] * narrow + [any_spec()],
        out_specs=[vmem_spec()] * narrow,
        scratch_shapes=[
            VMEM((tok_rows, depth), bf16),
            VMEM((3, wide, piece_rows, width), bf16),
            VMEM((tok_rows, width), f32),
            VMEM((tok_rows, width), bf16),
            pltpu.SemaphoreType.DMA((3,)),
        ],
        compiler_params=params(52),
        cost_estimate=pl.CostEstimate(
            flops=6 * tok_rows * depth * width,
            bytes_accessed=6 * depth * width,
            transcendentals=tok_rows * width,
        ),
        name="ffn",
    )(*normed_pieces, ffn_weights)

    hidden_rows = join(narrow_swap(parts, narrow), residual, mlp_row, False)
    hidden_pieces = narrow_swap(hidden_rows, narrow)

    one_offset = pair_offset + kind_index * HD
    next_weight = jnp.concatenate(
        [w_query2, lax.dynamic_slice_in_dim(w_keyval2, one_offset, HD, 1)], axis=1
    )
    next_bias = jnp.concatenate(
        [b_query2, lax.dynamic_slice_in_dim(b_keyval2, one_offset, HD, 0)]
    ).astype(f32)[None]
    next_weight, _ = lax.optimization_barrier((next_weight, residual))
    next_pieces = wide_pieces(next_weight, wide)
    next_width = query_width + HD
    hidden_out, next_query, next_keyval = pl.pallas_call(
        functools.partial(next_kernel, wide, narrow),
        out_shape=(
            jax.ShapeDtypeStruct((tok_rows, depth), bf16),
            jax.ShapeDtypeStruct((tok_rows, query_width), bf16),
            jax.ShapeDtypeStruct((tok_rows, HD), bf16),
        ),
        in_specs=[smem_spec()] * 2 + [vmem_spec()] * (2 + narrow) + [any_spec()] * wide,
        out_specs=(vmem_spec(),) * 3,
        scratch_shapes=[VMEM((depth, next_width), bf16), pltpu.SemaphoreType.DMA((wide,))],
        compiler_params=params(32),
        cost_estimate=pl.CostEstimate(
            flops=2 * tok_rows * depth * next_width,
            bytes_accessed=2 * depth * (2 * tok_rows + next_width),
            transcendentals=0,
        ),
        name="next",
    )(
        wide_index[None],
        narrow_index[None],
        next_gain.astype(f32)[None],
        next_bias,
        *hidden_pieces,
        *next_pieces,
    )

    source = lax.dynamic_slice_in_dim(kv_all, kind_index * HD, HD, 1)
    page_count = tok_rows // PAGE_LEN + 1
    cache_block = fill_pages(
        source, seg_lengths, seg_offsets, block_table, wide_index * page_count, page_count
    )
    return (hidden_out, next_query, next_keyval, cache_block[None])


def solution(mesh):
    placed = (
        P("wide", None),
        P("wide"),
        P(),
        P(),
        P(),
        P(),
        P("wide", "narrow"),
        P("narrow"),
        P("wide", None),
        P(),
        P("narrow", "wide"),
        P(),
        P("wide", "narrow"),
        P("wide", "narrow"),
        P("narrow", "wide"),
        P(),
        P("wide", "narrow"),
        P("narrow"),
        P("wide", None),
        P(),
    )
    return jax.shard_map(
        functools.partial(local, mesh.shape["wide"], mesh.shape["narrow"]),
        mesh=mesh,
        in_specs=placed,
        out_specs=(
            P("wide", None),
            P("wide", "narrow"),
            P("wide", "narrow"),
            P("narrow", "wide", None, None),
        ),
        check_vma=False,
    )
```

```python
import functools
import math

import jax
import jax.numpy as jnp
from jax import lax
from jax.experimental import pallas as pl
from jax.experimental.pallas import tpu as pltpu
from jax.sharding import PartitionSpec as P

HD = 128
PAGE_LEN = 128

norm_eps = 1e-06
rope_base = 1000000.0
masked_score = -1e30

f32 = jnp.float32
bf16 = jnp.bfloat16
VMEM = pltpu.VMEM
SMEM = pltpu.SMEM


def vmem_spec():
    return pl.BlockSpec(memory_space=VMEM)


def any_spec():
    return pl.BlockSpec(memory_space=pl.ANY)


def hbm_spec():
    return pl.BlockSpec(memory_space=pltpu.HBM)


def smem_spec():
    return pl.BlockSpec(memory_space=SMEM)


def params(mib):
    return pltpu.CompilerParams(vmem_limit_bytes=mib << 20)


def norm_rows(values, gain_row):
    row_scale = lax.rsqrt(jnp.mean(values * values, axis=-1, keepdims=True) + norm_eps)
    return (values * row_scale * gain_row).astype(bf16)


def lookup(table, indices):
    table_match = indices[..., None] == jnp.arange(table.shape[0], dtype=jnp.int32)
    return jnp.sum(jnp.where(table_match, table, 0), axis=-1)


def exchange(value, axis, size, mask):
    return lax.ppermute(value, axis, [(i, i ^ mask) for i in range(size)])


def wide_pieces(value, size):
    pieces = {0: value}
    for mask in range(2, size, 2):
        pieces[mask] = exchange(value, "wide", size, mask)
    for mask in range(0, size, 2):
        pieces[mask + 1] = exchange(pieces[mask], "wide", size, 1)
    return [pieces[m] for m in range(size)]


def after(values, *tokens):
    return lax.optimization_barrier((tuple(values), tokens))[0]


class Relay:
    def __init__(self, value, size):
        self.size = size
        if size != 8:
            self.pieces = [(m, 0, piece) for m, piece in enumerate(wide_pieces(value, size))]
            return
        self.across = exchange(value, "wide", 8, 2)
        self.along = exchange(value, "wide", 8, 4)
        self.pieces = [(0, 0, value), (1, 0, exchange(value, "wide", 8, 1))]

    def pass_on(self, *tokens):
        if self.size != 8:
            return
        across, along = after([self.across, self.along], *tokens)
        half = across.shape[0] // 2
        top = exchange(across[:half], "wide", 8, 4)
        low = exchange(along[half:], "wide", 8, 2)
        for mask, offset, piece in ((2, 0, across), (4, 0, along), (6, 0, top), (6, half, low)):
            self.pieces.append((mask, offset, piece))
            self.pieces.append((mask | 1, offset, exchange(piece, "wide", 8, 1)))


def narrow_swap(pieces, size):
    return [pieces[0]] + [exchange(pieces[k], "narrow", size, k) for k in range(1, size)]


def place_copies(piece_refs, target, sems, wide_index):
    rows = piece_refs[0].shape[0]
    copies = []
    for m, piece in enumerate(piece_refs):
        start = pl.multiple_of((wide_index ^ m) * rows, rows)
        copies.append(pltpu.make_async_copy(piece, target.at[pl.ds(start, rows)], sems.at[m]))
    return copies


def contract_last(left, right):
    return lax.dot_general(left, right, (((1,), (1,)), ((), ())), preferred_element_type=f32)


def qkv_kernel(wide, index_ref, hidden_ref, gain_ref, bias_ref, cos_ref, sin_ref, *rest):
    pieces, (q_ref, kv_ref, out_ref, weight, sems) = rest[:wide], rest[wide:]
    copies = place_copies(pieces, weight, sems, index_ref[0])
    for c in copies:
        c.start()
    normed = norm_rows(hidden_ref[...].astype(f32), gain_ref[...])
    cosine, sine = cos_ref[...], sin_ref[...]
    for c in copies:
        c.wait()
    heads = q_ref.shape[1] // HD + 2
    for h in range(heads):
        lanes = slice(h * HD, (h + 1) * HD)
        if h % 2 == 0:
            wider = slice(h * HD, min(h + 2, heads) * HD)
            both = jnp.dot(normed, weight[:, wider], preferred_element_type=f32)
        value = both[:, (h % 2) * HD : (h % 2 + 1) * HD] + bias_ref[:, lanes]
        if h < heads - 1:
            value = value * cosine + pltpu.roll(value, HD // 2, 1) * sine
        value = value.astype(bf16)
        if h < heads - 2:
            q_ref[:, lanes] = value
        else:
            kv_ref[:, (h - heads + 2) * HD : (h - heads + 3) * HD] = value
    out_ref[...] = weight[:, heads * HD :]


def attend_kernel(wide, narrow, key_block, wide_ref, narrow_ref, spots_ref, starts_ref, q_ref, w_out, *rest):
    kv_pieces, rest = rest[:wide], rest[wide:]
    part_refs, (kv_out, keyvals, mix, kv_sems, flush_sem) = rest[:narrow], rest[narrow:]
    wide_index, narrow_index = wide_ref[0], narrow_ref[0]
    kv_copies = place_copies(kv_pieces, keyvals, kv_sems, wide_index)
    for c in kv_copies:
        c.start()
    for c in kv_copies:
        c.wait()
    flush = pltpu.make_async_copy(keyvals, kv_out, flush_sem)
    flush.start()
    tok_rows = q_ref.shape[0]
    heads = q_ref.shape[1] // HD
    tile = key_block
    row_base = wide_index * tok_rows
    factor = HD ** (-0.5) * math.log2(math.e)
    for t in range(tok_rows // tile):
        rows = slice(t * tile, (t + 1) * tile)
        stacked = jnp.concatenate(
            [q_ref[rows, h * HD : (h + 1) * HD] for h in range(heads)], axis=0
        )
        first = row_base + t * tile
        diagonal = first // tile
        lowest = spots_ref[t * tile] // tile
        whole_from = (spots_ref[(t + 1) * tile - 1] + tile - 1) // tile
        starts = jnp.concatenate([starts_ref[rows, :]] * heads, axis=0)
        own = first + lax.broadcasted_iota(jnp.int32, (tile, 1), 0)
        own = jnp.concatenate([own] * heads, axis=0)

        def visit(block, state, masked, stacked=stacked, starts=starts, own=own):
            top, total, mixed = state
            begin = pl.multiple_of(block * tile, tile)
            keys = keyvals[pl.ds(begin, tile), :HD]
            values = keyvals[pl.ds(begin, tile), HD:]
            scores = contract_last(stacked, keys) * factor
            if masked:
                spot = begin + lax.broadcasted_iota(jnp.int32, (1, tile), 1)
                scores = jnp.where((spot >= starts) & (spot <= own), scores, masked_score)
            new_top = jnp.maximum(top, jnp.max(scores, axis=1, keepdims=True))
            weights = jnp.exp2(scores - new_top)
            scale = jnp.exp2(top - new_top)
            total = total * scale + jnp.sum(weights, axis=1, keepdims=True)
            mixed = mixed * scale + jnp.dot(
                weights.astype(bf16), values, preferred_element_type=f32
            )
            return new_top, total, mixed

        count = heads * tile
        state = (
            jnp.full((count, 1), masked_score, f32),
            jnp.zeros((count, 1), f32),
            jnp.zeros((count, HD), f32),
        )
        state = visit(diagonal, state, True)
        split = jnp.minimum(whole_from, diagonal)
        state = lax.fori_loop(lowest, split, lambda b, s: visit(b, s, True), state)
        split = jnp.maximum(split, lowest)
        _, total, mixed = lax.fori_loop(split, diagonal, lambda b, s: visit(b, s, False), state)
        mixed = (mixed / total).astype(bf16)
        for h in range(heads):
            mix[rows, h * HD : (h + 1) * HD] = mixed[h * tile : (h + 1) * tile]
    share = tok_rows // narrow
    for k in range(narrow):
        start = pl.multiple_of((narrow_index ^ k) * share, share)
        part_refs[k][...] = contract_last(mix[pl.ds(start, share), :], w_out[...]).astype(bf16)
    flush.wait()


def join_kernel(narrow, base_ref, gain_ref, *rest):
    parts, outs = rest[:narrow], rest[narrow:]
    total = parts[0][...].astype(f32)
    for part in parts[1:]:
        total = total + part[...].astype(f32)
    rounded = (base_ref[...].astype(f32) + total).astype(bf16)
    if len(outs) > narrow:
        outs[narrow][...] = rounded
        rounded = norm_rows(rounded.astype(f32), gain_ref[...])
    for out in outs[:narrow]:
        out[...] = rounded


def ffn_kernel(narrow, piece_rows, spots, wide_ref, *rest):
    x_refs, rest = rest[:narrow], rest[narrow:]
    piece_refs, rest = rest[: len(spots)], rest[len(spots) :]
    part_refs, (x, held, gate, hidden, sems) = rest[:narrow], rest[narrow:]
    copies = [[], [], []]
    for j in range(3):
        for (mask, offset), piece in zip(spots, piece_refs):
            low = max(offset, j * piece_rows)
            high = min(offset + piece.shape[0], (j + 1) * piece_rows)
            if low >= high:
                continue
            start = (wide_ref[0] ^ mask) * piece_rows + low - j * piece_rows
            target = held.at[j, pl.ds(pl.multiple_of(start, 16), high - low)]
            source = piece.at[pl.ds(low - offset, high - low)]
            sem = sems.at[j, len(copies[j])]
            copies[j].append(pltpu.make_async_copy(source, target, sem))
    for c in copies[0] + copies[1] + copies[2]:
        c.start()
    share = x_refs[0].shape[0]
    for k in range(narrow):
        x[k * share : (k + 1) * share, :] = x_refs[k][...]
    depth, width = held.shape[1:]
    tile = 256
    whole = width // tile

    def arrive(j):
        for c in copies[j]:
            c.wait()

    def each_tile(body):
        @pl.loop(0, whole)
        def _(j):
            body(pl.ds(pl.multiple_of(j * tile, tile), tile))

        if width % tile:
            body(slice(whole * tile, width))

    def gate_tile(lanes):
        gate[:, lanes] = jnp.dot(x[...], held[0, :, lanes], preferred_element_type=f32)

    def up_tile(lanes):
        up = jnp.dot(x[...], held[1, :, lanes], preferred_element_type=f32)
        value = gate[:, lanes]
        hidden[:, lanes] = (value / (1.0 + jnp.exp(-value)) * up).astype(bf16)

    arrive(0)
    each_tile(gate_tile)
    arrive(1)
    each_tile(up_tile)
    arrive(2)
    group = 768
    for g in range(depth // group):
        lanes = slice(g * group, (g + 1) * group)
        product = contract_last(hidden[...], held[2, lanes, :])
        for k in range(narrow):
            part_refs[k][:, lanes] = product[k * share : (k + 1) * share].astype(bf16)


def next_kernel(wide, narrow, wide_ref, narrow_ref, gain_ref, bias_ref, *rest):
    h_refs, pieces = rest[:narrow], rest[narrow : narrow + wide]
    out_ref, query_ref, keyval_ref, weight, sems = rest[narrow + wide :]
    wide_index, narrow_index = wide_ref[0], narrow_ref[0]
    copies = place_copies(pieces, weight, sems, wide_index)
    for c in copies:
        c.start()
    share = h_refs[0].shape[0]
    queries = query_ref.shape[1]
    for c in copies:
        c.wait()
    for k in range(narrow):
        rows = pl.ds(pl.multiple_of((narrow_index ^ k) * share, share), share)
        value = h_refs[k][...]
        out_ref[rows, :] = value
        normed = norm_rows(value.astype(f32), gain_ref[...])
        product = jnp.dot(normed, weight[...], preferred_element_type=f32) + bias_ref[...]
        query_ref[rows, :] = product[:, :queries].astype(bf16)
        keyval_ref[rows, :] = product[:, queries:].astype(bf16)


def fill_pages(source, seg_lengths, seg_offsets, block_table, first_page, page_count):
    pages_here = first_page + jnp.arange(page_count, dtype=jnp.int32)
    page_match = block_table[None, :, :] == pages_here[:, None, None]
    seg_grid = jnp.arange(block_table.shape[0], dtype=jnp.int32)[None, :, None]
    page_grid = jnp.arange(block_table.shape[1], dtype=jnp.int32)[None, None, :]
    page_owner = jnp.sum(jnp.where(page_match, seg_grid, 0), axis=(1, 2))
    logical = jnp.sum(jnp.where(page_match, page_grid, 0), axis=(1, 2))
    in_use = jnp.any(page_match, axis=(1, 2))
    first_token = lookup(seg_offsets, page_owner) + logical * PAGE_LEN
    filled = lookup(seg_lengths, page_owner) - logical * PAGE_LEN
    slot_index = jnp.arange(PAGE_LEN, dtype=jnp.int32)
    row_ids = jnp.clip(first_token[:, None] + slot_index[None, :], 0, source.shape[0] - 1)
    keep_slot = in_use[:, None] & (slot_index[None, :] < filled[:, None])
    taken_rows = jnp.take(source, row_ids.reshape(-1), axis=0).reshape(
        page_count, PAGE_LEN, source.shape[1]
    )
    return jnp.where(keep_slot[:, :, None], taken_rows, jnp.zeros((), source.dtype))


def local(
    wide,
    narrow,
    hidden_in,
    segment_ids,
    seg_lengths,
    seg_offsets,
    block_table,
    attn_gain,
    w_query,
    b_query,
    w_keyval,
    b_keyval,
    w_out,
    mlp_gain,
    w_gate,
    w_up,
    w_down,
    next_gain,
    w_query2,
    b_query2,
    w_keyval2,
    b_keyval2,
):
    tok_rows, depth = hidden_in.shape
    piece_rows = w_query.shape[0]
    query_width = w_query.shape[1]
    width = w_gate.shape[1]
    wide_index = lax.axis_index("wide")
    narrow_index = lax.axis_index("narrow")
    head_pair = narrow_index // 2
    kind_index = narrow_index % 2
    pair_offset = head_pair * 2 * HD
    share = tok_rows // narrow
    row_base = wide_index * tok_rows

    qkv_weight = jnp.concatenate(
        [w_query, lax.dynamic_slice_in_dim(w_keyval, pair_offset, 2 * HD, 1), w_out.T], axis=1
    )
    qkv_bias = jnp.concatenate(
        [b_query, lax.dynamic_slice_in_dim(b_keyval, pair_offset, 2 * HD, 0)]
    ).astype(f32)[None]
    qkv_pieces = wide_pieces(qkv_weight, wide)


    token_start = lookup(seg_offsets, segment_ids)
    positions = row_base + jnp.arange(tok_rows, dtype=jnp.int32) - token_start
    half = HD // 2
    frequency = rope_base ** (-(jnp.arange(half, dtype=f32) * 2.0 / HD))
    angles = positions.astype(f32)[:, None] * frequency
    cosine, sine = jnp.cos(angles), jnp.sin(angles)
    cosine = jnp.concatenate([cosine, cosine], axis=1)
    sine = jnp.concatenate([-sine, sine], axis=1)

    one_offset = pair_offset + kind_index * HD
    next_weight = jnp.concatenate(
        [w_query2, lax.dynamic_slice_in_dim(w_keyval2, one_offset, HD, 1)], axis=1
    )
    next_bias = jnp.concatenate(
        [b_query2, lax.dynamic_slice_in_dim(b_keyval2, one_offset, HD, 0)]
    ).astype(f32)[None]
    base_rows = lax.dynamic_slice_in_dim(hidden_in, narrow_index * share, share, 0)
    mlp_row = mlp_gain.astype(f32)[None]
    next_row = next_gain.astype(f32)[None]
    starts_column = token_start[:, None]
    packed = jnp.concatenate([w_gate, w_up, w_down.T])
    early = (
        packed,
        cosine,
        sine,
        qkv_bias,
        next_weight,
        next_bias,
        base_rows,
        mlp_row,
        next_row,
        starts_column,
    )
    early, qkv_pieces = lax.optimization_barrier((early, qkv_pieces))
    packed, cosine, sine, qkv_bias, next_weight, next_bias, base_rows = early[:7]
    mlp_row, next_row, starts_column = early[7:]

    qkv_width = query_width + 2 * HD
    queries, keyvals, out_weight = pl.pallas_call(
        functools.partial(qkv_kernel, wide),
        out_shape=(
            jax.ShapeDtypeStruct((tok_rows, query_width), bf16),
            jax.ShapeDtypeStruct((tok_rows, 2 * HD), bf16),
            jax.ShapeDtypeStruct((depth, query_width), bf16),
        ),
        in_specs=[smem_spec()] + [vmem_spec()] * 5 + [any_spec()] * wide,
        out_specs=(vmem_spec(),) * 3,
        scratch_shapes=[VMEM((depth, qkv_width + query_width), bf16), pltpu.SemaphoreType.DMA((wide,))],
        compiler_params=params(60),
        cost_estimate=pl.CostEstimate(
            flops=2 * tok_rows * depth * qkv_width,
            bytes_accessed=2 * depth * (tok_rows + qkv_width),
            transcendentals=0,
        ),
        name="qkv",
    )(
        wide_index[None],
        hidden_in,
        attn_gain.astype(f32)[None],
        qkv_bias,
        cosine,
        sine,
        *qkv_pieces,
    )

    kv_pieces = wide_pieces(keyvals, wide)

    (packed,) = after([packed], *kv_pieces[2::2])
    relay = Relay(packed, wide)

    tile = 256
    total_rows = wide * tok_rows
    *parts, kv_all = pl.pallas_call(
        functools.partial(attend_kernel, wide, narrow, tile),
        out_shape=[jax.ShapeDtypeStruct((share, depth), bf16)] * narrow
        + [jax.ShapeDtypeStruct((total_rows, 2 * HD), bf16)],
        in_specs=[smem_spec()] * 3 + [vmem_spec()] * 3 + [any_spec()] * wide,
        out_specs=[vmem_spec()] * narrow + [hbm_spec()],
        scratch_shapes=[
            VMEM((total_rows, 2 * HD), bf16),
            VMEM((tok_rows, query_width), bf16),
            pltpu.SemaphoreType.DMA((wide,)),
            pltpu.SemaphoreType.DMA,
        ],
        compiler_params=params(60),
        cost_estimate=pl.CostEstimate(
            flops=8 * tok_rows * query_width * depth,
            bytes_accessed=4 * total_rows * HD,
            transcendentals=tok_rows * depth,
        ),
        name="attend",
    )(
        wide_index[None],
        narrow_index[None],
        token_start,
        starts_column,
        queries,
        out_weight,
        *kv_pieces,
    )

    def join(parts, base_rows, gain, with_norm):
        shape = jax.ShapeDtypeStruct((share, depth), bf16)
        count = narrow + 1 if with_norm else narrow
        return pl.pallas_call(
            functools.partial(join_kernel, narrow),
            out_shape=[shape] * count,
            in_specs=[vmem_spec()] * (2 + narrow),
            out_specs=[vmem_spec()] * count,
            compiler_params=params(60),
            name="join",
        )(base_rows, gain, *parts)

    *normed, residual = join(narrow_swap(parts, narrow), base_rows, mlp_row, True)
    normed_pieces = narrow_swap(normed, narrow)

    source = lax.dynamic_slice_in_dim(kv_all, kind_index * HD, HD, 1)
    page_count = tok_rows // PAGE_LEN + 1
    cache_block = fill_pages(
        source, seg_lengths, seg_offsets, block_table, wide_index * page_count, page_count
    )
    relay.pass_on(normed_pieces[1])
    normed_pieces = after(normed_pieces, cache_block)
    spots = [(mask, offset) for mask, offset, _ in relay.pieces]
    bulk = [piece for _, _, piece in relay.pieces]
    parts = pl.pallas_call(
        functools.partial(ffn_kernel, narrow, piece_rows, spots),
        out_shape=[jax.ShapeDtypeStruct((share, depth), bf16)] * narrow,
        in_specs=[smem_spec()] + [vmem_spec()] * narrow + [hbm_spec()] * len(bulk),
        out_specs=[vmem_spec()] * narrow,
        scratch_shapes=[
            VMEM((tok_rows, depth), bf16),
            VMEM((3, depth, width), bf16),
            VMEM((tok_rows, width), f32),
            VMEM((tok_rows, width), bf16),
            pltpu.SemaphoreType.DMA((3, len(spots))),
        ],
        compiler_params=params(60),
        cost_estimate=pl.CostEstimate(
            flops=6 * tok_rows * depth * width,
            bytes_accessed=6 * depth * width,
            transcendentals=tok_rows * width,
        ),
        name="ffn",
    )(wide_index[None], *normed_pieces, *bulk)

    hidden_rows = join(narrow_swap(parts, narrow), residual, mlp_row, False)
    hidden_pieces = narrow_swap(hidden_rows, narrow)

    (next_weight,) = after([next_weight], parts[0])
    next_pieces = wide_pieces(next_weight, wide)
    next_width = query_width + HD
    hidden_out, next_query, next_keyval = pl.pallas_call(
        functools.partial(next_kernel, wide, narrow),
        out_shape=(
            jax.ShapeDtypeStruct((tok_rows, depth), bf16),
            jax.ShapeDtypeStruct((tok_rows, query_width), bf16),
            jax.ShapeDtypeStruct((tok_rows, HD), bf16),
        ),
        in_specs=[smem_spec()] * 2 + [vmem_spec()] * (2 + narrow) + [any_spec()] * wide,
        out_specs=(vmem_spec(),) * 3,
        scratch_shapes=[VMEM((depth, next_width), bf16), pltpu.SemaphoreType.DMA((wide,))],
        compiler_params=params(60),
        cost_estimate=pl.CostEstimate(
            flops=2 * tok_rows * depth * next_width,
            bytes_accessed=2 * depth * (2 * tok_rows + next_width),
            transcendentals=0,
        ),
        name="next",
    )(
        wide_index[None],
        narrow_index[None],
        next_row,
        next_bias,
        *hidden_pieces,
        *next_pieces,
    )

    return (hidden_out, next_query, next_keyval, cache_block[None])


def solution(mesh):
    placed = (
        P("wide", None),
        P("wide"),
        P(),
        P(),
        P(),
        P(),
        P("wide", "narrow"),
        P("narrow"),
        P("wide", None),
        P(),
        P("narrow", "wide"),
        P(),
        P("wide", "narrow"),
        P("wide", "narrow"),
        P("narrow", "wide"),
        P(),
        P("wide", "narrow"),
        P("narrow"),
        P("wide", None),
        P(),
    )
    return jax.shard_map(
        functools.partial(local, mesh.shape["wide"], mesh.shape["narrow"]),
        mesh=mesh,
        in_specs=placed,
        out_specs=(
            P("wide", None),
            P("wide", "narrow"),
            P("wide", "narrow"),
            P("narrow", "wide", None, None),
        ),
        check_vma=False,
    )
```

```python
import functools
import math

import jax
import jax.numpy as jnp
from jax import lax
from jax.experimental import pallas as pl
from jax.experimental.pallas import tpu as pltpu
from jax.sharding import PartitionSpec as P

HD = 128
PAGE_LEN = 128

norm_eps = 1e-06
rope_base = 1000000.0
masked_score = -1e30

f32 = jnp.float32
bf16 = jnp.bfloat16
VMEM = pltpu.VMEM
SMEM = pltpu.SMEM


def vmem_spec():
    return pl.BlockSpec(memory_space=VMEM)


def any_spec():
    return pl.BlockSpec(memory_space=pl.ANY)


def hbm_spec():
    return pl.BlockSpec(memory_space=pltpu.HBM)


def smem_spec():
    return pl.BlockSpec(memory_space=SMEM)


def params(mib):
    return pltpu.CompilerParams(vmem_limit_bytes=mib << 20)


def norm_rows(values, gain_row):
    row_scale = lax.rsqrt(jnp.mean(values * values, axis=-1, keepdims=True) + norm_eps)
    return (values * row_scale * gain_row).astype(bf16)


def lookup(table, indices):
    table_match = indices[..., None] == jnp.arange(table.shape[0], dtype=jnp.int32)
    return jnp.sum(jnp.where(table_match, table, 0), axis=-1)


def exchange(value, axis, size, mask):
    return lax.ppermute(value, axis, [(i, i ^ mask) for i in range(size)])


def wide_pieces(value, size):
    pieces = {0: value}
    for mask in range(2, size, 2):
        pieces[mask] = exchange(value, "wide", size, mask)
    for mask in range(0, size, 2):
        pieces[mask + 1] = exchange(pieces[mask], "wide", size, 1)
    return [pieces[m] for m in range(size)]


def after(values, *tokens):
    return lax.optimization_barrier((tuple(values), tokens))[0]


def narrow_swap(pieces, size):
    return [pieces[0]] + [exchange(pieces[k], "narrow", size, k) for k in range(1, size)]


def place_copies(piece_refs, target, sems, wide_index):
    rows = piece_refs[0].shape[0]
    copies = []
    for m, piece in enumerate(piece_refs):
        start = pl.multiple_of((wide_index ^ m) * rows, rows)
        copies.append(pltpu.make_async_copy(piece, target.at[pl.ds(start, rows)], sems.at[m]))
    return copies


def contract_last(left, right):
    return lax.dot_general(left, right, (((1,), (1,)), ((), ())), preferred_element_type=f32)


def qkv_kernel(wide, index_ref, hidden_ref, gain_ref, bias_ref, cos_ref, sin_ref, *rest):
    pieces, (q_ref, kv_ref, out_ref, weight, sems) = rest[:wide], rest[wide:]
    copies = place_copies(pieces, weight, sems, index_ref[0])
    for c in copies:
        c.start()
    normed = norm_rows(hidden_ref[...].astype(f32), gain_ref[...])
    cosine, sine = cos_ref[...], sin_ref[...]
    for c in copies:
        c.wait()
    heads = q_ref.shape[1] // HD + 2
    for h in range(heads):
        lanes = slice(h * HD, (h + 1) * HD)
        if h % 2 == 0:
            wider = slice(h * HD, min(h + 2, heads) * HD)
            both = jnp.dot(normed, weight[:, wider], preferred_element_type=f32)
        value = both[:, (h % 2) * HD : (h % 2 + 1) * HD] + bias_ref[:, lanes]
        if h < heads - 1:
            value = value * cosine + pltpu.roll(value, HD // 2, 1) * sine
        value = value.astype(bf16)
        if h < heads - 2:
            q_ref[:, lanes] = value
        else:
            kv_ref[:, (h - heads + 2) * HD : (h - heads + 3) * HD] = value
    out_ref[...] = weight[:, heads * HD :]


def attend_kernel(wide, shares, wide_ref, narrow_ref, spots_ref, starts_ref, q_ref, w_out, *rest):
    first_call = len(rest) > 4
    wide_index, narrow_index = wide_ref[0], narrow_ref[0]
    if first_call:
        kv_pieces, rest = rest[:wide], rest[wide:]
        part_refs, (kv_out, keyvals, mix, kv_sems, flush_sem) = rest[:2], rest[2:]
        kv_copies = place_copies(kv_pieces, keyvals, kv_sems, wide_index)
        for c in kv_copies:
            c.start()
        for c in kv_copies:
            c.wait()
        flush = pltpu.make_async_copy(keyvals, kv_out, flush_sem)
        flush.start()
    else:
        keyvals, *part_refs, mix = rest
    share = part_refs[0].shape[0]
    tile = 2 * share
    tok_rows = q_ref.shape[0]
    heads = q_ref.shape[1] // HD
    row_base = wide_index * tok_rows
    factor = HD ** (-0.5) * math.log2(math.e)
    begin_row = pl.multiple_of(((narrow_index ^ shares[0]) // 2) * tile, tile)
    rows = pl.ds(begin_row, tile)
    stacked = jnp.concatenate([q_ref[rows, h * HD : (h + 1) * HD] for h in range(heads)], axis=0)
    first = row_base + begin_row
    diagonal = first // tile
    lowest = spots_ref[begin_row] // tile
    whole_from = (spots_ref[begin_row + tile - 1] + tile - 1) // tile
    starts = jnp.concatenate([starts_ref[rows, :]] * heads, axis=0)
    own = first + lax.broadcasted_iota(jnp.int32, (tile, 1), 0)
    own = jnp.concatenate([own] * heads, axis=0)

    def visit(block, state, masked):
        top, total, mixed = state
        begin = pl.multiple_of(block * tile, tile)
        keys = keyvals[pl.ds(begin, tile), :HD]
        values = keyvals[pl.ds(begin, tile), HD:]
        scores = contract_last(stacked, keys) * factor
        if masked:
            spot = begin + lax.broadcasted_iota(jnp.int32, (1, tile), 1)
            scores = jnp.where((spot >= starts) & (spot <= own), scores, masked_score)
        new_top = jnp.maximum(top, jnp.max(scores, axis=1, keepdims=True))
        weights = jnp.exp2(scores - new_top)
        scale = jnp.exp2(top - new_top)
        total = total * scale + jnp.sum(weights, axis=1, keepdims=True)
        mixed = mixed * scale + jnp.dot(weights.astype(bf16), values, preferred_element_type=f32)
        return new_top, total, mixed

    count = heads * tile
    state = (
        jnp.full((count, 1), masked_score, f32),
        jnp.zeros((count, 1), f32),
        jnp.zeros((count, HD), f32),
    )
    state = visit(diagonal, state, True)
    split = jnp.minimum(whole_from, diagonal)
    state = lax.fori_loop(lowest, split, lambda b, s: visit(b, s, True), state)
    split = jnp.maximum(split, lowest)
    _, total, mixed = lax.fori_loop(split, diagonal, lambda b, s: visit(b, s, False), state)
    mixed = (mixed / total).astype(bf16)
    for h in range(heads):
        mix[:, h * HD : (h + 1) * HD] = mixed[h * tile : (h + 1) * tile]
    for k, part_ref in zip(shares, part_refs):
        start = pl.multiple_of(((narrow_index ^ k) % 2) * share, share)
        part_ref[...] = contract_last(mix[pl.ds(start, share), :], w_out[...]).astype(bf16)
    if first_call:
        flush.wait()


def join_kernel(narrow, base_ref, gain_ref, *rest):
    parts, outs = rest[:narrow], rest[narrow:]
    total = parts[0][...].astype(f32)
    for part in parts[1:]:
        total = total + part[...].astype(f32)
    rounded = (base_ref[...].astype(f32) + total).astype(bf16)
    if len(outs) > narrow:
        outs[narrow][...] = rounded
        rounded = norm_rows(rounded.astype(f32), gain_ref[...])
    for out in outs[:narrow]:
        out[...] = rounded


def ffn_kernel(count, *rest):
    x_refs, weights_ref, rest = rest[:count], rest[count], rest[count + 1 :]
    part_refs, (x, held, gate, hidden, sems) = rest[:count], rest[count:]
    copies = [
        pltpu.make_async_copy(weights_ref.at[:, j], held.at[j], sems.at[j]) for j in range(3)
    ]
    for c in copies:
        c.start()
    share = x_refs[0].shape[0]
    for k in range(len(x_refs)):
        x[k * share : (k + 1) * share, :] = x_refs[k][...]
    depth, width = x.shape[1], hidden.shape[1]
    tile = 256
    whole = width // tile

    def each_tile(body):
        @pl.loop(0, whole)
        def _(j):
            body(pl.ds(pl.multiple_of(j * tile, tile), tile))

        if width % tile:
            body(slice(whole * tile, width))

    def block(j, lanes):
        part = held[j, :, :, lanes]
        return part.reshape(depth, part.shape[-1])

    def gate_tile(lanes):
        gate[:, lanes] = jnp.dot(x[...], block(0, lanes), preferred_element_type=f32)

    def up_tile(lanes):
        up = jnp.dot(x[...], block(1, lanes), preferred_element_type=f32)
        value = gate[:, lanes]
        hidden[:, lanes] = (value / (1.0 + jnp.exp(-value)) * up).astype(bf16)

    copies[0].wait()
    each_tile(gate_tile)
    copies[1].wait()
    each_tile(up_tile)
    copies[2].wait()
    pieces, rows = held.shape[1], held.shape[2]
    group = 768 // rows
    for g in range(pieces // group):
        lanes = slice(g * group * rows, (g + 1) * group * rows)
        down = held[2, g * group : (g + 1) * group].reshape(group * rows, width)
        product = contract_last(hidden[...], down)
        for k in range(len(x_refs)):
            part_refs[k][:, lanes] = product[k * share : (k + 1) * share].astype(bf16)


def next_kernel(wide, narrow, wide_ref, narrow_ref, gain_ref, bias_ref, *rest):
    h_refs, pieces = rest[:narrow], rest[narrow : narrow + wide]
    out_ref, query_ref, keyval_ref, weight, sems = rest[narrow + wide :]
    wide_index, narrow_index = wide_ref[0], narrow_ref[0]
    copies = place_copies(pieces, weight, sems, wide_index)
    for c in copies:
        c.start()
    share = h_refs[0].shape[0]
    queries = query_ref.shape[1]
    for c in copies:
        c.wait()
    for k in range(narrow):
        rows = pl.ds(pl.multiple_of((narrow_index ^ k) * share, share), share)
        value = h_refs[k][...]
        out_ref[rows, :] = value
        normed = norm_rows(value.astype(f32), gain_ref[...])
        product = jnp.dot(normed, weight[...], preferred_element_type=f32) + bias_ref[...]
        query_ref[rows, :] = product[:, :queries].astype(bf16)
        keyval_ref[rows, :] = product[:, queries:].astype(bf16)


def fill_pages(source, seg_lengths, seg_offsets, block_table, first_page, page_count):
    pages_here = first_page + jnp.arange(page_count, dtype=jnp.int32)
    page_match = block_table[None, :, :] == pages_here[:, None, None]
    seg_grid = jnp.arange(block_table.shape[0], dtype=jnp.int32)[None, :, None]
    page_grid = jnp.arange(block_table.shape[1], dtype=jnp.int32)[None, None, :]
    page_owner = jnp.sum(jnp.where(page_match, seg_grid, 0), axis=(1, 2))
    logical = jnp.sum(jnp.where(page_match, page_grid, 0), axis=(1, 2))
    in_use = jnp.any(page_match, axis=(1, 2))
    first_token = lookup(seg_offsets, page_owner) + logical * PAGE_LEN
    filled = lookup(seg_lengths, page_owner) - logical * PAGE_LEN
    slot_index = jnp.arange(PAGE_LEN, dtype=jnp.int32)
    row_ids = jnp.clip(first_token[:, None] + slot_index[None, :], 0, source.shape[0] - 1)
    keep_slot = in_use[:, None] & (slot_index[None, :] < filled[:, None])
    taken_rows = jnp.take(source, row_ids.reshape(-1), axis=0).reshape(
        page_count, PAGE_LEN, source.shape[1]
    )
    return jnp.where(keep_slot[:, :, None], taken_rows, jnp.zeros((), source.dtype))


def local(
    wide,
    narrow,
    hidden_in,
    segment_ids,
    seg_lengths,
    seg_offsets,
    block_table,
    attn_gain,
    w_query,
    b_query,
    w_keyval,
    b_keyval,
    w_out,
    mlp_gain,
    w_gate,
    w_up,
    w_down,
    next_gain,
    w_query2,
    b_query2,
    w_keyval2,
    b_keyval2,
):
    tok_rows, depth = hidden_in.shape
    piece_rows = w_query.shape[0]
    query_width = w_query.shape[1]
    width = w_gate.shape[1]
    wide_index = lax.axis_index("wide")
    narrow_index = lax.axis_index("narrow")
    head_pair = narrow_index // 2
    kind_index = narrow_index % 2
    pair_offset = head_pair * 2 * HD
    share = tok_rows // narrow
    row_base = wide_index * tok_rows

    qkv_weight = jnp.concatenate(
        [w_query, lax.dynamic_slice_in_dim(w_keyval, pair_offset, 2 * HD, 1), w_out.T], axis=1
    )
    qkv_bias = jnp.concatenate(
        [b_query, lax.dynamic_slice_in_dim(b_keyval, pair_offset, 2 * HD, 0)]
    ).astype(f32)[None]
    qkv_pieces = wide_pieces(qkv_weight, wide)


    token_start = lookup(seg_offsets, segment_ids)
    positions = row_base + jnp.arange(tok_rows, dtype=jnp.int32) - token_start
    half = HD // 2
    frequency = rope_base ** (-(jnp.arange(half, dtype=f32) * 2.0 / HD))
    angles = positions.astype(f32)[:, None] * frequency
    cosine, sine = jnp.cos(angles), jnp.sin(angles)
    cosine = jnp.concatenate([cosine, cosine], axis=1)
    sine = jnp.concatenate([-sine, sine], axis=1)

    one_offset = pair_offset + kind_index * HD
    next_weight = jnp.concatenate(
        [w_query2, lax.dynamic_slice_in_dim(w_keyval2, one_offset, HD, 1)], axis=1
    )
    next_bias = jnp.concatenate(
        [b_query2, lax.dynamic_slice_in_dim(b_keyval2, one_offset, HD, 0)]
    ).astype(f32)[None]
    base_rows = lax.dynamic_slice_in_dim(hidden_in, narrow_index * share, share, 0)
    mlp_row = mlp_gain.astype(f32)[None]
    next_row = next_gain.astype(f32)[None]
    starts_column = token_start[:, None]
    packed = jnp.stack([w_gate, w_up, w_down.T])
    (packed,) = after([packed], *qkv_pieces[2::2])
    ffn_weights = lax.all_gather(packed, "wide", axis=0, tiled=False)
    early = (
        cosine,
        sine,
        qkv_bias,
        next_weight,
        next_bias,
        base_rows,
        mlp_row,
        next_row,
        starts_column,
    )
    early, qkv_pieces = lax.optimization_barrier((early, qkv_pieces))
    cosine, sine, qkv_bias, next_weight, next_bias, base_rows = early[:6]
    mlp_row, next_row, starts_column = early[6:]

    qkv_width = query_width + 2 * HD
    queries, keyvals, out_weight = pl.pallas_call(
        functools.partial(qkv_kernel, wide),
        out_shape=(
            jax.ShapeDtypeStruct((tok_rows, query_width), bf16),
            jax.ShapeDtypeStruct((tok_rows, 2 * HD), bf16),
            jax.ShapeDtypeStruct((depth, query_width), bf16),
        ),
        in_specs=[smem_spec()] + [vmem_spec()] * 5 + [any_spec()] * wide,
        out_specs=(vmem_spec(),) * 3,
        scratch_shapes=[VMEM((depth, qkv_width + query_width), bf16), pltpu.SemaphoreType.DMA((wide,))],
        compiler_params=params(60),
        cost_estimate=pl.CostEstimate(
            flops=2 * tok_rows * depth * qkv_width,
            bytes_accessed=2 * depth * (tok_rows + qkv_width),
            transcendentals=0,
        ),
        name="qkv",
    )(
        wide_index[None],
        hidden_in,
        attn_gain.astype(f32)[None],
        qkv_bias,
        cosine,
        sine,
        *qkv_pieces,
    )

    kv_pieces = wide_pieces(keyvals, wide)

    total_rows = wide * tok_rows
    share_shape = jax.ShapeDtypeStruct((share, depth), bf16)

    def attend(shares, first_call, sources):
        kv_shape = jax.ShapeDtypeStruct((total_rows, 2 * HD), bf16)
        mix = VMEM((2 * share, query_width), bf16)
        gather_scratch = [
            VMEM((total_rows, 2 * HD), bf16),
            mix,
            pltpu.SemaphoreType.DMA((wide,)),
            pltpu.SemaphoreType.DMA,
        ]
        source_specs = [any_spec()] * wide if first_call else [vmem_spec()]
        return pl.pallas_call(
            functools.partial(attend_kernel, wide, shares),
            out_shape=[share_shape] * 2 + [kv_shape] * first_call,
            in_specs=[smem_spec()] * 3 + [vmem_spec()] * 3 + source_specs,
            out_specs=[vmem_spec()] * 2 + [hbm_spec()] * first_call,
            scratch_shapes=gather_scratch if first_call else [mix],
            compiler_params=params(60 if first_call else 24),
            cost_estimate=pl.CostEstimate(
                flops=4 * tok_rows * query_width * depth,
                bytes_accessed=4 * total_rows * HD,
                transcendentals=tok_rows * depth,
            ),
            name="attend",
        )(
            wide_index[None],
            narrow_index[None],
            token_start,
            starts_column,
            queries,
            out_weight,
            *sources,
        )

    far_two, far_three, kv_all = attend((2, 3), True, kv_pieces)
    near_zero, near_one = attend((0, 1), False, [kv_all])
    parts = [near_zero, near_one, far_two, far_three]

    def join(parts, base_rows, gain, with_norm):
        shape = jax.ShapeDtypeStruct((share, depth), bf16)
        count = narrow + 1 if with_norm else narrow
        return pl.pallas_call(
            functools.partial(join_kernel, narrow),
            out_shape=[shape] * count,
            in_specs=[vmem_spec()] * (2 + narrow),
            out_specs=[vmem_spec()] * count,
            compiler_params=params(60),
            name="join",
        )(base_rows, gain, *parts)

    *normed, residual = join(narrow_swap(parts, narrow), base_rows, mlp_row, True)
    normed_pieces = narrow_swap(normed, narrow)

    source = lax.dynamic_slice_in_dim(kv_all, kind_index * HD, HD, 1)
    page_count = tok_rows // PAGE_LEN + 1
    cache_block = fill_pages(
        source, seg_lengths, seg_offsets, block_table, wide_index * page_count, page_count
    )
    def feed_forward(x_shares):
        count = len(x_shares)
        return pl.pallas_call(
            functools.partial(ffn_kernel, count),
            out_shape=[share_shape] * count,
            in_specs=[vmem_spec()] * count + [hbm_spec()],
            out_specs=[vmem_spec()] * count,
            scratch_shapes=[
                VMEM((count * share, depth), bf16),
                VMEM((3, wide, piece_rows, width), bf16),
                VMEM((count * share, width), f32),
                VMEM((count * share, width), bf16),
                pltpu.SemaphoreType.DMA((3,)),
            ],
            compiler_params=params(60 if x_shares is far else 44),
            cost_estimate=pl.CostEstimate(
                flops=6 * count * share * depth * width,
                bytes_accessed=6 * depth * width,
                transcendentals=count * share * width,
            ),
            name="ffn",
        )(*x_shares, ffn_weights)

    far = normed_pieces[2:]
    far_two, far_three = feed_forward(far)
    near_zero, near_one = feed_forward(list(after(normed_pieces[:2], far_two)))
    parts = [near_zero, near_one, far_two, far_three]

    hidden_rows = join(narrow_swap(parts, narrow), residual, mlp_row, False)
    hidden_pieces = narrow_swap(hidden_rows, narrow)

    (next_weight,) = after([next_weight], far_two)
    next_pieces = wide_pieces(next_weight, wide)
    next_width = query_width + HD
    hidden_out, next_query, next_keyval = pl.pallas_call(
        functools.partial(next_kernel, wide, narrow),
        out_shape=(
            jax.ShapeDtypeStruct((tok_rows, depth), bf16),
            jax.ShapeDtypeStruct((tok_rows, query_width), bf16),
            jax.ShapeDtypeStruct((tok_rows, HD), bf16),
        ),
        in_specs=[smem_spec()] * 2 + [vmem_spec()] * (2 + narrow) + [any_spec()] * wide,
        out_specs=(vmem_spec(),) * 3,
        scratch_shapes=[VMEM((depth, next_width), bf16), pltpu.SemaphoreType.DMA((wide,))],
        compiler_params=params(40),
        cost_estimate=pl.CostEstimate(
            flops=2 * tok_rows * depth * next_width,
            bytes_accessed=2 * depth * (2 * tok_rows + next_width),
            transcendentals=0,
        ),
        name="next",
    )(
        wide_index[None],
        narrow_index[None],
        next_row,
        next_bias,
        *hidden_pieces,
        *next_pieces,
    )

    return (hidden_out, next_query, next_keyval, cache_block[None])


def solution(mesh):
    placed = (
        P("wide", None),
        P("wide"),
        P(),
        P(),
        P(),
        P(),
        P("wide", "narrow"),
        P("narrow"),
        P("wide", None),
        P(),
        P("narrow", "wide"),
        P(),
        P("wide", "narrow"),
        P("wide", "narrow"),
        P("narrow", "wide"),
        P(),
        P("wide", "narrow"),
        P("narrow"),
        P("wide", None),
        P(),
    )
    return jax.shard_map(
        functools.partial(local, mesh.shape["wide"], mesh.shape["narrow"]),
        mesh=mesh,
        in_specs=placed,
        out_specs=(
            P("wide", None),
            P("wide", "narrow"),
            P("wide", "narrow"),
            P("narrow", "wide", None, None),
        ),
        check_vma=False,
    )
```

```python
import functools
import math

import jax
import jax.numpy as jnp
from jax import lax
from jax.experimental import pallas as pl
from jax.experimental.pallas import tpu as pltpu
from jax.sharding import PartitionSpec as P

HD = 128
PAGE_LEN = 128

norm_eps = 1e-06
rope_base = 1000000.0
masked_score = -1e30

f32 = jnp.float32
bf16 = jnp.bfloat16
VMEM = pltpu.VMEM
SMEM = pltpu.SMEM


def vmem_spec():
    return pl.BlockSpec(memory_space=VMEM)


def any_spec():
    return pl.BlockSpec(memory_space=pl.ANY)


def hbm_spec():
    return pl.BlockSpec(memory_space=pltpu.HBM)


def smem_spec():
    return pl.BlockSpec(memory_space=SMEM)


def params(mib):
    return pltpu.CompilerParams(vmem_limit_bytes=mib << 20)


def norm_rows(values, gain_row):
    row_scale = lax.rsqrt(jnp.mean(values * values, axis=-1, keepdims=True) + norm_eps)
    return (values * row_scale * gain_row).astype(bf16)


def lookup(table, indices):
    table_match = indices[..., None] == jnp.arange(table.shape[0], dtype=jnp.int32)
    return jnp.sum(jnp.where(table_match, table, 0), axis=-1)


def exchange(value, axis, size, mask):
    return lax.ppermute(value, axis, [(i, i ^ mask) for i in range(size)])


def wide_pieces(value, size):
    pieces = {0: value}
    for mask in range(2, size, 2):
        pieces[mask] = exchange(value, "wide", size, mask)
    for mask in range(0, size, 2):
        pieces[mask + 1] = exchange(pieces[mask], "wide", size, 1)
    return [pieces[m] for m in range(size)]


def after(values, *tokens):
    return lax.optimization_barrier((tuple(values), tokens))[0]


def narrow_swap(pieces, size):
    return [pieces[0]] + [exchange(pieces[k], "narrow", size, k) for k in range(1, size)]


def narrow_spread(copies, size):
    near = exchange(copies[1], "narrow", size, 1)
    far = exchange(copies[2], "narrow", size, 3)
    return [copies[0], near, exchange(far, "narrow", size, 1), far]


def place_copies(piece_refs, target, sems, wide_index):
    rows = piece_refs[0].shape[0]
    copies = []
    for m, piece in enumerate(piece_refs):
        start = pl.multiple_of((wide_index ^ m) * rows, rows)
        copies.append(pltpu.make_async_copy(piece, target.at[pl.ds(start, rows)], sems.at[m]))
    return copies


def contract_last(left, right):
    return lax.dot_general(left, right, (((1,), (1,)), ((), ())), preferred_element_type=f32)


def qkv_kernel(wide, index_ref, hidden_ref, gain_ref, bias_ref, cos_ref, sin_ref, *rest):
    pieces, (q_ref, kv_ref, out_ref, weight, sems) = rest[:wide], rest[wide:]
    copies = place_copies(pieces, weight, sems, index_ref[0])
    for c in copies:
        c.start()
    normed = norm_rows(hidden_ref[...].astype(f32), gain_ref[...])
    cosine, sine = cos_ref[...], sin_ref[...]
    for c in copies:
        c.wait()
    heads = q_ref.shape[1] // HD + 2
    for h in range(heads):
        lanes = slice(h * HD, (h + 1) * HD)
        if h % 2 == 0:
            wider = slice(h * HD, min(h + 2, heads) * HD)
            both = jnp.dot(normed, weight[:, wider], preferred_element_type=f32)
        value = both[:, (h % 2) * HD : (h % 2 + 1) * HD] + bias_ref[:, lanes]
        if h < heads - 1:
            value = value * cosine + pltpu.roll(value, HD // 2, 1) * sine
        value = value.astype(bf16)
        if h < heads - 2:
            q_ref[:, lanes] = value
        else:
            kv_ref[:, (h - heads + 2) * HD : (h - heads + 3) * HD] = value
    out_ref[...] = weight[:, heads * HD :]


def attend_kernel(wide, shares, wide_ref, narrow_ref, spots_ref, starts_ref, q_ref, w_out, *rest):
    first_call = len(rest) > 4
    wide_index, narrow_index = wide_ref[0], narrow_ref[0]
    if first_call:
        kv_pieces, rest = rest[:wide], rest[wide:]
        part_refs, (kv_out, keyvals, mix, kv_sems, flush_sem) = rest[:2], rest[2:]
        kv_copies = place_copies(kv_pieces, keyvals, kv_sems, wide_index)
        for c in kv_copies:
            c.start()
        for c in kv_copies:
            c.wait()
        flush = pltpu.make_async_copy(keyvals, kv_out, flush_sem)
        flush.start()
    else:
        keyvals, *part_refs, mix = rest
    share = part_refs[0].shape[0]
    tile = 2 * share
    tok_rows = q_ref.shape[0]
    heads = q_ref.shape[1] // HD
    row_base = wide_index * tok_rows
    factor = HD ** (-0.5) * math.log2(math.e)
    begin_row = pl.multiple_of(((narrow_index ^ shares[0]) // 2) * tile, tile)
    rows = pl.ds(begin_row, tile)
    stacked = jnp.concatenate([q_ref[rows, h * HD : (h + 1) * HD] for h in range(heads)], axis=0)
    first = row_base + begin_row
    diagonal = first // tile
    lowest = spots_ref[begin_row] // tile
    whole_from = (spots_ref[begin_row + tile - 1] + tile - 1) // tile
    starts = jnp.concatenate([starts_ref[rows, :]] * heads, axis=0)
    own = first + lax.broadcasted_iota(jnp.int32, (tile, 1), 0)
    own = jnp.concatenate([own] * heads, axis=0)

    def visit(block, state, masked):
        top, total, mixed = state
        begin = pl.multiple_of(block * tile, tile)
        keys = keyvals[pl.ds(begin, tile), :HD]
        values = keyvals[pl.ds(begin, tile), HD:]
        scores = contract_last(stacked, keys) * factor
        if masked:
            spot = begin + lax.broadcasted_iota(jnp.int32, (1, tile), 1)
            scores = jnp.where((spot >= starts) & (spot <= own), scores, masked_score)
        new_top = jnp.maximum(top, jnp.max(scores, axis=1, keepdims=True))
        weights = jnp.exp2(scores - new_top)
        scale = jnp.exp2(top - new_top)
        total = total * scale + jnp.sum(weights, axis=1, keepdims=True)
        mixed = mixed * scale + jnp.dot(weights.astype(bf16), values, preferred_element_type=f32)
        return new_top, total, mixed

    count = heads * tile
    state = (
        jnp.full((count, 1), masked_score, f32),
        jnp.zeros((count, 1), f32),
        jnp.zeros((count, HD), f32),
    )
    state = visit(diagonal, state, True)
    split = jnp.minimum(whole_from, diagonal)
    state = lax.fori_loop(lowest, split, lambda b, s: visit(b, s, True), state)
    split = jnp.maximum(split, lowest)
    _, total, mixed = lax.fori_loop(split, diagonal, lambda b, s: visit(b, s, False), state)
    mixed = (mixed / total).astype(bf16)
    for h in range(heads):
        mix[:, h * HD : (h + 1) * HD] = mixed[h * tile : (h + 1) * tile]
    for k, part_ref in zip(shares, part_refs):
        start = pl.multiple_of(((narrow_index ^ k) % 2) * share, share)
        part_ref[...] = contract_last(mix[pl.ds(start, share), :], w_out[...]).astype(bf16)
    if first_call:
        flush.wait()


def join_kernel(narrow, base_ref, gain_ref, *rest):
    parts, outs = rest[:narrow], rest[narrow:]
    total = parts[0][...].astype(f32)
    for part in parts[1:]:
        total = total + part[...].astype(f32)
    rounded = (base_ref[...].astype(f32) + total).astype(bf16)
    if len(outs) > 3:
        outs[3][...] = rounded
        rounded = norm_rows(rounded.astype(f32), gain_ref[...])
    for out in outs[:3]:
        out[...] = rounded


def ffn_kernel(count, *rest):
    x_refs, weights_ref, rest = rest[:count], rest[count], rest[count + 1 :]
    part_refs, (x, held, gate, hidden, sems) = rest[:count], rest[count:]
    copies = [
        pltpu.make_async_copy(weights_ref.at[:, j], held.at[j], sems.at[j]) for j in range(3)
    ]
    for c in copies:
        c.start()
    share = x_refs[0].shape[0]
    for k in range(len(x_refs)):
        x[k * share : (k + 1) * share, :] = x_refs[k][...]
    depth, width = x.shape[1], hidden.shape[1]
    tile = 256
    whole = width // tile

    def each_tile(body):
        @pl.loop(0, whole)
        def _(j):
            body(pl.ds(pl.multiple_of(j * tile, tile), tile))

        if width % tile:
            body(slice(whole * tile, width))

    def block(j, lanes):
        part = held[j, :, :, lanes]
        return part.reshape(depth, part.shape[-1])

    def gate_tile(lanes):
        gate[:, lanes] = jnp.dot(x[...], block(0, lanes), preferred_element_type=f32)

    def up_tile(lanes):
        up = jnp.dot(x[...], block(1, lanes), preferred_element_type=f32)
        value = gate[:, lanes]
        hidden[:, lanes] = (value / (1.0 + jnp.exp(-value)) * up).astype(bf16)

    copies[0].wait()
    each_tile(gate_tile)
    copies[1].wait()
    each_tile(up_tile)
    copies[2].wait()
    pieces, rows = held.shape[1], held.shape[2]
    group = 768 // rows
    for g in range(pieces // group):
        lanes = slice(g * group * rows, (g + 1) * group * rows)
        down = held[2, g * group : (g + 1) * group].reshape(group * rows, width)
        product = contract_last(hidden[...], down)
        for k in range(len(x_refs)):
            part_refs[k][:, lanes] = product[k * share : (k + 1) * share].astype(bf16)


def next_kernel(wide, shares, wide_ref, narrow_ref, gain_ref, bias_ref, *rest):
    count = len(shares)
    h_refs, pieces = rest[:count], rest[count : count + wide]
    *outs, weight, query, keyval, sems, out_sems = rest[-8:]
    copies = place_copies(pieces, weight, sems, wide_ref[0])
    for c in copies:
        c.start()
    share = h_refs[0].shape[0]
    width = query.shape[1]
    flushes = []

    def flush(source, k, j):
        begin = pl.multiple_of((narrow_ref[0] ^ k) * share, share)
        target = outs[j].at[pl.ds(begin, share)]
        copy = pltpu.make_async_copy(source, target, out_sems.at[len(flushes)])
        copy.start()
        flushes.append(copy)

    for i, k in enumerate(shares):
        flush(h_refs[i], k, 0)
    for c in copies:
        c.wait()
    for i, k in enumerate(shares):
        rows = slice(i * share, (i + 1) * share)
        normed = norm_rows(h_refs[i][...].astype(f32), gain_ref[...])
        product = jnp.dot(normed, weight[...], preferred_element_type=f32) + bias_ref[...]
        query[rows, :] = product[:, :width].astype(bf16)
        keyval[rows, :] = product[:, width:].astype(bf16)
        flush(query.at[pl.ds(i * share, share)], k, 1)
        flush(keyval.at[pl.ds(i * share, share)], k, 2)
    for c in flushes:
        c.wait()


def fill_pages(source, seg_lengths, seg_offsets, block_table, first_page, page_count):
    pages_here = first_page + jnp.arange(page_count, dtype=jnp.int32)
    page_match = block_table[None, :, :] == pages_here[:, None, None]
    seg_grid = jnp.arange(block_table.shape[0], dtype=jnp.int32)[None, :, None]
    page_grid = jnp.arange(block_table.shape[1], dtype=jnp.int32)[None, None, :]
    page_owner = jnp.sum(jnp.where(page_match, seg_grid, 0), axis=(1, 2))
    logical = jnp.sum(jnp.where(page_match, page_grid, 0), axis=(1, 2))
    in_use = jnp.any(page_match, axis=(1, 2))
    first_token = lookup(seg_offsets, page_owner) + logical * PAGE_LEN
    filled = lookup(seg_lengths, page_owner) - logical * PAGE_LEN
    slot_index = jnp.arange(PAGE_LEN, dtype=jnp.int32)
    row_ids = jnp.clip(first_token[:, None] + slot_index[None, :], 0, source.shape[0] - 1)
    keep_slot = in_use[:, None] & (slot_index[None, :] < filled[:, None])
    taken_rows = jnp.take(source, row_ids.reshape(-1), axis=0).reshape(
        page_count, PAGE_LEN, source.shape[1]
    )
    return jnp.where(keep_slot[:, :, None], taken_rows, jnp.zeros((), source.dtype))


def local(
    wide,
    narrow,
    hidden_in,
    segment_ids,
    seg_lengths,
    seg_offsets,
    block_table,
    attn_gain,
    w_query,
    b_query,
    w_keyval,
    b_keyval,
    w_out,
    mlp_gain,
    w_gate,
    w_up,
    w_down,
    next_gain,
    w_query2,
    b_query2,
    w_keyval2,
    b_keyval2,
):
    tok_rows, depth = hidden_in.shape
    piece_rows = w_query.shape[0]
    query_width = w_query.shape[1]
    width = w_gate.shape[1]
    wide_index = lax.axis_index("wide")
    narrow_index = lax.axis_index("narrow")
    head_pair = narrow_index // 2
    kind_index = narrow_index % 2
    pair_offset = head_pair * 2 * HD
    share = tok_rows // narrow
    row_base = wide_index * tok_rows

    qkv_weight = jnp.concatenate(
        [w_query, lax.dynamic_slice_in_dim(w_keyval, pair_offset, 2 * HD, 1), w_out.T], axis=1
    )
    qkv_bias = jnp.concatenate(
        [b_query, lax.dynamic_slice_in_dim(b_keyval, pair_offset, 2 * HD, 0)]
    ).astype(f32)[None]
    qkv_pieces = wide_pieces(qkv_weight, wide)


    token_start = lookup(seg_offsets, segment_ids)
    positions = row_base + jnp.arange(tok_rows, dtype=jnp.int32) - token_start
    half = HD // 2
    frequency = rope_base ** (-(jnp.arange(half, dtype=f32) * 2.0 / HD))
    angles = positions.astype(f32)[:, None] * frequency
    cosine, sine = jnp.cos(angles), jnp.sin(angles)
    cosine = jnp.concatenate([cosine, cosine], axis=1)
    sine = jnp.concatenate([-sine, sine], axis=1)

    one_offset = pair_offset + kind_index * HD
    next_weight = jnp.concatenate(
        [w_query2, lax.dynamic_slice_in_dim(w_keyval2, one_offset, HD, 1)], axis=1
    )
    next_bias = jnp.concatenate(
        [b_query2, lax.dynamic_slice_in_dim(b_keyval2, one_offset, HD, 0)]
    ).astype(f32)[None]
    base_rows = lax.dynamic_slice_in_dim(hidden_in, narrow_index * share, share, 0)
    mlp_row = mlp_gain.astype(f32)[None]
    next_row = next_gain.astype(f32)[None]
    starts_column = token_start[:, None]
    packed = jnp.stack([w_gate, w_up, w_down.T])
    (packed,) = after([packed], qkv_pieces[1])
    ffn_weights = lax.all_gather(packed, "wide", axis=0, tiled=False)
    early = (
        cosine,
        sine,
        qkv_bias,
        next_weight,
        next_bias,
        base_rows,
        mlp_row,
        next_row,
        starts_column,
    )
    early, qkv_pieces = lax.optimization_barrier((early, qkv_pieces))
    cosine, sine, qkv_bias, next_weight, next_bias, base_rows = early[:6]
    mlp_row, next_row, starts_column = early[6:]

    qkv_width = query_width + 2 * HD
    queries, keyvals, out_weight = pl.pallas_call(
        functools.partial(qkv_kernel, wide),
        out_shape=(
            jax.ShapeDtypeStruct((tok_rows, query_width), bf16),
            jax.ShapeDtypeStruct((tok_rows, 2 * HD), bf16),
            jax.ShapeDtypeStruct((depth, query_width), bf16),
        ),
        in_specs=[smem_spec()] + [vmem_spec()] * 5 + [any_spec()] * wide,
        out_specs=(vmem_spec(),) * 3,
        scratch_shapes=[VMEM((depth, qkv_width + query_width), bf16), pltpu.SemaphoreType.DMA((wide,))],
        compiler_params=params(60),
        cost_estimate=pl.CostEstimate(
            flops=2 * tok_rows * depth * qkv_width,
            bytes_accessed=2 * depth * (tok_rows + qkv_width),
            transcendentals=0,
        ),
        name="qkv",
    )(
        wide_index[None],
        hidden_in,
        attn_gain.astype(f32)[None],
        qkv_bias,
        cosine,
        sine,
        *qkv_pieces,
    )

    kv_pieces = wide_pieces(keyvals, wide)

    total_rows = wide * tok_rows
    share_shape = jax.ShapeDtypeStruct((share, depth), bf16)

    def attend(shares, first_call, sources):
        kv_shape = jax.ShapeDtypeStruct((total_rows, 2 * HD), bf16)
        mix = VMEM((2 * share, query_width), bf16)
        gather_scratch = [
            VMEM((total_rows, 2 * HD), bf16),
            mix,
            pltpu.SemaphoreType.DMA((wide,)),
            pltpu.SemaphoreType.DMA,
        ]
        source_specs = [any_spec()] * wide if first_call else [vmem_spec()]
        return pl.pallas_call(
            functools.partial(attend_kernel, wide, shares),
            out_shape=[share_shape] * 2 + [kv_shape] * first_call,
            in_specs=[smem_spec()] * 3 + [vmem_spec()] * 3 + source_specs,
            out_specs=[vmem_spec()] * 2 + [hbm_spec()] * first_call,
            scratch_shapes=gather_scratch if first_call else [mix],
            compiler_params=params(60 if first_call else 24),
            cost_estimate=pl.CostEstimate(
                flops=4 * tok_rows * query_width * depth,
                bytes_accessed=4 * total_rows * HD,
                transcendentals=tok_rows * depth,
            ),
            name="attend",
        )(
            wide_index[None],
            narrow_index[None],
            token_start,
            starts_column,
            queries,
            out_weight,
            *sources,
        )

    far_two, far_three, kv_all = attend((2, 3), True, kv_pieces)
    near_zero, near_one = attend((0, 1), False, [kv_all])
    parts = [near_zero, near_one, far_two, far_three]

    def join(parts, base_rows, gain, with_norm):
        shape = jax.ShapeDtypeStruct((share, depth), bf16)
        count = 4 if with_norm else 3
        return pl.pallas_call(
            functools.partial(join_kernel, narrow),
            out_shape=[shape] * count,
            in_specs=[vmem_spec()] * (2 + narrow),
            out_specs=[vmem_spec()] * count,
            compiler_params=params(60),
            name="join",
        )(base_rows, gain, *parts)

    *normed, residual = join(narrow_swap(parts, narrow), base_rows, mlp_row, True)
    normed_pieces = narrow_spread(normed, narrow)

    source = lax.dynamic_slice_in_dim(kv_all, kind_index * HD, HD, 1)
    page_count = tok_rows // PAGE_LEN + 1
    cache_block = fill_pages(
        source, seg_lengths, seg_offsets, block_table, wide_index * page_count, page_count
    )
    def feed_forward(x_shares):
        count = len(x_shares)
        return pl.pallas_call(
            functools.partial(ffn_kernel, count),
            out_shape=[share_shape] * count,
            in_specs=[vmem_spec()] * count + [hbm_spec()],
            out_specs=[vmem_spec()] * count,
            scratch_shapes=[
                VMEM((count * share, depth), bf16),
                VMEM((3, wide, piece_rows, width), bf16),
                VMEM((count * share, width), f32),
                VMEM((count * share, width), bf16),
                pltpu.SemaphoreType.DMA((3,)),
            ],
            compiler_params=params(60 if x_shares is far else 44),
            cost_estimate=pl.CostEstimate(
                flops=6 * count * share * depth * width,
                bytes_accessed=6 * depth * width,
                transcendentals=count * share * width,
            ),
            name="ffn",
        )(*x_shares, ffn_weights)

    far = [normed_pieces[3], normed_pieces[0]]
    part_three, part_zero = feed_forward(far)
    part_one, part_two = feed_forward(list(after(normed_pieces[1:3], part_three)))
    parts = [part_zero, part_one, part_two, part_three]

    (next_weight,) = after([next_weight], part_three)
    next_pieces = wide_pieces(next_weight, wide)
    (residual,) = after([residual], *next_pieces)
    hidden_rows = join(narrow_swap(parts, narrow), residual, mlp_row, False)
    hidden_pieces = narrow_spread(hidden_rows, narrow)

    next_width = query_width + HD
    def project(shares, outputs):
        count = len(shares)
        operands = 4 + count + wide
        return pl.pallas_call(
            functools.partial(next_kernel, wide, shares),
            out_shape=(
                jax.ShapeDtypeStruct((tok_rows, depth), bf16),
                jax.ShapeDtypeStruct((tok_rows, query_width), bf16),
                jax.ShapeDtypeStruct((tok_rows, HD), bf16),
            ),
            in_specs=[smem_spec()] * 2
            + [vmem_spec()] * (2 + count)
            + [any_spec()] * wide
            + [hbm_spec()] * len(outputs),
            out_specs=(hbm_spec(),) * 3,
            scratch_shapes=[
                VMEM((depth, next_width), bf16),
                VMEM((count * share, query_width), bf16),
                VMEM((count * share, HD), bf16),
                pltpu.SemaphoreType.DMA((wide,)),
                pltpu.SemaphoreType.DMA((3 * count,)),
            ],
            input_output_aliases={operands + i: i for i in range(len(outputs))},
            compiler_params=params(40),
            cost_estimate=pl.CostEstimate(
                flops=2 * count * share * depth * next_width,
                bytes_accessed=2 * depth * (2 * tok_rows + next_width),
                transcendentals=0,
            ),
            name="next",
        )(
            wide_index[None],
            narrow_index[None],
            next_row,
            next_bias,
            *[hidden_pieces[k] for k in shares],
            *next_pieces,
            *outputs,
        )

    outputs = project((0, 1, 3), ())
    hidden_out, next_query, next_keyval = project((2,), outputs)

    return (hidden_out, next_query, next_keyval, cache_block[None])


def solution(mesh):
    placed = (
        P("wide", None),
        P("wide"),
        P(),
        P(),
        P(),
        P(),
        P("wide", "narrow"),
        P("narrow"),
        P("wide", None),
        P(),
        P("narrow", "wide"),
        P(),
        P("wide", "narrow"),
        P("wide", "narrow"),
        P("narrow", "wide"),
        P(),
        P("wide", "narrow"),
        P("narrow"),
        P("wide", None),
        P(),
    )
    return jax.shard_map(
        functools.partial(local, mesh.shape["wide"], mesh.shape["narrow"]),
        mesh=mesh,
        in_specs=placed,
        out_specs=(
            P("wide", None),
            P("wide", "narrow"),
            P("wide", "narrow"),
            P("narrow", "wide", None, None),
        ),
        check_vma=False,
    )
```

```python
import functools
import math

import jax
import jax.numpy as jnp
from jax import lax
from jax.experimental import pallas as pl
from jax.experimental.pallas import tpu as pltpu
from jax.sharding import PartitionSpec as P

HD = 128
PAGE_LEN = 128

norm_eps = 1e-06
rope_base = 1000000.0
masked_score = -1e30

f32 = jnp.float32
bf16 = jnp.bfloat16
VMEM = pltpu.VMEM
SMEM = pltpu.SMEM


def vmem_spec():
    return pl.BlockSpec(memory_space=VMEM)


def any_spec():
    return pl.BlockSpec(memory_space=pl.ANY)


def hbm_spec():
    return pl.BlockSpec(memory_space=pltpu.HBM)


def smem_spec():
    return pl.BlockSpec(memory_space=SMEM)


def params(mib):
    return pltpu.CompilerParams(vmem_limit_bytes=mib << 20)


def norm_rows(values, gain_row):
    row_scale = lax.rsqrt(jnp.mean(values * values, axis=-1, keepdims=True) + norm_eps)
    return (values * row_scale * gain_row).astype(bf16)


def lookup(table, indices):
    table_match = indices[..., None] == jnp.arange(table.shape[0], dtype=jnp.int32)
    return jnp.sum(jnp.where(table_match, table, 0), axis=-1)


def exchange(value, axis, size, mask):
    return lax.ppermute(value, axis, [(i, i ^ mask) for i in range(size)])


def wide_pieces(value, size, *tokens):
    pieces = {0: value}
    for mask in range(2, size, 2):
        pieces[mask] = exchange(value, "wide", size, mask)
    for mask in range(0, size, 2):
        source = pieces[mask]
        if tokens and mask:
            (source,) = after([source], *tokens)
        pieces[mask + 1] = exchange(source, "wide", size, 1)
    return [pieces[m] for m in range(size)]


def after(values, *tokens):
    return lax.optimization_barrier((tuple(values), tokens))[0]


def narrow_swap(pieces, size):
    return [pieces[0]] + [exchange(pieces[k], "narrow", size, k) for k in range(1, size)]


def narrow_spread(copies, size):
    near = exchange(copies[1], "narrow", size, 1)
    far = exchange(copies[2], "narrow", size, 3)
    return [copies[0], near, exchange(far, "narrow", size, 1), far]


def place_copies(piece_refs, target, sems, wide_index):
    rows = piece_refs[0].shape[0]
    copies = []
    for m, piece in enumerate(piece_refs):
        start = pl.multiple_of((wide_index ^ m) * rows, rows)
        copies.append(pltpu.make_async_copy(piece, target.at[pl.ds(start, rows)], sems.at[m]))
    return copies


def contract_last(left, right):
    return lax.dot_general(left, right, (((1,), (1,)), ((), ())), preferred_element_type=f32)


def qkv_kernel(wide, index_ref, hidden_ref, gain_ref, bias_ref, cos_ref, sin_ref, *rest):
    pieces, (q_ref, kv_ref, out_ref, weight, sems) = rest[:wide], rest[wide:]
    copies = place_copies(pieces, weight, sems, index_ref[0])
    for c in copies:
        c.start()
    normed = norm_rows(hidden_ref[...].astype(f32), gain_ref[...])
    cosine, sine = cos_ref[...], sin_ref[...]
    for c in copies:
        c.wait()
    heads = q_ref.shape[1] // HD + 2
    for h in range(heads):
        lanes = slice(h * HD, (h + 1) * HD)
        if h % 2 == 0:
            wider = slice(h * HD, min(h + 2, heads) * HD)
            both = jnp.dot(normed, weight[:, wider], preferred_element_type=f32)
        value = both[:, (h % 2) * HD : (h % 2 + 1) * HD] + bias_ref[:, lanes]
        if h < heads - 1:
            value = value * cosine + pltpu.roll(value, HD // 2, 1) * sine
        value = value.astype(bf16)
        if h < heads - 2:
            q_ref[:, lanes] = value
        else:
            kv_ref[:, (h - heads + 2) * HD : (h - heads + 3) * HD] = value
    out_ref[...] = weight[:, heads * HD :]


def attend_kernel(wide, shares, wide_ref, narrow_ref, spots_ref, starts_ref, q_ref, w_out, *rest):
    first_call = len(rest) > 4
    wide_index, narrow_index = wide_ref[0], narrow_ref[0]
    if first_call:
        kv_pieces, rest = rest[:wide], rest[wide:]
        part_refs, (kv_out, keyvals, mix, kv_sems, flush_sem) = rest[:2], rest[2:]
        kv_copies = place_copies(kv_pieces, keyvals, kv_sems, wide_index)
        for c in kv_copies:
            c.start()
        for c in kv_copies:
            c.wait()
        flush = pltpu.make_async_copy(keyvals, kv_out, flush_sem)
        flush.start()
    else:
        keyvals, *part_refs, mix = rest
    share = part_refs[0].shape[0]
    tile = 2 * share
    tok_rows = q_ref.shape[0]
    heads = q_ref.shape[1] // HD
    row_base = wide_index * tok_rows
    factor = HD ** (-0.5) * math.log2(math.e)
    begin_row = pl.multiple_of(((narrow_index ^ shares[0]) // 2) * tile, tile)
    rows = pl.ds(begin_row, tile)
    stacked = jnp.concatenate([q_ref[rows, h * HD : (h + 1) * HD] for h in range(heads)], axis=0)
    first = row_base + begin_row
    diagonal = first // tile
    lowest = spots_ref[begin_row] // tile
    whole_from = (spots_ref[begin_row + tile - 1] + tile - 1) // tile
    starts = jnp.concatenate([starts_ref[rows, :]] * heads, axis=0)
    own = first + lax.broadcasted_iota(jnp.int32, (tile, 1), 0)
    own = jnp.concatenate([own] * heads, axis=0)

    def visit(block, state, masked):
        top, total, mixed = state
        begin = pl.multiple_of(block * tile, tile)
        keys = keyvals[pl.ds(begin, tile), :HD]
        values = keyvals[pl.ds(begin, tile), HD:]
        scores = contract_last(stacked, keys) * factor
        if masked:
            spot = begin + lax.broadcasted_iota(jnp.int32, (1, tile), 1)
            scores = jnp.where((spot >= starts) & (spot <= own), scores, masked_score)
        new_top = jnp.maximum(top, jnp.max(scores, axis=1, keepdims=True))
        weights = jnp.exp2(scores - new_top)
        scale = jnp.exp2(top - new_top)
        total = total * scale + jnp.sum(weights, axis=1, keepdims=True)
        mixed = mixed * scale + jnp.dot(weights.astype(bf16), values, preferred_element_type=f32)
        return new_top, total, mixed

    count = heads * tile
    state = (
        jnp.full((count, 1), masked_score, f32),
        jnp.zeros((count, 1), f32),
        jnp.zeros((count, HD), f32),
    )
    state = visit(diagonal, state, True)
    split = jnp.minimum(whole_from, diagonal)
    state = lax.fori_loop(lowest, split, lambda b, s: visit(b, s, True), state)
    split = jnp.maximum(split, lowest)
    _, total, mixed = lax.fori_loop(split, diagonal, lambda b, s: visit(b, s, False), state)
    mixed = (mixed / total).astype(bf16)
    for h in range(heads):
        mix[:, h * HD : (h + 1) * HD] = mixed[h * tile : (h + 1) * tile]
    for k, part_ref in zip(shares, part_refs):
        start = pl.multiple_of(((narrow_index ^ k) % 2) * share, share)
        part_ref[...] = contract_last(mix[pl.ds(start, share), :], w_out[...]).astype(bf16)
    if first_call:
        flush.wait()


def join_kernel(narrow, base_ref, gain_ref, *rest):
    parts, outs = rest[:narrow], rest[narrow:]
    total = parts[0][...].astype(f32)
    for part in parts[1:]:
        total = total + part[...].astype(f32)
    rounded = (base_ref[...].astype(f32) + total).astype(bf16)
    if len(outs) > 3:
        outs[3][...] = rounded
        rounded = norm_rows(rounded.astype(f32), gain_ref[...])
    for out in outs[:3]:
        out[...] = rounded


def ffn_kernel(count, *rest):
    x_refs, weights_ref, rest = rest[:count], rest[count], rest[count + 1 :]
    part_refs, (x, held, gate, hidden, sems) = rest[:count], rest[count:]
    copies = [
        [
            pltpu.make_async_copy(weights_ref.at[p, j], held.at[j, p], sems.at[j, p])
            for p in range(held.shape[1])
        ]
        for j in range(3)
    ]
    for group in copies:
        for c in group:
            c.start()
    share = x_refs[0].shape[0]
    for k in range(len(x_refs)):
        x[k * share : (k + 1) * share, :] = x_refs[k][...]
    depth, width = x.shape[1], hidden.shape[1]
    tile = 1024
    whole = width // tile

    def each_tile(body):
        @pl.loop(0, whole)
        def _(j):
            body(pl.ds(pl.multiple_of(j * tile, tile), tile))

        if width % tile:
            body(slice(whole * tile, width))

    def block(j, lanes):
        part = held[j, :, :, lanes]
        return part.reshape(depth, part.shape[-1])

    def gate_tile(lanes):
        gate[:, lanes] = jnp.dot(x[...], block(0, lanes), preferred_element_type=f32)

    def up_tile(lanes):
        up = jnp.dot(x[...], block(1, lanes), preferred_element_type=f32)
        value = gate[:, lanes]
        hidden[:, lanes] = (value / (1.0 + jnp.exp(-value)) * up).astype(bf16)

    for c in copies[0]:
        c.wait()
    each_tile(gate_tile)
    for c in copies[1]:
        c.wait()
    each_tile(up_tile)
    for c in copies[2]:
        c.wait()
    pieces, rows = held.shape[1], held.shape[2]
    group = 768 // rows
    for g in range(pieces // group):
        lanes = slice(g * group * rows, (g + 1) * group * rows)
        down = held[2, g * group : (g + 1) * group].reshape(group * rows, width)
        product = contract_last(hidden[...], down)
        for k in range(len(x_refs)):
            part_refs[k][:, lanes] = product[k * share : (k + 1) * share].astype(bf16)


def next_kernel(shares, narrow_ref, gain_ref, bias_ref, weight, *rest):
    h_refs = rest[: len(shares)]
    *outs, query, keyval, out_sems = rest[-6:]
    share = h_refs[0].shape[0]
    width = query.shape[1]
    flushes = []

    def flush(source, k, j):
        begin = pl.multiple_of((narrow_ref[0] ^ k) * share, share)
        target = outs[j].at[pl.ds(begin, share)]
        copy = pltpu.make_async_copy(source, target, out_sems.at[len(flushes)])
        copy.start()
        flushes.append(copy)

    for i, k in enumerate(shares):
        flush(h_refs[i], k, 0)
    for i, k in enumerate(shares):
        rows = slice(i * share, (i + 1) * share)
        normed = norm_rows(h_refs[i][...].astype(f32), gain_ref[...])
        product = jnp.dot(normed, weight[...], preferred_element_type=f32) + bias_ref[...]
        query[rows, :] = product[:, :width].astype(bf16)
        keyval[rows, :] = product[:, width:].astype(bf16)
        flush(query.at[pl.ds(i * share, share)], k, 1)
        flush(keyval.at[pl.ds(i * share, share)], k, 2)
    for c in flushes:
        c.wait()


def fill_pages(source, seg_lengths, seg_offsets, block_table, first_page, page_count):
    pages_here = first_page + jnp.arange(page_count, dtype=jnp.int32)
    page_match = block_table[None, :, :] == pages_here[:, None, None]
    seg_grid = jnp.arange(block_table.shape[0], dtype=jnp.int32)[None, :, None]
    page_grid = jnp.arange(block_table.shape[1], dtype=jnp.int32)[None, None, :]
    page_owner = jnp.sum(jnp.where(page_match, seg_grid, 0), axis=(1, 2))
    logical = jnp.sum(jnp.where(page_match, page_grid, 0), axis=(1, 2))
    in_use = jnp.any(page_match, axis=(1, 2))
    first_token = lookup(seg_offsets, page_owner) + logical * PAGE_LEN
    filled = lookup(seg_lengths, page_owner) - logical * PAGE_LEN
    slot_index = jnp.arange(PAGE_LEN, dtype=jnp.int32)
    row_ids = jnp.clip(first_token[:, None] + slot_index[None, :], 0, source.shape[0] - 1)
    keep_slot = in_use[:, None] & (slot_index[None, :] < filled[:, None])
    taken_rows = jnp.take(source, row_ids.reshape(-1), axis=0).reshape(
        page_count, PAGE_LEN, source.shape[1]
    )
    return jnp.where(keep_slot[:, :, None], taken_rows, jnp.zeros((), source.dtype))


def local(
    wide,
    narrow,
    hidden_in,
    segment_ids,
    seg_lengths,
    seg_offsets,
    block_table,
    attn_gain,
    w_query,
    b_query,
    w_keyval,
    b_keyval,
    w_out,
    mlp_gain,
    w_gate,
    w_up,
    w_down,
    next_gain,
    w_query2,
    b_query2,
    w_keyval2,
    b_keyval2,
):
    tok_rows, depth = hidden_in.shape
    piece_rows = w_query.shape[0]
    query_width = w_query.shape[1]
    width = w_gate.shape[1]
    wide_index = lax.axis_index("wide")
    narrow_index = lax.axis_index("narrow")
    head_pair = narrow_index // 2
    kind_index = narrow_index % 2
    pair_offset = head_pair * 2 * HD
    share = tok_rows // narrow
    row_base = wide_index * tok_rows

    qkv_weight = jnp.concatenate(
        [w_query, lax.dynamic_slice_in_dim(w_keyval, pair_offset, 2 * HD, 1), w_out.T], axis=1
    )
    qkv_bias = jnp.concatenate(
        [b_query, lax.dynamic_slice_in_dim(b_keyval, pair_offset, 2 * HD, 0)]
    ).astype(f32)[None]


    token_start = lookup(seg_offsets, segment_ids)
    positions = row_base + jnp.arange(tok_rows, dtype=jnp.int32) - token_start
    half = HD // 2
    frequency = rope_base ** (-(jnp.arange(half, dtype=f32) * 2.0 / HD))
    angles = positions.astype(f32)[:, None] * frequency
    cosine, sine = jnp.cos(angles), jnp.sin(angles)
    cosine = jnp.concatenate([cosine, cosine], axis=1)
    sine = jnp.concatenate([-sine, sine], axis=1)

    one_offset = pair_offset + kind_index * HD
    next_weight = jnp.concatenate(
        [w_query2, lax.dynamic_slice_in_dim(w_keyval2, one_offset, HD, 1)], axis=1
    )
    next_bias = jnp.concatenate(
        [b_query2, lax.dynamic_slice_in_dim(b_keyval2, one_offset, HD, 0)]
    ).astype(f32)[None]
    base_rows = lax.dynamic_slice_in_dim(hidden_in, narrow_index * share, share, 0)
    mlp_row = mlp_gain.astype(f32)[None]
    next_row = next_gain.astype(f32)[None]
    starts_column = token_start[:, None]
    packed = jnp.stack([w_gate, w_up, w_down.T])
    ffn_weights = lax.all_gather(packed, "wide", axis=0, tiled=False)
    early = (
        cosine,
        sine,
        qkv_bias,
        next_weight,
        next_bias,
        base_rows,
        mlp_row,
        next_row,
        starts_column,
    )
    early = lax.optimization_barrier(early)
    qkv_pieces = wide_pieces(qkv_weight, wide, *early)
    cosine, sine, qkv_bias, next_weight, next_bias, base_rows = early[:6]
    mlp_row, next_row, starts_column = early[6:]

    qkv_width = query_width + 2 * HD
    queries, keyvals, out_weight = pl.pallas_call(
        functools.partial(qkv_kernel, wide),
        out_shape=(
            jax.ShapeDtypeStruct((tok_rows, query_width), bf16),
            jax.ShapeDtypeStruct((tok_rows, 2 * HD), bf16),
            jax.ShapeDtypeStruct((depth, query_width), bf16),
        ),
        in_specs=[smem_spec()] + [vmem_spec()] * 5 + [any_spec()] * wide,
        out_specs=(vmem_spec(),) * 3,
        scratch_shapes=[VMEM((depth, qkv_width + query_width), bf16), pltpu.SemaphoreType.DMA((wide,))],
        compiler_params=params(60),
        cost_estimate=pl.CostEstimate(
            flops=2 * tok_rows * depth * qkv_width,
            bytes_accessed=2 * depth * (tok_rows + qkv_width),
            transcendentals=0,
        ),
        name="qkv",
    )(
        wide_index[None],
        hidden_in,
        attn_gain.astype(f32)[None],
        qkv_bias,
        cosine,
        sine,
        *qkv_pieces,
    )

    kv_pieces = wide_pieces(keyvals, wide)

    total_rows = wide * tok_rows
    share_shape = jax.ShapeDtypeStruct((share, depth), bf16)

    def attend(shares, first_call, sources):
        kv_shape = jax.ShapeDtypeStruct((total_rows, 2 * HD), bf16)
        mix = VMEM((2 * share, query_width), bf16)
        gather_scratch = [
            VMEM((total_rows, 2 * HD), bf16),
            mix,
            pltpu.SemaphoreType.DMA((wide,)),
            pltpu.SemaphoreType.DMA,
        ]
        source_specs = [any_spec()] * wide if first_call else [vmem_spec()]
        return pl.pallas_call(
            functools.partial(attend_kernel, wide, shares),
            out_shape=[share_shape] * 2 + [kv_shape] * first_call,
            in_specs=[smem_spec()] * 3 + [vmem_spec()] * 3 + source_specs,
            out_specs=[vmem_spec()] * 2 + [hbm_spec()] * first_call,
            scratch_shapes=gather_scratch if first_call else [mix],
            compiler_params=params(60 if first_call else 24),
            cost_estimate=pl.CostEstimate(
                flops=4 * tok_rows * query_width * depth,
                bytes_accessed=4 * total_rows * HD,
                transcendentals=tok_rows * depth,
            ),
            name="attend",
        )(
            wide_index[None],
            narrow_index[None],
            token_start,
            starts_column,
            queries,
            out_weight,
            *sources,
        )

    far_two, far_three, kv_all = attend((2, 3), True, kv_pieces)
    near_zero, near_one = attend((0, 1), False, [kv_all])
    parts = [near_zero, near_one, far_two, far_three]

    def join(parts, base_rows, gain, with_norm):
        shape = jax.ShapeDtypeStruct((share, depth), bf16)
        count = 4 if with_norm else 3
        return pl.pallas_call(
            functools.partial(join_kernel, narrow),
            out_shape=[shape] * count,
            in_specs=[vmem_spec()] * (2 + narrow),
            out_specs=[vmem_spec()] * count,
            compiler_params=params(60),
            name="join",
        )(base_rows, gain, *parts)

    *normed, residual = join(narrow_swap(parts, narrow), base_rows, mlp_row, True)
    normed_pieces = narrow_spread(normed, narrow)

    source = lax.dynamic_slice_in_dim(kv_all, kind_index * HD, HD, 1)
    page_count = tok_rows // PAGE_LEN + 1
    cache_block = fill_pages(
        source, seg_lengths, seg_offsets, block_table, wide_index * page_count, page_count
    )
    def feed_forward(x_shares):
        count = len(x_shares)
        return pl.pallas_call(
            functools.partial(ffn_kernel, count),
            out_shape=[share_shape] * count,
            in_specs=[vmem_spec()] * count + [hbm_spec()],
            out_specs=[vmem_spec()] * count,
            scratch_shapes=[
                VMEM((count * share, depth), bf16),
                VMEM((3, wide, piece_rows, width), bf16),
                VMEM((count * share, width), f32),
                VMEM((count * share, width), bf16),
                pltpu.SemaphoreType.DMA((3, wide)),
            ],
            compiler_params=params(60 if x_shares is far else 44),
            cost_estimate=pl.CostEstimate(
                flops=6 * count * share * depth * width,
                bytes_accessed=6 * depth * width,
                transcendentals=count * share * width,
            ),
            name="ffn",
        )(*x_shares, ffn_weights)

    far = [normed_pieces[3], normed_pieces[0]]
    part_three, part_zero = feed_forward(far)
    part_one, part_two = feed_forward(list(after(normed_pieces[1:3], part_three)))
    parts = [part_zero, part_one, part_two, part_three]

    (next_weight,) = after([next_weight], residual)
    next_weight = lax.all_gather(next_weight, "wide", axis=0, tiled=True)
    hidden_rows = join(narrow_swap(parts, narrow), residual, mlp_row, False)
    hidden_pieces = narrow_spread(hidden_rows, narrow)

    next_width = query_width + HD
    def project(shares, outputs):
        count = len(shares)
        operands = 4 + count
        return pl.pallas_call(
            functools.partial(next_kernel, shares),
            out_shape=(
                jax.ShapeDtypeStruct((tok_rows, depth), bf16),
                jax.ShapeDtypeStruct((tok_rows, query_width), bf16),
                jax.ShapeDtypeStruct((tok_rows, HD), bf16),
            ),
            in_specs=[smem_spec()]
            + [vmem_spec()] * (3 + count)
            + [hbm_spec()] * len(outputs),
            out_specs=(hbm_spec(),) * 3,
            scratch_shapes=[
                VMEM((count * share, query_width), bf16),
                VMEM((count * share, HD), bf16),
                pltpu.SemaphoreType.DMA((3 * count,)),
            ],
            input_output_aliases={operands + i: i for i in range(len(outputs))},
            compiler_params=params(40),
            cost_estimate=pl.CostEstimate(
                flops=2 * count * share * depth * next_width,
                bytes_accessed=2 * depth * (2 * tok_rows + next_width),
                transcendentals=0,
            ),
            name="next",
        )(
            narrow_index[None],
            next_row,
            next_bias,
            next_weight,
            *[hidden_pieces[k] for k in shares],
            *outputs,
        )

    outputs = project((0, 1, 3), ())
    hidden_out, next_query, next_keyval = project((2,), outputs)

    return (hidden_out, next_query, next_keyval, cache_block[None])


def solution(mesh):
    placed = (
        P("wide", None),
        P("wide"),
        P(),
        P(),
        P(),
        P(),
        P("wide", "narrow"),
        P("narrow"),
        P("wide", None),
        P(),
        P("narrow", "wide"),
        P(),
        P("wide", "narrow"),
        P("wide", "narrow"),
        P("narrow", "wide"),
        P(),
        P("wide", "narrow"),
        P("narrow"),
        P("wide", None),
        P(),
    )
    return jax.shard_map(
        functools.partial(local, mesh.shape["wide"], mesh.shape["narrow"]),
        mesh=mesh,
        in_specs=placed,
        out_specs=(
            P("wide", None),
            P("wide", "narrow"),
            P("wide", "narrow"),
            P("narrow", "wide", None, None),
        ),
        check_vma=False,
    )
```

```python
import functools
import math

import jax
import jax.numpy as jnp
from jax import lax
from jax.experimental import pallas as pl
from jax.experimental.pallas import tpu as pltpu
from jax.sharding import PartitionSpec as P

HD = 128
PAGE_LEN = 128

norm_eps = 1e-06
rope_base = 1000000.0
masked_score = -1e30

f32 = jnp.float32
bf16 = jnp.bfloat16
VMEM = pltpu.VMEM
SMEM = pltpu.SMEM


def vmem_spec():
    return pl.BlockSpec(memory_space=VMEM)


def any_spec():
    return pl.BlockSpec(memory_space=pl.ANY)


def hbm_spec():
    return pl.BlockSpec(memory_space=pltpu.HBM)


def smem_spec():
    return pl.BlockSpec(memory_space=SMEM)


def params(mib):
    return pltpu.CompilerParams(vmem_limit_bytes=mib << 20)


def norm_rows(values, gain_row):
    row_scale = lax.rsqrt(jnp.mean(values * values, axis=-1, keepdims=True) + norm_eps)
    return (values * row_scale * gain_row).astype(bf16)


def lookup(table, indices):
    table_match = indices[..., None] == jnp.arange(table.shape[0], dtype=jnp.int32)
    return jnp.sum(jnp.where(table_match, table, 0), axis=-1)


def exchange(value, axis, size, mask):
    return lax.ppermute(value, axis, [(i, i ^ mask) for i in range(size)])


def wide_pieces(value, size, *tokens):
    pieces = {0: value}
    for mask in range(2, size, 2):
        pieces[mask] = exchange(value, "wide", size, mask)
    for mask in range(0, size, 2):
        source = pieces[mask]
        if tokens and mask:
            (source,) = after([source], *tokens)
        pieces[mask + 1] = exchange(source, "wide", size, 1)
    return [pieces[m] for m in range(size)]


def after(values, *tokens):
    return lax.optimization_barrier((tuple(values), tokens))[0]


def narrow_swap(pieces, size):
    return [pieces[0]] + [exchange(pieces[k], "narrow", size, k) for k in range(1, size)]


def narrow_spread(copies, size):
    near = exchange(copies[1], "narrow", size, 1)
    far = exchange(copies[2], "narrow", size, 3)
    return [copies[0], near, exchange(far, "narrow", size, 1), far]


def place_copies(piece_refs, target, sems, wide_index):
    rows = piece_refs[0].shape[0]
    copies = []
    for m, piece in enumerate(piece_refs):
        start = pl.multiple_of((wide_index ^ m) * rows, rows)
        copies.append(pltpu.make_async_copy(piece, target.at[pl.ds(start, rows)], sems.at[m]))
    return copies


def contract_last(left, right):
    return lax.dot_general(left, right, (((1,), (1,)), ((), ())), preferred_element_type=f32)


def qkv_kernel(wide, index_ref, hidden_ref, gain_ref, bias_ref, cos_ref, sin_ref, *rest):
    pieces, (q_ref, kv_ref, out_ref, weight, sems) = rest[:wide], rest[wide:]
    copies = place_copies(pieces, weight, sems, index_ref[0])
    for c in copies:
        c.start()
    normed = norm_rows(hidden_ref[...].astype(f32), gain_ref[...])
    cosine, sine = cos_ref[...], sin_ref[...]
    for c in copies:
        c.wait()
    heads = q_ref.shape[1] // HD + 2
    for h in range(heads):
        lanes = slice(h * HD, (h + 1) * HD)
        if h % 2 == 0:
            wider = slice(h * HD, min(h + 2, heads) * HD)
            both = jnp.dot(normed, weight[:, wider], preferred_element_type=f32)
        value = both[:, (h % 2) * HD : (h % 2 + 1) * HD] + bias_ref[:, lanes]
        if h < heads - 1:
            value = value * cosine + pltpu.roll(value, HD // 2, 1) * sine
        value = value.astype(bf16)
        if h < heads - 2:
            q_ref[:, lanes] = value
        else:
            kv_ref[:, (h - heads + 2) * HD : (h - heads + 3) * HD] = value
    out_ref[...] = weight[:, heads * HD :]


def attend_kernel(wide, shares, wide_ref, narrow_ref, spots_ref, starts_ref, q_ref, w_out, *rest):
    first_call = len(rest) > 4
    wide_index, narrow_index = wide_ref[0], narrow_ref[0]
    if first_call:
        kv_pieces, rest = rest[:wide], rest[wide:]
        part_refs, (kv_out, keyvals, mix, kv_sems, flush_sem) = rest[:2], rest[2:]
        kv_copies = place_copies(kv_pieces, keyvals, kv_sems, wide_index)
        for c in kv_copies:
            c.start()
        for c in kv_copies:
            c.wait()
        flush = pltpu.make_async_copy(keyvals, kv_out, flush_sem)
        flush.start()
    else:
        keyvals, *part_refs, mix = rest
    share = part_refs[0].shape[0]
    tile = 2 * share
    tok_rows = q_ref.shape[0]
    heads = q_ref.shape[1] // HD
    row_base = wide_index * tok_rows
    factor = HD ** (-0.5) * math.log2(math.e)
    begin_row = pl.multiple_of(((narrow_index ^ shares[0]) // 2) * tile, tile)
    rows = pl.ds(begin_row, tile)
    stacked = jnp.concatenate([q_ref[rows, h * HD : (h + 1) * HD] for h in range(heads)], axis=0)
    first = row_base + begin_row
    diagonal = first // tile
    lowest = spots_ref[begin_row] // tile
    whole_from = (spots_ref[begin_row + tile - 1] + tile - 1) // tile
    starts = jnp.concatenate([starts_ref[rows, :]] * heads, axis=0)
    own = first + lax.broadcasted_iota(jnp.int32, (tile, 1), 0)
    own = jnp.concatenate([own] * heads, axis=0)

    def visit(block, state, masked):
        top, total, mixed = state
        begin = pl.multiple_of(block * tile, tile)
        keys = keyvals[pl.ds(begin, tile), :HD]
        values = keyvals[pl.ds(begin, tile), HD:]
        scores = contract_last(stacked, keys) * factor
        if masked:
            spot = begin + lax.broadcasted_iota(jnp.int32, (1, tile), 1)
            scores = jnp.where((spot >= starts) & (spot <= own), scores, masked_score)
        new_top = jnp.maximum(top, jnp.max(scores, axis=1, keepdims=True))
        weights = jnp.exp2(scores - new_top)
        scale = jnp.exp2(top - new_top)
        total = total * scale + jnp.sum(weights, axis=1, keepdims=True)
        mixed = mixed * scale + jnp.dot(weights.astype(bf16), values, preferred_element_type=f32)
        return new_top, total, mixed

    count = heads * tile
    state = (
        jnp.full((count, 1), masked_score, f32),
        jnp.zeros((count, 1), f32),
        jnp.zeros((count, HD), f32),
    )
    state = visit(diagonal, state, True)
    split = jnp.minimum(whole_from, diagonal)
    state = lax.fori_loop(lowest, split, lambda b, s: visit(b, s, True), state)
    split = jnp.maximum(split, lowest)
    _, total, mixed = lax.fori_loop(split, diagonal, lambda b, s: visit(b, s, False), state)
    mixed = (mixed / total).astype(bf16)
    for h in range(heads):
        mix[:, h * HD : (h + 1) * HD] = mixed[h * tile : (h + 1) * tile]
    for k, part_ref in zip(shares, part_refs):
        start = pl.multiple_of(((narrow_index ^ k) % 2) * share, share)
        part_ref[...] = contract_last(mix[pl.ds(start, share), :], w_out[...]).astype(bf16)
    if first_call:
        flush.wait()


def join_kernel(narrow, base_ref, gain_ref, *rest):
    parts, outs = rest[:narrow], rest[narrow:]
    total = parts[0][...].astype(f32)
    for part in parts[1:]:
        total = total + part[...].astype(f32)
    rounded = (base_ref[...].astype(f32) + total).astype(bf16)
    if len(outs) > 3:
        outs[3][...] = rounded
        rounded = norm_rows(rounded.astype(f32), gain_ref[...])
    for out in outs[:3]:
        out[...] = rounded


def ffn_kernel(count, *rest):
    x_refs, weights_ref, rest = rest[:count], rest[count], rest[count + 1 :]
    part_refs, (x, held, gate, hidden, sems) = rest[:count], rest[count:]
    copies = [
        [
            pltpu.make_async_copy(weights_ref.at[p, j], held.at[j, p], sems.at[j, p])
            for p in range(held.shape[1])
        ]
        for j in range(3)
    ]
    for group in copies:
        for c in group:
            c.start()
    share = x_refs[0].shape[0]
    for k in range(len(x_refs)):
        x[k * share : (k + 1) * share, :] = x_refs[k][...]
    depth, width = x.shape[1], hidden.shape[1]
    tile = 1024
    whole = width // tile

    def each_tile(body):
        @pl.loop(0, whole)
        def _(j):
            body(pl.ds(pl.multiple_of(j * tile, tile), tile))

        if width % tile:
            body(slice(whole * tile, width))

    def block(j, lanes):
        part = held[j, :, :, lanes]
        return part.reshape(depth, part.shape[-1])

    def gate_tile(lanes):
        gate[:, lanes] = jnp.dot(x[...], block(0, lanes), preferred_element_type=f32)

    def up_tile(lanes):
        up = jnp.dot(x[...], block(1, lanes), preferred_element_type=f32)
        value = gate[:, lanes]
        hidden[:, lanes] = (value / (1.0 + jnp.exp(-value)) * up).astype(bf16)

    for c in copies[0]:
        c.wait()
    each_tile(gate_tile)
    for c in copies[1]:
        c.wait()
    each_tile(up_tile)
    for c in copies[2]:
        c.wait()
    pieces, rows = held.shape[1], held.shape[2]
    group = 768 // rows
    for g in range(pieces // group):
        lanes = slice(g * group * rows, (g + 1) * group * rows)
        down = held[2, g * group : (g + 1) * group].reshape(group * rows, width)
        product = contract_last(hidden[...], down)
        for k in range(len(x_refs)):
            part_refs[k][:, lanes] = product[k * share : (k + 1) * share].astype(bf16)


def next_kernel(shares, narrow_ref, gain_ref, bias_ref, weight, *rest):
    h_refs = rest[: len(shares)]
    *outs, query, keyval, out_sems = rest[-6:]
    share = h_refs[0].shape[0]
    width = query.shape[1]
    flushes = []

    def flush(source, k, j):
        begin = pl.multiple_of((narrow_ref[0] ^ k) * share, share)
        target = outs[j].at[pl.ds(begin, share)]
        copy = pltpu.make_async_copy(source, target, out_sems.at[len(flushes)])
        copy.start()
        flushes.append(copy)

    for i, k in enumerate(shares):
        flush(h_refs[i], k, 0)
    for i, k in enumerate(shares):
        rows = slice(i * share, (i + 1) * share)
        normed = norm_rows(h_refs[i][...].astype(f32), gain_ref[...])
        product = jnp.dot(normed, weight[...], preferred_element_type=f32) + bias_ref[...]
        query[rows, :] = product[:, :width].astype(bf16)
        keyval[rows, :] = product[:, width:].astype(bf16)
        flush(query.at[pl.ds(i * share, share)], k, 1)
        flush(keyval.at[pl.ds(i * share, share)], k, 2)
    for c in flushes:
        c.wait()


def fill_pages(source, seg_lengths, seg_offsets, block_table, first_page, page_count):
    pages_here = first_page + jnp.arange(page_count, dtype=jnp.int32)
    page_match = block_table[None, :, :] == pages_here[:, None, None]
    seg_grid = jnp.arange(block_table.shape[0], dtype=jnp.int32)[None, :, None]
    page_grid = jnp.arange(block_table.shape[1], dtype=jnp.int32)[None, None, :]
    page_owner = jnp.sum(jnp.where(page_match, seg_grid, 0), axis=(1, 2))
    logical = jnp.sum(jnp.where(page_match, page_grid, 0), axis=(1, 2))
    in_use = jnp.any(page_match, axis=(1, 2))
    first_token = lookup(seg_offsets, page_owner) + logical * PAGE_LEN
    filled = lookup(seg_lengths, page_owner) - logical * PAGE_LEN
    slot_index = jnp.arange(PAGE_LEN, dtype=jnp.int32)
    row_ids = jnp.clip(first_token[:, None] + slot_index[None, :], 0, source.shape[0] - 1)
    keep_slot = in_use[:, None] & (slot_index[None, :] < filled[:, None])
    taken_rows = jnp.take(source, row_ids.reshape(-1), axis=0).reshape(
        page_count, PAGE_LEN, source.shape[1]
    )
    return jnp.where(keep_slot[:, :, None], taken_rows, jnp.zeros((), source.dtype))


def local(
    wide,
    narrow,
    hidden_in,
    segment_ids,
    seg_lengths,
    seg_offsets,
    block_table,
    attn_gain,
    w_query,
    b_query,
    w_keyval,
    b_keyval,
    w_out,
    mlp_gain,
    w_gate,
    w_up,
    w_down,
    next_gain,
    w_query2,
    b_query2,
    w_keyval2,
    b_keyval2,
):
    tok_rows, depth = hidden_in.shape
    piece_rows = w_query.shape[0]
    query_width = w_query.shape[1]
    width = w_gate.shape[1]
    wide_index = lax.axis_index("wide")
    narrow_index = lax.axis_index("narrow")
    head_pair = narrow_index // 2
    kind_index = narrow_index % 2
    pair_offset = head_pair * 2 * HD
    share = tok_rows // narrow
    row_base = wide_index * tok_rows

    qkv_weight = jnp.concatenate(
        [w_query, lax.dynamic_slice_in_dim(w_keyval, pair_offset, 2 * HD, 1), w_out.T], axis=1
    )
    qkv_bias = jnp.concatenate(
        [b_query, lax.dynamic_slice_in_dim(b_keyval, pair_offset, 2 * HD, 0)]
    ).astype(f32)[None]


    token_start = lookup(seg_offsets, segment_ids)
    positions = row_base + jnp.arange(tok_rows, dtype=jnp.int32) - token_start
    half = HD // 2
    frequency = rope_base ** (-(jnp.arange(half, dtype=f32) * 2.0 / HD))
    angles = positions.astype(f32)[:, None] * frequency
    cosine, sine = jnp.cos(angles), jnp.sin(angles)
    cosine = jnp.concatenate([cosine, cosine], axis=1)
    sine = jnp.concatenate([-sine, sine], axis=1)

    one_offset = pair_offset + kind_index * HD
    next_weight = jnp.concatenate(
        [w_query2, lax.dynamic_slice_in_dim(w_keyval2, one_offset, HD, 1)], axis=1
    )
    next_bias = jnp.concatenate(
        [b_query2, lax.dynamic_slice_in_dim(b_keyval2, one_offset, HD, 0)]
    ).astype(f32)[None]
    base_rows = lax.dynamic_slice_in_dim(hidden_in, narrow_index * share, share, 0)
    mlp_row = mlp_gain.astype(f32)[None]
    next_row = next_gain.astype(f32)[None]
    starts_column = token_start[:, None]
    packed = jnp.stack([w_gate, w_up, w_down.T])
    ffn_weights = lax.all_gather(packed, "wide", axis=0, tiled=False)
    early = (
        cosine,
        sine,
        qkv_bias,
        next_weight,
        next_bias,
        base_rows,
        mlp_row,
        next_row,
        starts_column,
    )
    early = lax.optimization_barrier(early)
    qkv_pieces = wide_pieces(qkv_weight, wide, *early)
    cosine, sine, qkv_bias, next_weight, next_bias, base_rows = early[:6]
    mlp_row, next_row, starts_column = early[6:]

    qkv_width = query_width + 2 * HD
    queries, keyvals, out_weight = pl.pallas_call(
        functools.partial(qkv_kernel, wide),
        out_shape=(
            jax.ShapeDtypeStruct((tok_rows, query_width), bf16),
            jax.ShapeDtypeStruct((tok_rows, 2 * HD), bf16),
            jax.ShapeDtypeStruct((depth, query_width), bf16),
        ),
        in_specs=[smem_spec()] + [vmem_spec()] * 5 + [any_spec()] * wide,
        out_specs=(vmem_spec(),) * 3,
        scratch_shapes=[VMEM((depth, qkv_width + query_width), bf16), pltpu.SemaphoreType.DMA((wide,))],
        compiler_params=params(60),
        cost_estimate=pl.CostEstimate(
            flops=2 * tok_rows * depth * qkv_width,
            bytes_accessed=2 * depth * (tok_rows + qkv_width),
            transcendentals=0,
        ),
        name="qkv",
    )(
        wide_index[None],
        hidden_in,
        attn_gain.astype(f32)[None],
        qkv_bias,
        cosine,
        sine,
        *qkv_pieces,
    )

    kv_pieces = wide_pieces(keyvals, wide)

    total_rows = wide * tok_rows
    share_shape = jax.ShapeDtypeStruct((share, depth), bf16)

    def attend(shares, first_call, sources):
        kv_shape = jax.ShapeDtypeStruct((total_rows, 2 * HD), bf16)
        mix = VMEM((2 * share, query_width), bf16)
        gather_scratch = [
            VMEM((total_rows, 2 * HD), bf16),
            mix,
            pltpu.SemaphoreType.DMA((wide,)),
            pltpu.SemaphoreType.DMA,
        ]
        source_specs = [any_spec()] * wide if first_call else [vmem_spec()]
        return pl.pallas_call(
            functools.partial(attend_kernel, wide, shares),
            out_shape=[share_shape] * 2 + [kv_shape] * first_call,
            in_specs=[smem_spec()] * 3 + [vmem_spec()] * 3 + source_specs,
            out_specs=[vmem_spec()] * 2 + [hbm_spec()] * first_call,
            scratch_shapes=gather_scratch if first_call else [mix],
            compiler_params=params(60 if first_call else 24),
            cost_estimate=pl.CostEstimate(
                flops=4 * tok_rows * query_width * depth,
                bytes_accessed=4 * total_rows * HD,
                transcendentals=tok_rows * depth,
            ),
            name="attend",
        )(
            wide_index[None],
            narrow_index[None],
            token_start,
            starts_column,
            queries,
            out_weight,
            *sources,
        )

    far_two, far_three, kv_all = attend((2, 3), True, kv_pieces)
    near_zero, near_one = attend((0, 1), False, [kv_all])
    parts = [near_zero, near_one, far_two, far_three]

    def join(parts, base_rows, gain, with_norm):
        shape = jax.ShapeDtypeStruct((share, depth), bf16)
        count = 4 if with_norm else 3
        return pl.pallas_call(
            functools.partial(join_kernel, narrow),
            out_shape=[shape] * count,
            in_specs=[vmem_spec()] * (2 + narrow),
            out_specs=[vmem_spec()] * count,
            compiler_params=params(60),
            name="join",
        )(base_rows, gain, *parts)

    *normed, residual = join(narrow_swap(parts, narrow), base_rows, mlp_row, True)
    normed_pieces = narrow_spread(normed, narrow)

    source = lax.dynamic_slice_in_dim(kv_all, kind_index * HD, HD, 1)
    page_count = tok_rows // PAGE_LEN + 1
    cache_block = fill_pages(
        source, seg_lengths, seg_offsets, block_table, wide_index * page_count, page_count
    )
    def feed_forward(x_shares):
        count = len(x_shares)
        return pl.pallas_call(
            functools.partial(ffn_kernel, count),
            out_shape=[share_shape] * count,
            in_specs=[vmem_spec()] * count + [hbm_spec()],
            out_specs=[vmem_spec()] * count,
            scratch_shapes=[
                VMEM((count * share, depth), bf16),
                VMEM((3, wide, piece_rows, width), bf16),
                VMEM((count * share, width), f32),
                VMEM((count * share, width), bf16),
                pltpu.SemaphoreType.DMA((3, wide)),
            ],
            compiler_params=params(60 if x_shares is far else 44),
            cost_estimate=pl.CostEstimate(
                flops=6 * count * share * depth * width,
                bytes_accessed=6 * depth * width,
                transcendentals=count * share * width,
            ),
            name="ffn",
        )(*x_shares, ffn_weights)

    far = [normed_pieces[3], normed_pieces[0]]
    part_three, part_zero = feed_forward(far)
    part_one, part_two = feed_forward(list(after(normed_pieces[1:3], part_three)))
    parts = [part_zero, part_one, part_two, part_three]

    (next_weight,) = after([next_weight], residual)
    next_weight = lax.all_gather(next_weight, "wide", axis=0, tiled=True)
    summed = residual.astype(f32)
    swapped = narrow_swap(parts, narrow)
    for part in [swapped[k] for k in (0, 2, 3, 1)]:
        summed = summed + part.astype(f32)
    hidden_rows = [summed.astype(bf16)] * 3
    hidden_pieces = narrow_spread(hidden_rows, narrow)

    next_width = query_width + HD
    def project(shares, outputs):
        count = len(shares)
        operands = 4 + count
        return pl.pallas_call(
            functools.partial(next_kernel, shares),
            out_shape=(
                jax.ShapeDtypeStruct((tok_rows, depth), bf16),
                jax.ShapeDtypeStruct((tok_rows, query_width), bf16),
                jax.ShapeDtypeStruct((tok_rows, HD), bf16),
            ),
            in_specs=[smem_spec()]
            + [vmem_spec()] * (3 + count)
            + [hbm_spec()] * len(outputs),
            out_specs=(hbm_spec(),) * 3,
            scratch_shapes=[
                VMEM((count * share, query_width), bf16),
                VMEM((count * share, HD), bf16),
                pltpu.SemaphoreType.DMA((3 * count,)),
            ],
            input_output_aliases={operands + i: i for i in range(len(outputs))},
            compiler_params=params(40),
            cost_estimate=pl.CostEstimate(
                flops=2 * count * share * depth * next_width,
                bytes_accessed=2 * depth * (2 * tok_rows + next_width),
                transcendentals=0,
            ),
            name="next",
        )(
            narrow_index[None],
            next_row,
            next_bias,
            next_weight,
            *[hidden_pieces[k] for k in shares],
            *outputs,
        )

    outputs = project((0, 1, 3), ())
    hidden_out, next_query, next_keyval = project((2,), outputs)

    return (hidden_out, next_query, next_keyval, cache_block[None])


def solution(mesh):
    placed = (
        P("wide", None),
        P("wide"),
        P(),
        P(),
        P(),
        P(),
        P("wide", "narrow"),
        P("narrow"),
        P("wide", None),
        P(),
        P("narrow", "wide"),
        P(),
        P("wide", "narrow"),
        P("wide", "narrow"),
        P("narrow", "wide"),
        P(),
        P("wide", "narrow"),
        P("narrow"),
        P("wide", None),
        P(),
    )
    return jax.shard_map(
        functools.partial(local, mesh.shape["wide"], mesh.shape["narrow"]),
        mesh=mesh,
        in_specs=placed,
        out_specs=(
            P("wide", None),
            P("wide", "narrow"),
            P("wide", "narrow"),
            P("narrow", "wide", None, None),
        ),
        check_vma=False,
    )
```

```python
import functools
import math

import jax
import jax.numpy as jnp
from jax import lax
from jax.experimental import pallas as pl
from jax.experimental.pallas import tpu as pltpu
from jax.sharding import PartitionSpec as P

HD = 128
PAGE_LEN = 128

norm_eps = 1e-06
rope_base = 1000000.0
masked_score = -1e30

f32 = jnp.float32
bf16 = jnp.bfloat16
VMEM = pltpu.VMEM
SMEM = pltpu.SMEM


def vmem_spec():
    return pl.BlockSpec(memory_space=VMEM)


def any_spec():
    return pl.BlockSpec(memory_space=pl.ANY)


def hbm_spec():
    return pl.BlockSpec(memory_space=pltpu.HBM)


def smem_spec():
    return pl.BlockSpec(memory_space=SMEM)


def params(mib):
    return pltpu.CompilerParams(vmem_limit_bytes=mib << 20)


def norm_rows(values, gain_row):
    row_scale = lax.rsqrt(jnp.mean(values * values, axis=-1, keepdims=True) + norm_eps)
    return (values * row_scale * gain_row).astype(bf16)


def lookup(table, indices):
    table_match = indices[..., None] == jnp.arange(table.shape[0], dtype=jnp.int32)
    return jnp.sum(jnp.where(table_match, table, 0), axis=-1)


def exchange(value, axis, size, mask):
    return lax.ppermute(value, axis, [(i, i ^ mask) for i in range(size)])


def wide_pieces(value, size, *tokens):
    pieces = {0: value}
    for mask in range(2, size, 2):
        pieces[mask] = exchange(value, "wide", size, mask)
    for mask in range(0, size, 2):
        source = pieces[mask]
        if tokens and mask:
            (source,) = after([source], *tokens)
        pieces[mask + 1] = exchange(source, "wide", size, 1)
    return [pieces[m] for m in range(size)]


def after(values, *tokens):
    return lax.optimization_barrier((tuple(values), tokens))[0]


def narrow_swap(pieces, size):
    return [pieces[0]] + [exchange(pieces[k], "narrow", size, k) for k in range(1, size)]


def narrow_spread(copies, size):
    near = exchange(copies[1], "narrow", size, 1)
    far = exchange(copies[2], "narrow", size, 3)
    return [copies[0], near, exchange(far, "narrow", size, 1), far]


def place_copies(piece_refs, target, sems, wide_index):
    rows = piece_refs[0].shape[0]
    copies = []
    for m, piece in enumerate(piece_refs):
        start = pl.multiple_of((wide_index ^ m) * rows, rows)
        copies.append(pltpu.make_async_copy(piece, target.at[pl.ds(start, rows)], sems.at[m]))
    return copies


def contract_last(left, right):
    return lax.dot_general(left, right, (((1,), (1,)), ((), ())), preferred_element_type=f32)


def qkv_kernel(wide, index_ref, hidden_ref, gain_ref, bias_ref, cos_ref, sin_ref, *rest):
    pieces, (q_ref, kv_ref, out_ref, weight, sems) = rest[:wide], rest[wide:]
    copies = place_copies(pieces, weight, sems, index_ref[0])
    for c in copies:
        c.start()
    normed = norm_rows(hidden_ref[...].astype(f32), gain_ref[...])
    cosine, sine = cos_ref[...], sin_ref[...]
    for c in copies:
        c.wait()
    heads = q_ref.shape[1] // HD + 2
    for h in range(heads):
        lanes = slice(h * HD, (h + 1) * HD)
        if h % 2 == 0:
            wider = slice(h * HD, min(h + 2, heads) * HD)
            both = jnp.dot(normed, weight[:, wider], preferred_element_type=f32)
        value = both[:, (h % 2) * HD : (h % 2 + 1) * HD] + bias_ref[:, lanes]
        if h < heads - 1:
            value = value * cosine + pltpu.roll(value, HD // 2, 1) * sine
        value = value.astype(bf16)
        if h < heads - 2:
            q_ref[:, lanes] = value
        else:
            kv_ref[:, (h - heads + 2) * HD : (h - heads + 3) * HD] = value
    out_ref[...] = weight[:, heads * HD :]


def attend_kernel(wide, shares, wide_ref, narrow_ref, spots_ref, starts_ref, q_ref, w_out, *rest):
    first_call = len(rest) > 4
    wide_index, narrow_index = wide_ref[0], narrow_ref[0]
    if first_call:
        kv_pieces, rest = rest[:wide], rest[wide:]
        part_refs, (kv_out, keyvals, mix, kv_sems, flush_sem) = rest[:2], rest[2:]
        kv_copies = place_copies(kv_pieces, keyvals, kv_sems, wide_index)
        for c in kv_copies:
            c.start()
        for c in kv_copies:
            c.wait()
        flush = pltpu.make_async_copy(keyvals, kv_out, flush_sem)
        flush.start()
    else:
        keyvals, *part_refs, mix = rest
    share = part_refs[0].shape[0]
    tile = 2 * share
    tok_rows = q_ref.shape[0]
    heads = q_ref.shape[1] // HD
    row_base = wide_index * tok_rows
    factor = HD ** (-0.5) * math.log2(math.e)
    begin_row = pl.multiple_of(((narrow_index ^ shares[0]) // 2) * tile, tile)
    rows = pl.ds(begin_row, tile)
    stacked = jnp.concatenate([q_ref[rows, h * HD : (h + 1) * HD] for h in range(heads)], axis=0)
    first = row_base + begin_row
    diagonal = first // tile
    lowest = spots_ref[begin_row] // tile
    whole_from = (spots_ref[begin_row + tile - 1] + tile - 1) // tile
    starts = jnp.concatenate([starts_ref[rows, :]] * heads, axis=0)
    own = first + lax.broadcasted_iota(jnp.int32, (tile, 1), 0)
    own = jnp.concatenate([own] * heads, axis=0)

    def visit(block, state, masked):
        top, total, mixed = state
        begin = pl.multiple_of(block * tile, tile)
        keys = keyvals[pl.ds(begin, tile), :HD]
        values = keyvals[pl.ds(begin, tile), HD:]
        scores = contract_last(stacked, keys) * factor
        if masked:
            spot = begin + lax.broadcasted_iota(jnp.int32, (1, tile), 1)
            scores = jnp.where((spot >= starts) & (spot <= own), scores, masked_score)
        new_top = jnp.maximum(top, jnp.max(scores, axis=1, keepdims=True))
        weights = jnp.exp2(scores - new_top)
        scale = jnp.exp2(top - new_top)
        total = total * scale + jnp.sum(weights, axis=1, keepdims=True)
        mixed = mixed * scale + jnp.dot(weights.astype(bf16), values, preferred_element_type=f32)
        return new_top, total, mixed

    count = heads * tile
    state = (
        jnp.full((count, 1), masked_score, f32),
        jnp.zeros((count, 1), f32),
        jnp.zeros((count, HD), f32),
    )
    state = visit(diagonal, state, True)
    split = jnp.minimum(whole_from, diagonal)
    state = lax.fori_loop(lowest, split, lambda b, s: visit(b, s, True), state)
    split = jnp.maximum(split, lowest)
    _, total, mixed = lax.fori_loop(split, diagonal, lambda b, s: visit(b, s, False), state)
    mixed = (mixed / total).astype(bf16)
    for h in range(heads):
        mix[:, h * HD : (h + 1) * HD] = mixed[h * tile : (h + 1) * tile]
    for k, part_ref in zip(shares, part_refs):
        start = pl.multiple_of(((narrow_index ^ k) % 2) * share, share)
        part_ref[...] = contract_last(mix[pl.ds(start, share), :], w_out[...]).astype(bf16)
    if first_call:
        flush.wait()


def join_kernel(narrow, base_ref, gain_ref, *rest):
    parts, outs = rest[:narrow], rest[narrow:]
    total = parts[0][...].astype(f32)
    for part in parts[1:]:
        total = total + part[...].astype(f32)
    rounded = (base_ref[...].astype(f32) + total).astype(bf16)
    if len(outs) > 3:
        outs[3][...] = rounded
        rounded = norm_rows(rounded.astype(f32), gain_ref[...])
    for out in outs[:3]:
        out[...] = rounded


def ffn_kernel(count, *rest):
    x_refs, weights_ref, rest = rest[:count], rest[count], rest[count + 1 :]
    part_refs, (x, held, gate, hidden, sems) = rest[:count], rest[count:]
    copies = [
        [
            pltpu.make_async_copy(weights_ref.at[p, j], held.at[j, p], sems.at[j, p])
            for p in range(held.shape[1])
        ]
        for j in range(3)
    ]
    for group in copies:
        for c in group:
            c.start()
    share = x_refs[0].shape[0]
    for k in range(len(x_refs)):
        x[k * share : (k + 1) * share, :] = x_refs[k][...]
    depth, width = x.shape[1], hidden.shape[1]

    def each_tile(body):
        body(slice(0, width))

    def block(j, lanes):
        part = held[j, :, :, lanes]
        return part.reshape(depth, part.shape[-1])

    def gate_tile(lanes):
        gate[:, lanes] = jnp.dot(x[...], block(0, lanes), preferred_element_type=f32)

    def up_tile(lanes):
        up = jnp.dot(x[...], block(1, lanes), preferred_element_type=f32)
        value = gate[:, lanes]
        hidden[:, lanes] = (value / (1.0 + jnp.exp(-value)) * up).astype(bf16)

    for c in copies[0]:
        c.wait()
    each_tile(gate_tile)
    for c in copies[1]:
        c.wait()
    each_tile(up_tile)
    for c in copies[2]:
        c.wait()
    pieces, rows = held.shape[1], held.shape[2]
    group = 768 // rows
    for g in range(pieces // group):
        lanes = slice(g * group * rows, (g + 1) * group * rows)
        down = held[2, g * group : (g + 1) * group].reshape(group * rows, width)
        product = contract_last(hidden[...], down)
        for k in range(len(x_refs)):
            part_refs[k][:, lanes] = product[k * share : (k + 1) * share].astype(bf16)


def next_kernel(shares, narrow_ref, gain_ref, bias_ref, weight, *rest):
    h_refs = rest[: len(shares)]
    *outs, query, keyval, out_sems = rest[-6:]
    share = h_refs[0].shape[0]
    width = query.shape[1]
    flushes = []

    def flush(source, k, j):
        begin = pl.multiple_of((narrow_ref[0] ^ k) * share, share)
        target = outs[j].at[pl.ds(begin, share)]
        copy = pltpu.make_async_copy(source, target, out_sems.at[len(flushes)])
        copy.start()
        flushes.append(copy)

    for i, k in enumerate(shares):
        flush(h_refs[i], k, 0)
    for i, k in enumerate(shares):
        rows = slice(i * share, (i + 1) * share)
        normed = norm_rows(h_refs[i][...].astype(f32), gain_ref[...])
        product = jnp.dot(normed, weight[...], preferred_element_type=f32) + bias_ref[...]
        query[rows, :] = product[:, :width].astype(bf16)
        keyval[rows, :] = product[:, width:].astype(bf16)
        flush(query.at[pl.ds(i * share, share)], k, 1)
        flush(keyval.at[pl.ds(i * share, share)], k, 2)
    for c in flushes:
        c.wait()


def fill_pages(source, seg_lengths, seg_offsets, block_table, first_page, page_count):
    pages_here = first_page + jnp.arange(page_count, dtype=jnp.int32)
    page_match = block_table[None, :, :] == pages_here[:, None, None]
    seg_grid = jnp.arange(block_table.shape[0], dtype=jnp.int32)[None, :, None]
    page_grid = jnp.arange(block_table.shape[1], dtype=jnp.int32)[None, None, :]
    page_owner = jnp.sum(jnp.where(page_match, seg_grid, 0), axis=(1, 2))
    logical = jnp.sum(jnp.where(page_match, page_grid, 0), axis=(1, 2))
    in_use = jnp.any(page_match, axis=(1, 2))
    first_token = lookup(seg_offsets, page_owner) + logical * PAGE_LEN
    filled = lookup(seg_lengths, page_owner) - logical * PAGE_LEN
    slot_index = jnp.arange(PAGE_LEN, dtype=jnp.int32)
    row_ids = jnp.clip(first_token[:, None] + slot_index[None, :], 0, source.shape[0] - 1)
    keep_slot = in_use[:, None] & (slot_index[None, :] < filled[:, None])
    taken_rows = jnp.take(source, row_ids.reshape(-1), axis=0).reshape(
        page_count, PAGE_LEN, source.shape[1]
    )
    return jnp.where(keep_slot[:, :, None], taken_rows, jnp.zeros((), source.dtype))


def local(
    wide,
    narrow,
    hidden_in,
    segment_ids,
    seg_lengths,
    seg_offsets,
    block_table,
    attn_gain,
    w_query,
    b_query,
    w_keyval,
    b_keyval,
    w_out,
    mlp_gain,
    w_gate,
    w_up,
    w_down,
    next_gain,
    w_query2,
    b_query2,
    w_keyval2,
    b_keyval2,
):
    tok_rows, depth = hidden_in.shape
    piece_rows = w_query.shape[0]
    query_width = w_query.shape[1]
    width = w_gate.shape[1]
    wide_index = lax.axis_index("wide")
    narrow_index = lax.axis_index("narrow")
    head_pair = narrow_index // 2
    kind_index = narrow_index % 2
    pair_offset = head_pair * 2 * HD
    share = tok_rows // narrow
    row_base = wide_index * tok_rows

    qkv_weight = jnp.concatenate(
        [w_query, lax.dynamic_slice_in_dim(w_keyval, pair_offset, 2 * HD, 1), w_out.T], axis=1
    )
    qkv_bias = jnp.concatenate(
        [b_query, lax.dynamic_slice_in_dim(b_keyval, pair_offset, 2 * HD, 0)]
    ).astype(f32)[None]


    token_start = lookup(seg_offsets, segment_ids)
    positions = row_base + jnp.arange(tok_rows, dtype=jnp.int32) - token_start
    half = HD // 2
    frequency = rope_base ** (-(jnp.arange(half, dtype=f32) * 2.0 / HD))
    angles = positions.astype(f32)[:, None] * frequency
    cosine, sine = jnp.cos(angles), jnp.sin(angles)
    cosine = jnp.concatenate([cosine, cosine], axis=1)
    sine = jnp.concatenate([-sine, sine], axis=1)

    one_offset = pair_offset + kind_index * HD
    next_weight = jnp.concatenate(
        [w_query2, lax.dynamic_slice_in_dim(w_keyval2, one_offset, HD, 1)], axis=1
    )
    next_bias = jnp.concatenate(
        [b_query2, lax.dynamic_slice_in_dim(b_keyval2, one_offset, HD, 0)]
    ).astype(f32)[None]
    base_rows = lax.dynamic_slice_in_dim(hidden_in, narrow_index * share, share, 0)
    mlp_row = mlp_gain.astype(f32)[None]
    next_row = next_gain.astype(f32)[None]
    starts_column = token_start[:, None]
    packed = jnp.stack([w_gate, w_up, w_down.T])
    ffn_weights = lax.all_gather(packed, "wide", axis=0, tiled=False)
    early = (
        cosine,
        sine,
        qkv_bias,
        next_weight,
        next_bias,
        base_rows,
        mlp_row,
        next_row,
        starts_column,
    )
    early = lax.optimization_barrier(early)
    qkv_pieces = wide_pieces(qkv_weight, wide, *early)
    cosine, sine, qkv_bias, next_weight, next_bias, base_rows = early[:6]
    mlp_row, next_row, starts_column = early[6:]

    qkv_width = query_width + 2 * HD
    queries, keyvals, out_weight = pl.pallas_call(
        functools.partial(qkv_kernel, wide),
        out_shape=(
            jax.ShapeDtypeStruct((tok_rows, query_width), bf16),
            jax.ShapeDtypeStruct((tok_rows, 2 * HD), bf16),
            jax.ShapeDtypeStruct((depth, query_width), bf16),
        ),
        in_specs=[smem_spec()] + [vmem_spec()] * 5 + [any_spec()] * wide,
        out_specs=(vmem_spec(),) * 3,
        scratch_shapes=[VMEM((depth, qkv_width + query_width), bf16), pltpu.SemaphoreType.DMA((wide,))],
        compiler_params=params(60),
        cost_estimate=pl.CostEstimate(
            flops=2 * tok_rows * depth * qkv_width,
            bytes_accessed=2 * depth * (tok_rows + qkv_width),
            transcendentals=0,
        ),
        name="qkv",
    )(
        wide_index[None],
        hidden_in,
        attn_gain.astype(f32)[None],
        qkv_bias,
        cosine,
        sine,
        *qkv_pieces,
    )

    kv_pieces = wide_pieces(keyvals, wide)

    total_rows = wide * tok_rows
    share_shape = jax.ShapeDtypeStruct((share, depth), bf16)

    def attend(shares, first_call, sources):
        kv_shape = jax.ShapeDtypeStruct((total_rows, 2 * HD), bf16)
        mix = VMEM((2 * share, query_width), bf16)
        gather_scratch = [
            VMEM((total_rows, 2 * HD), bf16),
            mix,
            pltpu.SemaphoreType.DMA((wide,)),
            pltpu.SemaphoreType.DMA,
        ]
        source_specs = [any_spec()] * wide if first_call else [vmem_spec()]
        return pl.pallas_call(
            functools.partial(attend_kernel, wide, shares),
            out_shape=[share_shape] * 2 + [kv_shape] * first_call,
            in_specs=[smem_spec()] * 3 + [vmem_spec()] * 3 + source_specs,
            out_specs=[vmem_spec()] * 2 + [hbm_spec()] * first_call,
            scratch_shapes=gather_scratch if first_call else [mix],
            compiler_params=params(60 if first_call else 24),
            cost_estimate=pl.CostEstimate(
                flops=4 * tok_rows * query_width * depth,
                bytes_accessed=4 * total_rows * HD,
                transcendentals=tok_rows * depth,
            ),
            name="attend",
        )(
            wide_index[None],
            narrow_index[None],
            token_start,
            starts_column,
            queries,
            out_weight,
            *sources,
        )

    far_two, far_three, kv_all = attend((2, 3), True, kv_pieces)
    near_zero, near_one = attend((0, 1), False, [kv_all])
    parts = [near_zero, near_one, far_two, far_three]

    def join(parts, base_rows, gain, with_norm):
        shape = jax.ShapeDtypeStruct((share, depth), bf16)
        count = 4 if with_norm else 3
        return pl.pallas_call(
            functools.partial(join_kernel, narrow),
            out_shape=[shape] * count,
            in_specs=[vmem_spec()] * (2 + narrow),
            out_specs=[vmem_spec()] * count,
            compiler_params=params(60),
            name="join",
        )(base_rows, gain, *parts)

    *normed, residual = join(narrow_swap(parts, narrow), base_rows, mlp_row, True)
    normed_pieces = narrow_spread(normed, narrow)

    source = lax.dynamic_slice_in_dim(kv_all, kind_index * HD, HD, 1)
    page_count = tok_rows // PAGE_LEN + 1
    cache_block = fill_pages(
        source, seg_lengths, seg_offsets, block_table, wide_index * page_count, page_count
    )
    def feed_forward(x_shares):
        count = len(x_shares)
        return pl.pallas_call(
            functools.partial(ffn_kernel, count),
            out_shape=[share_shape] * count,
            in_specs=[vmem_spec()] * count + [hbm_spec()],
            out_specs=[vmem_spec()] * count,
            scratch_shapes=[
                VMEM((count * share, depth), bf16),
                VMEM((3, wide, piece_rows, width), bf16),
                VMEM((count * share, width), f32),
                VMEM((count * share, width), bf16),
                pltpu.SemaphoreType.DMA((3, wide)),
            ],
            compiler_params=params(60 if x_shares is far else 44),
            cost_estimate=pl.CostEstimate(
                flops=6 * count * share * depth * width,
                bytes_accessed=6 * depth * width,
                transcendentals=count * share * width,
            ),
            name="ffn",
        )(*x_shares, ffn_weights)

    far = [normed_pieces[3], normed_pieces[0]]
    part_three, part_zero = feed_forward(far)
    part_one, part_two = feed_forward(list(after(normed_pieces[1:3], part_three)))
    parts = [part_zero, part_one, part_two, part_three]

    (next_weight,) = after([next_weight], residual)
    next_weight = lax.all_gather(next_weight, "wide", axis=0, tiled=True)
    summed = residual.astype(f32)
    swapped = narrow_swap(parts, narrow)
    for part in [swapped[k] for k in (0, 2, 3, 1)]:
        summed = summed + part.astype(f32)
    hidden_rows = [summed.astype(bf16)] * 3
    hidden_pieces = narrow_spread(hidden_rows, narrow)

    next_width = query_width + HD
    def project(shares, outputs):
        count = len(shares)
        operands = 4 + count
        return pl.pallas_call(
            functools.partial(next_kernel, shares),
            out_shape=(
                jax.ShapeDtypeStruct((tok_rows, depth), bf16),
                jax.ShapeDtypeStruct((tok_rows, query_width), bf16),
                jax.ShapeDtypeStruct((tok_rows, HD), bf16),
            ),
            in_specs=[smem_spec()]
            + [vmem_spec()] * (3 + count)
            + [hbm_spec()] * len(outputs),
            out_specs=(hbm_spec(),) * 3,
            scratch_shapes=[
                VMEM((count * share, query_width), bf16),
                VMEM((count * share, HD), bf16),
                pltpu.SemaphoreType.DMA((3 * count,)),
            ],
            input_output_aliases={operands + i: i for i in range(len(outputs))},
            compiler_params=params(40),
            cost_estimate=pl.CostEstimate(
                flops=2 * count * share * depth * next_width,
                bytes_accessed=2 * depth * (2 * tok_rows + next_width),
                transcendentals=0,
            ),
            name="next",
        )(
            narrow_index[None],
            next_row,
            next_bias,
            next_weight,
            *[hidden_pieces[k] for k in shares],
            *outputs,
        )

    outputs = project((0, 1, 3), ())
    hidden_out, next_query, next_keyval = project((2,), outputs)

    return (hidden_out, next_query, next_keyval, cache_block[None])


def solution(mesh):
    placed = (
        P("wide", None),
        P("wide"),
        P(),
        P(),
        P(),
        P(),
        P("wide", "narrow"),
        P("narrow"),
        P("wide", None),
        P(),
        P("narrow", "wide"),
        P(),
        P("wide", "narrow"),
        P("wide", "narrow"),
        P("narrow", "wide"),
        P(),
        P("wide", "narrow"),
        P("narrow"),
        P("wide", None),
        P(),
    )
    return jax.shard_map(
        functools.partial(local, mesh.shape["wide"], mesh.shape["narrow"]),
        mesh=mesh,
        in_specs=placed,
        out_specs=(
            P("wide", None),
            P("wide", "narrow"),
            P("wide", "narrow"),
            P("narrow", "wide", None, None),
        ),
        check_vma=False,
    )
```
